32 devices in a mesh: wide: 8 (over z, core), narrow: 4 (over y, x).
Axes of the slice: x: 2, y: 2, z: 4, core: 2. Of those that a mesh axis runs over, the one named last changes fastest.
Arguments:
- tokens: bfloat16 [8192, 2048], P('wide'), may hold values from -4 to 4
- cotangent: bfloat16 [8192, 2048], P('wide'), may hold values from -4 to 4
- noise_emb: float32 [128, 2048], P('wide'), may hold values from -2.5 to 2.5
- offsets: int32 [8, 16], P('wide'), may hold values from 0 to 1024, as said below
- lengths: int32 [8, 16], P('wide'), may hold values from 0 to 1024, as said below
- group_ids: int32 [8, 16], P('wide'), may hold values from 0 to 2, as said below
- group_table: float32 [3, 2048], replicated, may hold values from -2.5 to 2.5
- w_qkv: bfloat16 [3, 2048, 2048], P(None, None, 'narrow'), may hold values from -0.125 to 0.125
- w_out: bfloat16 [2048, 2048], P('narrow'), may hold values from -0.5 to 0.5
- w_up: bfloat16 [2048, 8192], P(None, 'narrow'), may hold values from -0.125 to 0.125
- b_up: float32 [8192], P('narrow'), may hold values from -2.5 to 2.5
- w_down: bfloat16 [8192, 2048], P('narrow'), may hold values from -0.09375 to 0.09375
- w_mod: bfloat16 [2048, 6, 2048], P(None, None, 'narrow'), may hold values from -0.0625 to 0.0625
- b_mod: float32 [6, 2048], P(None, 'narrow'), may hold values from -1.5 to 1.5
Outputs:
- result: bfloat16 [8192, 2048], P('wide')
- grad_tokens: bfloat16 [8192, 2048], P('wide')
- grad_noise: float32 [128, 2048], P('wide')
- grad_group_table: float32 [3, 2048], P(None, 'wide')
- grad_w_qkv: float32 [3, 2048, 2048], P(None, 'wide', 'narrow')
- grad_w_out: float32 [2048, 2048], P('narrow', 'wide')
- grad_w_up: float32 [2048, 8192], P('wide', 'narrow')
- grad_b_up: float32 [8192], P(('narrow', 'wide'))
- grad_w_down: float32 [8192, 2048], P('narrow', 'wide')
- grad_w_mod: float32 [2048, 6, 2048], P('wide', None, 'narrow')
- grad_b_mod: float32 [6, 2048], P(None, ('narrow', 'wide'))
The draws below stay inside these ranges and needn't reach their ends.
Inputs may be any that keep to these rules, and one draw needn't show every extreme that they name: `offsets`: each index of wide holds images of one length, 1024, 256 or 64 tokens, laid end to end from token 0 and filling its 1024 tokens: slot s starts at s times that length. Slots past the last image start at 1024. Every length occurs on some index of wide. `lengths`: the length of each image slot; 0 for slots past the last image of an index of wide. `group_ids`: 0 on indices of wide with images of 1024 tokens, 1 with 256, 2 with 64, for all slots of that index; every group occurs.
All inputs are finite; a program needn't handle non-finite values.
Results may differ from the reference program's by a relative error of at most 0.018.
Values may be sent and summed in bfloat16 or wider, within the bound.
No kernel may reach another device: no remote copies, remote signals or barrier semaphores. Data moves between devices by JAX's collectives and lax.ppermute only.
A program may use at most 320 MiB of HBM per device.

```python
import jax
import jax.numpy as jnp
from jax import lax

D = 2048
HEADS = 16
HEAD_DIM = 128
FF = 8192
GROUPS = 3
LEN_BIG = 1024
LEN_MID = 256
LEN_SMALL = 64
TOK_DEV = 1024
SLOTS = 16
TOKENS = 8192
IMAGES = 128
N_WIDE = 8


def layout(key):
    kinds = jax.random.permutation(jax.random.fold_in(key, 11), N_WIDE) % 3
    length = jnp.where(kinds == 0, LEN_BIG, jnp.where(kinds == 1, LEN_MID, LEN_SMALL)).astype(jnp.int32)
    slot = jnp.arange(SLOTS, dtype=jnp.int32)[None, :]
    used = slot < (TOK_DEV // length)[:, None]
    counts = jnp.where(used, length[:, None], 0).astype(jnp.int32)
    starts = jnp.where(used, slot * length[:, None], TOK_DEV).astype(jnp.int32)
    groups = jnp.broadcast_to(kinds[:, None], (N_WIDE, SLOTS)).astype(jnp.int32)
    return (starts, counts, groups)


def draw_offsets(key, part):
    return layout(key)[0]


def draw_lengths(key, part):
    return layout(key)[1]


def draw_group_ids(key, part):
    return layout(key)[2]


def block_levels(stream_key, dims, pieces, smallest, high):
    loudness, own = 1.0, jax.random.fold_in(stream_key, 6)
    for position, blocks in pieces:
        heights = jnp.exp(jax.random.uniform(jax.random.fold_in(own, position), (blocks,), jnp.float32, smallest / len(pieces), high / len(pieces)))
        loudness = loudness * jnp.repeat(heights, dims[position] // blocks).reshape([-1 if axis == position else 1 for axis in range(len(dims))])
    return loudness


def normal_values(stream_key, dims, scale, reach, cuts=(), kind=jnp.bfloat16):
    entries = scale * jax.random.normal(stream_key, dims, jnp.float32)
    if cuts:
        entries = entries * block_levels(stream_key, dims, cuts, -0.22, 0.18)
    return jnp.clip(entries, -reach, reach).astype(kind)


def setup_inputs(seed: int = 0) -> dict:
    seeds = jax.random.split(jax.random.key(seed), 15)
    tokens = normal_values(seeds[0], (TOKENS, D), 1.0, 4.0, ((0, 8),))
    cotangent = normal_values(seeds[1], (TOKENS, D), 1.0, 4.0, ((0, 8),))
    noise_emb = normal_values(seeds[2], (IMAGES, D), 0.5, 2.5, ((0, 8),), jnp.float32)
    offsets = draw_offsets(jax.random.fold_in(seeds[14], 71), 0)
    lengths = draw_lengths(jax.random.fold_in(seeds[14], 71), 0)
    group_ids = draw_group_ids(jax.random.fold_in(seeds[14], 71), 0)
    group_table = normal_values(seeds[6], (GROUPS, D), 0.5, 2.5, (), jnp.float32)
    w_qkv = normal_values(seeds[7], (3, D, D), D ** -0.5, 0.125, ((2, 4),))
    w_out = normal_values(seeds[8], (D, D), (D // 16) ** -0.5, 0.5, ((0, 4),))
    w_up = normal_values(seeds[9], (D, FF), D ** -0.5, 0.125, ((1, 4),))
    b_up = normal_values(seeds[10], (FF,), 0.5, 2.5, ((0, 4),), jnp.float32)
    w_down = normal_values(seeds[11], (FF, D), (FF // 2) ** -0.5, 0.09375, ((0, 4),))
    w_mod = normal_values(seeds[12], (D, 6, D), (4 * D) ** -0.5, 0.0625, ((2, 4),))
    b_mod = normal_values(seeds[13], (6, D), 0.3, 1.5, ((1, 4),), jnp.float32)
    return dict(tokens=tokens, cotangent=cotangent, noise_emb=noise_emb, offsets=offsets, lengths=lengths, group_ids=group_ids, group_table=group_table, w_qkv=w_qkv, w_out=w_out, w_up=w_up, b_up=b_up, w_down=w_down, w_mod=w_mod, b_mod=b_mod)


highest = lax.Precision.HIGHEST

@jax.custom_vjp
def low(v):
    return lax.optimization_barrier(v.astype(jnp.bfloat16)).astype(jnp.float32)

@jax.custom_vjp
def low_back(v):
    return v

def low_keep(v):
    return (low(v), None)

def low_pass(kept, grad):
    return (grad,)

def back_keep(v):
    return (v, None)

def back_low(kept, grad):
    return (low(grad),)
low.defvjp(low_keep, low_pass)
low_back.defvjp(back_keep, back_low)

def matmul(left, right):
    return jnp.dot(left, right, precision=highest, preferred_element_type=jnp.float32)

def layer_norm(values):
    centred = values - lax.optimization_barrier(jnp.mean(values, axis=-1, keepdims=True))
    return centred * lax.rsqrt(lax.optimization_barrier(jnp.mean(centred * centred, axis=-1, keepdims=True)) + 1e-06)

def member_table(starts, counts):
    positions = jnp.arange(TOK_DEV, dtype=jnp.int32)[:, None]
    inside = (positions >= starts[None, :]) & (positions < (starts + counts)[None, :])
    return inside.astype(jnp.float32)

def group_layer(tokens, modes, member, w_qkv, w_out, w_up, b_up, w_down):
    per_token = matmul(member, modes.reshape(SLOTS, 6 * D)).reshape(TOK_DEV, 6, D)
    shift_a = per_token[:, 0]
    scale_a = per_token[:, 1]
    gate_a = per_token[:, 2]
    shift_b = per_token[:, 3]
    scale_b = per_token[:, 4]
    gate_b = per_token[:, 5]
    mixed_a = low(layer_norm(tokens) * (1.0 + scale_a) + shift_a)
    factor = HEAD_DIM ** (-0.5)
    query = low(low_back(matmul(mixed_a, w_qkv[0])) * factor).reshape(TOK_DEV, HEADS, HEAD_DIM)
    keys = low(low_back(matmul(mixed_a, w_qkv[1]))).reshape(TOK_DEV, HEADS, HEAD_DIM)
    values = low(low_back(matmul(mixed_a, w_qkv[2]))).reshape(TOK_DEV, HEADS, HEAD_DIM)
    scores = low_back(jnp.einsum('qhd,khd->hqk', query, keys, precision=highest))
    same = matmul(member, member.T) > 0.5
    scores = jnp.where(same[None], scores, -1e+30)
    probs = jax.nn.softmax(scores, axis=-1)
    heads_out = jnp.einsum('hqk,khd->qhd', low(probs), values, precision=highest).reshape(TOK_DEV, D)
    attended = low_back(matmul(low_back(low(heads_out)), w_out))
    middle = tokens + gate_a * attended
    mixed_b = low(layer_norm(middle) * (1.0 + scale_b) + shift_b)
    hidden_pre = low_back(matmul(mixed_b, w_up) + b_up)
    hidden = low_back(low(jax.nn.gelu(hidden_pre, approximate=False)))
    return middle + gate_b * low_back(matmul(hidden, w_down))

def forward(tokens, noise_emb, group_table, w_qkv, w_out, w_up, b_up, w_down, w_mod, b_mod, members, group_hot):
    cond = noise_emb + matmul(group_hot, group_table)
    modes = low_back(matmul(low(jax.nn.silu(cond)), w_mod.reshape(D, 6 * D)) + b_mod.reshape(6 * D))
    modes = modes.reshape(N_WIDE, SLOTS, 6, D)
    layer = jax.checkpoint(group_layer)

    def advance(carry, item):
        return (carry, layer(item[0], item[1], item[2], w_qkv, w_out, w_up, b_up, w_down))
    start = jnp.zeros((), jnp.float32)
    _, outputs = lax.scan(advance, start, (tokens.reshape(N_WIDE, TOK_DEV, D), modes, members))
    return outputs.reshape(TOKENS, D)

def reference(tokens, cotangent, noise_emb, offsets, lengths, group_ids, group_table, w_qkv, w_out, w_up, b_up, w_down, w_mod, b_mod):
    members = jax.vmap(member_table)(offsets, lengths)
    group_hot = (group_ids.reshape(IMAGES)[:, None] == jnp.arange(GROUPS, dtype=jnp.int32)[None, :]).astype(jnp.float32)
    floats = [tokens, noise_emb, group_table, w_qkv, w_out, w_up, b_up, w_down, w_mod, b_mod]
    floats = [item.astype(jnp.float32) for item in floats]

    def wrapped(tok_f, noise_f, table_f, qkv_f, out_f, up_f, bias_up, down_f, mod_f, bias_mod):
        return forward(tok_f, noise_f, table_f, qkv_f, out_f, up_f, bias_up, down_f, mod_f, bias_mod, members, group_hot)
    result, pullback = jax.vjp(wrapped, *floats)
    grads = pullback(cotangent.astype(jnp.float32))
    return (result.astype(jnp.bfloat16), grads[0].astype(jnp.bfloat16), grads[1], grads[2], grads[3], grads[4], grads[5], grads[6], grads[7], grads[8], grads[9])
```

```python
import jax
import jax.numpy as jnp
from jax import lax
from jax.experimental import pallas as pl
from jax.experimental.pallas import tpu as pltpu
from jax.sharding import PartitionSpec as P

HEAD_DIM = 128
SPAN = 64
MASKED = -1e30

f32 = jnp.float32
half = jnp.bfloat16
highest = lax.Precision.HIGHEST
MIB = 1 << 20


def dot(left, right, dims):
    return lax.dot_general(left, right, (dims, ((), ())), preferred_element_type=f32)


def spec(shape, index):
    return pl.BlockSpec(shape, index)


def params(mib=56):
    return pltpu.CompilerParams(vmem_limit_bytes=mib * MIB)


def hop(values, distance, size):
    return lax.ppermute(values, "narrow", [(i, i ^ distance) for i in range(size)])


def spread(shard, size):
    if size != 4:
        return [shard] + [hop(shard, d, size) for d in range(1, size)]
    mid = shard.shape[0] // 2
    one = hop(shard, 1, size)
    two = hop(shard, 2, size)
    first = hop(two[:mid], 1, size)
    second = hop(one[mid:], 2, size)
    return [shard, one, two, jnp.concatenate([first, second], axis=0)]


def collect(chunks, size):
    own = chunks[0].astype(f32)
    if size != 4:
        for d in range(1, size):
            own = own + hop(chunks[d].astype(half), d, size).astype(f32)
        return own
    mid = chunks[0].shape[0] // 2
    far = chunks[3].astype(half)
    one = chunks[1]
    two = chunks[2]
    via_two = hop(far[:mid], 2, size)
    via_one = hop(far[mid:], 1, size)
    one = jnp.concatenate(
        [(one[:mid].astype(f32) + via_two.astype(f32)).astype(half), one[mid:].astype(half)], axis=0
    )
    two = jnp.concatenate(
        [two[:mid].astype(half), (two[mid:].astype(f32) + via_one.astype(f32)).astype(half)], axis=0
    )
    return own + hop(one, 1, size).astype(f32) + hop(two, 2, size).astype(f32)


def in_order(pieces, index, axis=0):
    step = pieces[0].shape[axis]
    shape = list(pieces[0].shape)
    shape[axis] = step * len(pieces)
    joined = jnp.zeros(shape, pieces[0].dtype)
    for d, piece in enumerate(pieces):
        joined = lax.dynamic_update_slice_in_dim(joined, piece, (index ^ d) * step, axis)
    return joined


def modes_kernel(silu_ref, w_ref, b_ref, out_ref):
    out_ref[0] = (
        jnp.dot(silu_ref[...], w_ref[0], preferred_element_type=f32) + b_ref[0]
    )


def modes_call(silu_low, w_mod, b_mod):
    slots, width = silu_low.shape
    local = w_mod.shape[2]
    return pl.pallas_call(
        modes_kernel,
        grid=(6,),
        in_specs=[
            spec((slots, width), lambda g: (0, 0)),
            spec((1, width, local), lambda g: (g, 0, 0)),
            spec((1, 1, local), lambda g: (g, 0, 0)),
        ],
        out_specs=spec((1, slots, local), lambda g: (g, 0, 0)),
        out_shape=jax.ShapeDtypeStruct((6, slots, local), f32),
        compiler_params=params(),
        name="modes",
    )(silu_low, w_mod, b_mod[:, None, :])


def silu_back_kernel(d_ref, w_ref, out_ref):
    part = dot(d_ref[0], w_ref[0], ((1,), (1,)))

    @pl.when(pl.program_id(0) == 0)
    def _():
        out_ref[...] = part

    @pl.when(pl.program_id(0) > 0)
    def _():
        out_ref[...] = out_ref[...] + part


def silu_back_call(d_modes, w_mod):
    groups, slots, local = d_modes.shape
    width = w_mod.shape[1]
    return pl.pallas_call(
        silu_back_kernel,
        grid=(groups,),
        in_specs=[
            spec((1, slots, local), lambda g: (g, 0, 0)),
            spec((1, width, local), lambda g: (g, 0, 0)),
        ],
        out_specs=spec((slots, width), lambda g: (0, 0)),
        out_shape=jax.ShapeDtypeStruct((slots, width), f32),
        compiler_params=params(),
        name="silu_back",
    )(d_modes, w_mod)


def mix_kernel(order_ref, slot_ref, tok_ref, shift_ref, scale_ref, out_ref):
    step = pl.program_id(0)
    spans = tok_ref.shape[0] // SPAN
    for i in range(spans):
        rows = slice(i * SPAN, (i + 1) * SPAN)
        slot = slot_ref[step * spans + i]
        values = tok_ref[rows, :].astype(f32)
        centred = values - jnp.mean(values, axis=-1, keepdims=True)
        recip = lax.rsqrt(jnp.mean(centred * centred, axis=-1, keepdims=True) + 1e-06)
        shift = shift_ref[0, pl.ds(slot, 1), :]
        scale = scale_ref[0, pl.ds(slot, 1), :]
        out_ref[rows, :] = (centred * recip * (1.0 + scale) + shift).astype(half)


def gate_kernel(order_ref, slot_ref, grad_ref, gate_ref, out_ref):
    step = pl.program_id(0)
    spans = grad_ref.shape[0] // SPAN
    for i in range(spans):
        rows = slice(i * SPAN, (i + 1) * SPAN)
        gate = gate_ref[0, pl.ds(slot_ref[step * spans + i], 1), :]
        out_ref[rows, :] = (grad_ref[rows, :].astype(f32) * gate).astype(half)


def by_chunk(kernel, name, order, slots, values, modes, columns):
    rows, width = values.shape
    chunk = rows // order.shape[0]
    count = modes.shape[1]
    mode_specs = [
        spec((1, count, width), lambda i, o, s, column=column: (column, 0, 0)) for column in columns
    ]
    return pl.pallas_call(
        kernel,
        grid_spec=pltpu.PrefetchScalarGridSpec(
            num_scalar_prefetch=2,
            grid=(order.shape[0],),
            in_specs=[spec((chunk, width), lambda i, o, s: (o[i], 0))] + mode_specs,
            out_specs=spec((chunk, width), lambda i, o, s: (i, 0)),
        ),
        out_shape=jax.ShapeDtypeStruct((rows, width), half),
        compiler_params=params(),
        name=name,
    )(order, slots, values, *([modes] * len(columns)))


def attend_kernel(q_ref, k_ref, v_ref, qcode_ref, kcode_ref, out_ref, lse_ref):
    heads = q_ref.shape[1] // HEAD_DIM
    for h in range(heads):
        cols = slice(h * HEAD_DIM, (h + 1) * HEAD_DIM)
        keys = jnp.concatenate([k_ref[:, cols], kcode_ref[...]], axis=1)
        query = jnp.concatenate([q_ref[:, cols], qcode_ref[...]], axis=1)
        scores = dot(keys, query, ((1,), (1,)))
        top = jnp.max(scores, axis=0, keepdims=True)
        expo = jnp.exp(scores - top)
        total = jnp.sum(expo, axis=0, keepdims=True)
        out = dot(v_ref[:, cols], expo.astype(half), ((0,), (0,)))
        out_ref[:, cols] = (out / total).T.astype(half)
        lse_ref[0, h : h + 1, :] = top + jnp.log(total)


def attend_call(query, keys, values, qcode, kcode, chunks):
    rows, local = query.shape
    chunk = rows // chunks
    heads = local // HEAD_DIM
    whole = lambda i: (0, 0)
    part = lambda i: (i, 0)
    return pl.pallas_call(
        attend_kernel,
        grid=(chunks,),
        in_specs=[
            spec((chunk, local), part),
            spec((rows, local), whole),
            spec((rows, local), whole),
            spec((chunk, HEAD_DIM), part),
            spec((rows, HEAD_DIM), whole),
        ],
        out_specs=[spec((chunk, local), part), spec((1, heads, chunk), lambda i: (i, 0, 0))],
        out_shape=[
            jax.ShapeDtypeStruct((rows, local), half),
            jax.ShapeDtypeStruct((chunks, heads, chunk), f32),
        ],
        compiler_params=params(),
        cost_estimate=pl.CostEstimate(
            flops=6 * rows * rows * local, transcendentals=rows * rows * heads, bytes_accessed=8 * rows * local
        ),
        name="attend",
    )(query, keys, values, qcode, kcode)


def attend_back_kernel(q_ref, k_ref, v_ref, qcode_ref, kcode_ref, d_ref, lse_ref, dq_ref, dk_ref, dv_ref, dk_acc, dv_acc):
    heads = q_ref.shape[1] // HEAD_DIM
    step = pl.program_id(0)
    factor = HEAD_DIM ** (-0.5)

    @pl.when(step == 0)
    def _():
        dk_acc[...] = jnp.zeros_like(dk_acc)
        dv_acc[...] = jnp.zeros_like(dv_acc)

    for h in range(heads):
        cols = slice(h * HEAD_DIM, (h + 1) * HEAD_DIM)
        keys = jnp.concatenate([k_ref[:, cols], kcode_ref[...]], axis=1)
        query = jnp.concatenate([q_ref[:, cols], qcode_ref[...]], axis=1)
        grad = d_ref[:, cols]
        scores = dot(keys, query, ((1,), (1,)))
        probs = jnp.exp(scores - lse_ref[0, h : h + 1, :])
        d_probs = dot(v_ref[:, cols], grad, ((1,), (1,)))
        inner = jnp.sum(probs * d_probs, axis=0, keepdims=True)
        d_scores = (probs * (d_probs - inner)).astype(half)
        dv_acc[:, cols] += dot(probs.astype(half), grad, ((1,), (0,)))
        dk_acc[:, cols] += dot(d_scores, q_ref[:, cols], ((1,), (0,)))
        dq = dot(k_ref[:, cols], d_scores, ((0,), (0,)))
        dq_ref[:, cols] = (dq.T * factor).astype(half)

    @pl.when(step == pl.num_programs(0) - 1)
    def _():
        dk_ref[...] = dk_acc[...].astype(half)
        dv_ref[...] = dv_acc[...].astype(half)


def attend_back_call(query, keys, values, qcode, kcode, d_heads, lse):
    rows, local = query.shape
    chunks, heads, chunk = lse.shape
    whole = lambda i: (0, 0)
    part = lambda i: (i, 0)
    shape = jax.ShapeDtypeStruct((rows, local), half)
    return pl.pallas_call(
        attend_back_kernel,
        grid=(chunks,),
        in_specs=[
            spec((chunk, local), part),
            spec((rows, local), whole),
            spec((rows, local), whole),
            spec((chunk, HEAD_DIM), part),
            spec((rows, HEAD_DIM), whole),
            spec((chunk, local), part),
            spec((1, heads, chunk), lambda i: (i, 0, 0)),
        ],
        out_specs=[spec((chunk, local), part), spec((rows, local), whole), spec((rows, local), whole)],
        out_shape=[shape, shape, shape],
        scratch_shapes=[pltpu.VMEM((rows, local), f32), pltpu.VMEM((rows, local), f32)],
        compiler_params=params(),
        cost_estimate=pl.CostEstimate(
            flops=14 * rows * rows * local, transcendentals=rows * rows * heads, bytes_accessed=16 * rows * local
        ),
        name="attend_back",
    )(query, keys, values, qcode, kcode, d_heads, lse)


def mlp_kernel(x_ref, up_ref, b_ref, d_ref, hidden_ref, d_pre_ref, dx_ref, acc_ref):
    step = pl.program_id(0)
    pre = jnp.dot(x_ref[...], up_ref[...], preferred_element_type=f32) + b_ref[...]
    cumul = 0.5 * (1.0 + lax.erf(pre * 0.7071067811865476))
    density = jnp.exp(-0.5 * pre * pre) * 0.3989422804014327
    hidden_ref[...] = (pre * cumul).astype(half)
    d_pre = (d_ref[...].astype(f32) * (cumul + pre * density)).astype(half)
    d_pre_ref[...] = d_pre
    part = dot(d_pre, up_ref[...], ((1,), (1,)))

    @pl.when(step == 0)
    def _():
        acc_ref[...] = part

    @pl.when(step > 0)
    def _():
        acc_ref[...] += part

    @pl.when(step == pl.num_programs(0) - 1)
    def _():
        dx_ref[...] = acc_ref[...].astype(half)


def mlp_call(mixed, w_up, b_up, d_hidden):
    rows, width = mixed.shape
    ff = w_up.shape[1]
    block = min(512, ff)
    return pl.pallas_call(
        mlp_kernel,
        grid=(ff // block,),
        in_specs=[
            spec((rows, width), lambda j: (0, 0)),
            spec((width, block), lambda j: (0, j)),
            spec((1, block), lambda j: (0, j)),
            spec((rows, block), lambda j: (0, j)),
        ],
        out_specs=[
            spec((rows, block), lambda j: (0, j)),
            spec((rows, block), lambda j: (0, j)),
            spec((rows, width), lambda j: (0, 0)),
        ],
        out_shape=[
            jax.ShapeDtypeStruct((rows, ff), half),
            jax.ShapeDtypeStruct((rows, ff), half),
            jax.ShapeDtypeStruct((rows, width), half),
        ],
        scratch_shapes=[pltpu.VMEM((rows, width), f32)],
        compiler_params=params(),
        cost_estimate=pl.CostEstimate(
            flops=4 * rows * width * ff, transcendentals=rows * ff, bytes_accessed=2 * width * ff + 6 * rows * ff
        ),
        name="mlp",
    )(mixed, w_up, b_up[None, :], d_hidden)


def normalize(values):
    centred = values - jnp.mean(values, axis=-1, keepdims=True)
    recip = lax.rsqrt(jnp.mean(centred * centred, axis=-1, keepdims=True) + 1e-06)
    return (centred * recip, recip)


def norm_back(grad, normed, recip):
    first = jnp.mean(grad, axis=-1, keepdims=True)
    second = jnp.mean(grad * normed, axis=-1, keepdims=True)
    return recip * (grad - first - normed * second)


def after(values, *others):
    return lax.optimization_barrier((values, *others))[0]


def make_body(n_wide, n_narrow):
    def body(
        tokens,
        cotangent,
        noise_emb,
        offsets,
        lengths,
        group_ids,
        group_table,
        w_qkv,
        w_out,
        w_up,
        b_up,
        w_down,
        w_mod,
        b_mod,
    ):
        tok_dev, width = tokens.shape
        slots = offsets.shape[1]
        local = w_qkv.shape[2]
        groups = group_table.shape[0]
        rows = tok_dev // n_narrow
        spans = rows // SPAN
        me = lax.axis_index("narrow")
        place = lax.axis_index("wide")
        order = me ^ jnp.arange(n_narrow, dtype=jnp.int32)

        starts = (order[:, None] * spans + jnp.arange(spans, dtype=jnp.int32)[None, :]).reshape(-1, 1) * SPAN
        inside = (starts >= offsets) & (starts < offsets + lengths)
        slot_hot = inside.astype(f32)
        slot_of = jnp.sum(inside * jnp.arange(slots, dtype=jnp.int32)[None, :], axis=1).astype(jnp.int32)
        lanes = jnp.arange(HEAD_DIM, dtype=jnp.int32)
        same = jnp.repeat(slot_of, SPAN)[:, None] == lanes[None, :]
        kcode = same.astype(half)
        qcode = jnp.where(same, 0.0, MASKED).astype(half)

        group_hot = (group_ids[0][:, None] == jnp.arange(groups, dtype=jnp.int32)[None, :]).astype(f32)
        cond = noise_emb + jnp.dot(group_hot, group_table, precision=highest)
        silu_low = jax.nn.silu(cond).astype(half)
        w_mod_t = w_mod.transpose(1, 0, 2)
        modes_own = modes_call(silu_low, w_mod_t, b_mod)
        modes = in_order([modes_own] + [hop(modes_own, d, n_narrow) for d in range(1, n_narrow)], me, 2)

        mixed_a = by_chunk(mix_kernel, "mix_a", order, slot_of, tokens, modes, (0, 1))
        factor = HEAD_DIM ** (-0.5)
        query = (jnp.dot(mixed_a, w_qkv[0], preferred_element_type=f32) * factor).astype(half)
        keys = jnp.dot(mixed_a, w_qkv[1], preferred_element_type=f32).astype(half)
        values = jnp.dot(mixed_a, w_qkv[2], preferred_element_type=f32).astype(half)
        heads_out, lse = attend_call(query, keys, values, qcode, kcode, n_narrow)

        def chunk(array, d):
            return array[d * rows : (d + 1) * rows]

        sent = [
            jnp.dot(chunk(heads_out, d), w_out, preferred_element_type=f32).astype(half if d else f32)
            for d in range(n_narrow)
        ]
        attended = collect(sent, n_narrow)

        mine = jnp.einsum("bs,gsv->gbv", slot_hot[:spans], modes, precision=highest)

        def per_token(column):
            return jnp.broadcast_to(mine[column][:, None, :], (spans, SPAN, width)).reshape(rows, width)

        tok_own = lax.dynamic_slice_in_dim(tokens, me * rows, rows, 0).astype(f32)
        grad_own = lax.dynamic_slice_in_dim(cotangent, me * rows, rows, 0).astype(f32)
        middle = tok_own + per_token(2) * attended
        normed_b, recip_b = normalize(middle)
        mixed_own = (normed_b * (1.0 + per_token(4)) + per_token(3)).astype(half)
        mixed_b = spread(mixed_own, n_narrow)

        d_mlp = by_chunk(gate_kernel, "d_mlp", order, slot_of, cotangent, modes, (5,))
        d_hidden = dot(d_mlp, w_down, ((1,), (1,))).astype(half)
        hidden, d_pre, d_mixed = [], [], []
        for d in range(n_narrow):
            outs = mlp_call(mixed_b[d], w_up, b_up, chunk(d_hidden, d))
            hidden.append(outs[0])
            d_pre.append(outs[1])
            d_mixed.append(outs[2])
        d_mixed_b = collect(d_mixed, n_narrow)

        d_middle = grad_own + norm_back(d_mixed_b * (1.0 + per_token(4)), normed_b, recip_b)
        d_attn_own = (d_middle * per_token(2)).astype(half)
        d_attn = jnp.concatenate(spread(d_attn_own, n_narrow), axis=0)

        hidden = jnp.concatenate(hidden, axis=0)
        d_pre = jnp.concatenate(d_pre, axis=0)
        mixed_b = jnp.concatenate(mixed_b, axis=0)
        grad_b_up = jnp.sum(d_pre.astype(f32), axis=0)
        grad_w_down = dot(d_mlp, hidden, ((0,), (0,))).astype(half)
        grad_w_up = dot(mixed_b, d_pre, ((0,), (0,))).astype(half)
        sum_w_down = lax.psum_scatter(grad_w_down, "wide", scatter_dimension=0, tiled=True)
        sum_w_up = lax.psum_scatter(grad_w_up, "wide", scatter_dimension=0, tiled=True)

        mlp_sent = [
            jnp.dot(chunk(hidden, d), w_down, preferred_element_type=f32).astype(half if d else f32)
            for d in range(n_narrow)
        ]
        mlp_out = collect(mlp_sent, n_narrow)
        result_own = (middle + per_token(5) * mlp_out).astype(half)
        result = in_order(spread(result_own, n_narrow), me)

        d_heads = dot(d_attn, w_out, ((1,), (1,))).astype(half)
        grad_w_out = dot(d_attn, heads_out, ((0,), (0,))).astype(half)
        sum_w_out = lax.psum_scatter(grad_w_out, "wide", scatter_dimension=0, tiled=True)
        d_query, d_key, d_value = attend_back_call(query, keys, values, qcode, kcode, d_heads, lse)
        d_proj = jnp.concatenate([d_query, d_key, d_value], axis=1)
        w_flat = jnp.concatenate([w_qkv[0], w_qkv[1], w_qkv[2]], axis=1)
        sent_a = [
            dot(chunk(d_proj, d), w_flat, ((1,), (1,))).astype(half if d else f32) for d in range(n_narrow)
        ]
        d_mixed_a = collect(sent_a, n_narrow)
        grad_w_qkv = dot(mixed_a, d_proj, ((0,), (0,))).astype(half)
        sum_w_qkv = lax.psum_scatter(grad_w_qkv, "wide", scatter_dimension=0, tiled=True)

        normed_a, recip_a = normalize(tok_own)
        grad_tok_own = (d_middle + norm_back(d_mixed_a * (1.0 + per_token(1)), normed_a, recip_a)).astype(half)
        grad_tokens = in_order(spread(grad_tok_own, n_narrow), me)

        def span_sums(terms):
            return jnp.sum(terms.reshape(spans, SPAN, width), axis=1)

        sums = jnp.stack(
            [
                span_sums(d_mixed_a),
                span_sums(d_mixed_a * normed_a),
                span_sums(d_middle * attended),
                span_sums(d_mixed_b),
                span_sums(d_mixed_b * normed_b),
                span_sums(grad_own * mlp_out),
            ]
        )
        pieces = [
            hop(lax.dynamic_slice_in_dim(sums, (me ^ d) * local, local, 2), d, n_narrow) if d else
            lax.dynamic_slice_in_dim(sums, me * local, local, 2)
            for d in range(n_narrow)
        ]
        d_modes = jnp.einsum(
            "bs,gbv->gsv", slot_hot, jnp.concatenate(pieces, axis=1), precision=highest
        ).astype(half)
        d_silu_part = silu_back_call(d_modes, w_mod_t).astype(half)
        d_silu = d_silu_part.astype(f32)
        for d in range(1, n_narrow):
            d_silu = d_silu + hop(d_silu_part, d, n_narrow).astype(f32)
        sigma = jax.nn.sigmoid(cond)
        grad_noise = d_silu * sigma * (1.0 + cond * (1.0 - sigma))
        table_part = jnp.dot(group_hot.T, grad_noise, precision=highest).astype(half)

        col = width // n_wide
        silu_all = lax.all_gather(silu_low, "wide", axis=0, tiled=True)
        silu_cols = lax.dynamic_slice_in_dim(silu_all, place * col, col, 1)
        b_up_all = lax.all_gather(grad_b_up.astype(half), "wide", axis=0)
        ff_part = b_up_all.shape[1] // n_wide
        sum_b_up = jnp.sum(
            lax.dynamic_slice_in_dim(b_up_all, place * ff_part, ff_part, 1).astype(f32), axis=0
        )
        d_modes_all = lax.all_gather(d_modes, "wide", axis=1, tiled=True)
        grad_w_mod = jnp.einsum("sd,gsv->gdv", silu_cols, d_modes_all, preferred_element_type=f32).transpose(1, 0, 2)
        part_b = local // n_wide
        sum_b_mod = jnp.sum(
            lax.dynamic_slice_in_dim(d_modes_all, place * part_b, part_b, 2).astype(f32), axis=1
        )
        table_all = lax.all_gather(table_part, "wide", axis=0)
        sum_table = jnp.sum(lax.dynamic_slice_in_dim(table_all, place * col, col, 2).astype(f32), axis=0)

        out_qkv = sum_w_qkv.astype(f32).reshape(col, 3, local).transpose(1, 0, 2)
        return (
            result,
            grad_tokens,
            grad_noise,
            sum_table,
            out_qkv,
            sum_w_out.astype(f32).T,
            sum_w_up.astype(f32),
            sum_b_up,
            sum_w_down.astype(f32).T,
            grad_w_mod,
            sum_b_mod,
        )

    return body


def solution(mesh):
    in_specs = (
        P("wide", None),
        P("wide", None),
        P("wide", None),
        P("wide", None),
        P("wide", None),
        P("wide", None),
        P(),
        P(None, None, "narrow"),
        P("narrow", None),
        P(None, "narrow"),
        P("narrow"),
        P("narrow", None),
        P(None, None, "narrow"),
        P(None, "narrow"),
    )
    out_specs = (
        P("wide", None),
        P("wide", None),
        P("wide", None),
        P(None, "wide"),
        P(None, "wide", "narrow"),
        P("narrow", "wide"),
        P("wide", "narrow"),
        P(("narrow", "wide")),
        P("narrow", "wide"),
        P("wide", None, "narrow"),
        P(None, ("narrow", "wide")),
    )
    body = make_body(mesh.shape["wide"], mesh.shape["narrow"])
    return jax.shard_map(body, mesh=mesh, in_specs=in_specs, out_specs=out_specs, check_vma=False)
```

```python
import jax
import jax.numpy as jnp
from jax import lax
from jax.experimental import pallas as pl
from jax.experimental.pallas import tpu as pltpu
from jax.sharding import PartitionSpec as P

HEAD_DIM = 128
SPAN = 64
MASKED = -1e30

f32 = jnp.float32
half = jnp.bfloat16
highest = lax.Precision.HIGHEST
MIB = 1 << 20


def dot(left, right, dims):
    return lax.dot_general(left, right, (dims, ((), ())), preferred_element_type=f32)


def normalize(values):
    centred = values - jnp.mean(values, axis=-1, keepdims=True)
    recip = lax.rsqrt(jnp.mean(centred * centred, axis=-1, keepdims=True) + 1e-06)
    return (centred * recip, recip)


def norm_back(grad, normed, recip):
    first = jnp.mean(grad, axis=-1, keepdims=True)
    second = jnp.mean(grad * normed, axis=-1, keepdims=True)
    return recip * (grad - first - normed * second)


def spec(shape, index):
    return pl.BlockSpec(shape, index)


def fixed(shape):
    zeros = (0,) * len(shape)
    return pl.BlockSpec(shape, lambda *_: zeros)


def held(shape):
    zeros = (0,) * len(shape)
    return pl.BlockSpec(shape, lambda *_: zeros, pipeline_mode=pl.Buffered(1))


def in_hbm(array):
    return pltpu.with_memory_space_constraint(array, pltpu.HBM)


def params(mib):
    return pltpu.CompilerParams(vmem_limit_bytes=mib * MIB)


def cost(micros):
    return pl.CostEstimate(flops=int(micros * 1.15e+09), transcendentals=0, bytes_accessed=0)


def shaped(shape, kind):
    return jax.ShapeDtypeStruct(shape, kind)


def after(values, *others):
    return lax.optimization_barrier((values, *others))[0]


def hop(values, distance, size):
    return lax.ppermute(values, "narrow", [(i, i ^ distance) for i in range(size)])


def exchange(chunks, size):
    return [chunks[0]] + [hop(chunks[d], d, size) for d in range(1, size)]


def spread_near(shard, size):
    return [shard] + [hop(shard, d, size) for d in range(1, size if size != 4 else 3)]


def spread(near, size, *gates):
    if size != 4:
        return [[piece] for piece in near]
    one, two = near[1:]
    mid = one.shape[0] // 2
    two, one = after(two[:mid], *gates), after(one[mid:], *gates)
    return [[piece] for piece in near] + [[hop(two, 1, size), hop(one, 2, size)]]


def joined(pieces):
    return jnp.concatenate(pieces, axis=0) if len(pieces) > 1 else pieces[0]


def flat(lists):
    return [piece for pieces in lists for piece in pieces]


def collect_far(far, size):
    if size != 4:
        return []
    mid = far.shape[0] // 2
    return [hop(far[:mid], 2, size), hop(far[mid:], 1, size)]


def collect(chunks, size, via):
    if size != 4:
        return exchange(chunks, size)
    own, one, two, _ = chunks
    mid = own.shape[0] // 2
    via_two, via_one = via
    one = joined([(one[:mid].astype(f32) + via_two.astype(f32)).astype(half), one[mid:]])
    two = joined([two[:mid], (two[mid:].astype(f32) + via_one.astype(f32)).astype(half)])
    return [own, hop(one, 1, size), hop(two, 2, size)]


def in_order(pieces, index, axis):
    return jnp.concatenate([lax.select_n(index ^ k, *pieces) for k in range(len(pieces))], axis=axis)


def settle_kernel(layout, order_ref, *refs):
    out_ref = refs[-1]
    for d, count in enumerate(layout):

        @pl.when(pl.program_id(0) == d)
        def _(pieces=refs[sum(layout[:d]) :][:count]):
            at = 0
            for piece in pieces:
                out_ref[at : at + piece.shape[0], :] = piece[...]
                at += piece.shape[0]


def settle(chunks, order):
    rows = sum(piece.shape[0] for piece in chunks[0])
    width = chunks[0][0].shape[1]
    return pl.pallas_call(
        lambda *refs: settle_kernel([len(pieces) for pieces in chunks], *refs),
        grid_spec=pltpu.PrefetchScalarGridSpec(
            num_scalar_prefetch=1,
            grid=(len(chunks),),
            in_specs=[held(piece.shape) for piece in flat(chunks)],
            out_specs=spec((rows, width), lambda i, o: (o[i], 0)),
        ),
        out_shape=pltpu.HBM((rows * len(chunks), width), chunks[0][0].dtype),
        compiler_params=params(16),
        cost_estimate=cost(20),
        name="settle",
    )(order, *flat(chunks))


def modes_kernel(silu_ref, w_ref, b_ref, out_ref):
    out_ref[0] = (
        jnp.dot(silu_ref[...], w_ref[0], preferred_element_type=f32) + b_ref[0]
    )


def modes_call(silu_low, w_mod, b_mod, first, count):
    slots, width = silu_low.shape
    local = w_mod.shape[2]
    return pl.pallas_call(
        modes_kernel,
        grid=(count,),
        in_specs=[
            spec((slots, width), lambda g: (0, 0)),
            spec((1, width, local), lambda g: (first + g, 0, 0)),
            spec((1, 1, local), lambda g: (first + g, 0, 0)),
        ],
        out_specs=spec((1, slots, local), lambda g: (g, 0, 0)),
        out_shape=shaped((count, slots, local), f32),
        cost_estimate=cost(5),
        compiler_params=params(24),
        name="modes",
    )(silu_low, w_mod, b_mod[:, None, :])


def silu_back_kernel(d_ref, w_ref, out_ref):
    part = dot(d_ref[0], w_ref[0], ((1,), (1,)))

    @pl.when(pl.program_id(0) == 0)
    def _():
        out_ref[...] = part

    @pl.when(pl.program_id(0) > 0)
    def _():
        out_ref[...] = out_ref[...] + part


def silu_back_call(d_modes, w_mod, group_of):
    groups, slots, local = d_modes.shape
    width = w_mod.shape[1]
    return pl.pallas_call(
        silu_back_kernel,
        grid=(groups,),
        in_specs=[
            spec((1, slots, local), lambda g: (g, 0, 0)),
            spec((1, width, local), lambda g: (group_of(g), 0, 0)),
        ],
        out_specs=fixed((slots, width)),
        out_shape=shaped((slots, width), f32),
        compiler_params=params(16),
        cost_estimate=cost(0),
        name="silu_back",
    )(d_modes, w_mod)


def row_of(ref, slot):
    return ref[0, pl.ds(slot, 1), :]


def mix_kernel(order_ref, slot_ref, tok_ref, shift_ref, scale_ref, out_ref):
    step = pl.program_id(0)
    spans = tok_ref.shape[0] // SPAN
    for i in range(spans):
        rows = slice(i * SPAN, (i + 1) * SPAN)
        slot = slot_ref[step * spans + i]
        normed, _ = normalize(tok_ref[rows, :].astype(f32))
        out_ref[rows, :] = (normed * (1.0 + row_of(scale_ref, slot)) + row_of(shift_ref, slot)).astype(half)


def gate_kernel(order_ref, slot_ref, grad_ref, gate_ref, out_ref):
    step = pl.program_id(0)
    spans = grad_ref.shape[0] // SPAN
    for i in range(spans):
        rows = slice(i * SPAN, (i + 1) * SPAN)
        gate = row_of(gate_ref, slot_ref[step * spans + i])
        out_ref[rows, :] = (grad_ref[rows, :].astype(f32) * gate).astype(half)


def mode_specs(modes, columns):
    _, count, width = modes.shape
    return [spec((1, count, width), lambda i, *_, column=column: (column, 0, 0)) for column in columns]


def by_chunk(kernel, name, order, slots, values, modes, columns):
    rows, width = values.shape
    chunk = rows // order.shape[0]
    return pl.pallas_call(
        kernel,
        grid_spec=pltpu.PrefetchScalarGridSpec(
            num_scalar_prefetch=2,
            grid=(order.shape[0],),
            in_specs=[spec((chunk, width), lambda i, o, s: (o[i], 0))] + mode_specs(modes, columns),
            out_specs=spec((chunk, width), lambda i, o, s: (i, 0)),
        ),
        out_shape=shaped((rows, width), half),
        compiler_params=params(24),
        cost_estimate=cost(5),
        name=name,
    )(order, slots, values, *([modes] * len(columns)))


def product_kernel(dims, scales, left_ref, right_ref, out_ref):
    total = dot(left_ref[...], right_ref[...].reshape(right_ref.shape[-2:]), dims)
    if scales is not None:
        total = total * jnp.where(pl.program_id(0) == 0, scales, 1.0)
    out_ref[...] = total.astype(half).reshape(out_ref.shape)


def product(left, right, dims, name, block=512, out=shaped, micros=4, columns=None, first=0, before=None):
    free = 1 - dims[1][0]
    count = right.shape[free]
    rows = left.shape[1 - dims[0][0]]
    block = min(block, count)
    shape = (block, right.shape[1]) if free == 0 else (right.shape[0], block)
    index = (lambda j: (j, 0)) if free == 0 else (lambda j: (0, j))
    given = [] if before is None else [before]
    return pl.pallas_call(
        lambda left_ref, right_ref, *refs: product_kernel(dims, None, left_ref, right_ref, refs[-1]),
        grid=(count // block,),
        in_specs=[held(left.shape), spec(shape, index)] + [pl.BlockSpec(memory_space=pl.ANY)] * len(given),
        out_specs=spec((rows, block), lambda j: (0, first // block + j)),
        out_shape=out((rows, columns or count), half),
        input_output_aliases={2: 0} if given else {},
        compiler_params=params(28),
        cost_estimate=cost(micros),
        name=name,
    )(left, right, *given)


def project_call(mixed, w_qkv, factor):
    count, width, local = w_qkv.shape
    rows = mixed.shape[0]
    return pl.pallas_call(
        lambda *refs: product_kernel(((1,), (0,)), factor, *refs),
        grid=(count,),
        in_specs=[held(mixed.shape), spec((1, width, local), lambda i: (i, 0, 0))],
        out_specs=spec((1, rows, local), lambda i: (i, 0, 0)),
        out_shape=shaped((count, rows, local), half),
        compiler_params=params(28),
        cost_estimate=cost(9),
        name="project",
    )(mixed, w_qkv)


def attend_kernel(q_ref, k_ref, v_ref, qcode_ref, kcode_ref, w_ref, heads_ref, lse_ref, out_ref):
    heads = q_ref.shape[2] // HEAD_DIM
    for h in range(heads):
        cols = slice(h * HEAD_DIM, (h + 1) * HEAD_DIM)
        keys = jnp.concatenate([k_ref[0, :, cols], kcode_ref[...]], axis=1)
        query = jnp.concatenate([q_ref[0, :, cols], qcode_ref[...]], axis=1)
        scores = dot(keys, query, ((1,), (1,)))
        top = jnp.max(scores, axis=0, keepdims=True)
        expo = jnp.exp(scores - top)
        total = jnp.sum(expo, axis=0, keepdims=True)
        out = dot(v_ref[0, :, cols], expo.astype(half), ((0,), (0,)))
        heads_ref[:, cols] = (out / total).T.astype(half)
        lse_ref[0, h : h + 1, :] = top + jnp.log(total)
    out_ref[...] = jnp.dot(heads_ref[...], w_ref[...], preferred_element_type=f32).astype(half)


def attend_call(qkv, qcode, kcode, w_out, chunk, first, count):
    _, rows, local = qkv.shape
    width = w_out.shape[1]
    heads = local // HEAD_DIM
    return pl.pallas_call(
        attend_kernel,
        grid=(count,),
        in_specs=[
            spec((1, chunk, local), lambda i: (0, first + i, 0)),
            spec((1, rows, local), lambda i: (1, 0, 0)),
            spec((1, rows, local), lambda i: (2, 0, 0)),
            spec((chunk, HEAD_DIM), lambda i: (first + i, 0)),
            fixed((rows, HEAD_DIM)),
            held(w_out.shape),
        ],
        out_specs=[
            spec((chunk, local), lambda i: (i, 0)),
            spec((1, heads, chunk), lambda i: (i, 0, 0)),
            spec((chunk, width), lambda i: (i, 0)),
        ],
        out_shape=[
            shaped((count * chunk, local), half),
            shaped((count, heads, chunk), f32),
            shaped((count * chunk, width), half),
        ],
        compiler_params=params(32),
        cost_estimate=cost(2 + 3.3 * count),
        name="attend",
    )(qkv, qkv, qkv, qcode, kcode, w_out)


def attend_back_kernel(final, layout, q_ref, k_ref, v_ref, qcode_ref, kcode_ref, lse_ref, w_ref, *refs):
    chunk, local = q_ref.shape[1:]
    pieces, refs, d_heads_ref = refs[: sum(layout)], refs[sum(layout) : -1], refs[-1]
    heads = local // HEAD_DIM
    step = pl.program_id(0)
    factor = HEAD_DIM ** (-0.5)
    if final:
        dk_old, dv_old, dq_ref, dk_ref, dv_ref, dk_acc, dv_acc = refs
    else:
        dq_ref, dk_acc, dv_acc = refs

    @pl.when(step == 0)
    def _():
        dk_acc[...] = dk_old[...] if final else jnp.zeros_like(dk_acc)
        dv_acc[...] = dv_old[...] if final else jnp.zeros_like(dv_acc)

    for d, count in enumerate(layout):

        @pl.when(step == d)
        def _(refs=pieces[sum(layout[:d]) :][:count]):
            at = 0
            for ref in refs:
                d_heads_ref[at : at + ref.shape[0], :] = dot(ref[...], w_ref[...], ((1,), (1,))).astype(half)
                at += ref.shape[0]

    for h in range(heads):
        cols = slice(h * HEAD_DIM, (h + 1) * HEAD_DIM)
        keys = jnp.concatenate([k_ref[0, :, cols], kcode_ref[...]], axis=1)
        query = jnp.concatenate([q_ref[0, :, cols], qcode_ref[...]], axis=1)
        grad = d_heads_ref[:, cols]
        scores = dot(keys, query, ((1,), (1,)))
        probs = jnp.exp(scores - lse_ref[0, h : h + 1, :])
        d_probs = dot(v_ref[0, :, cols], grad, ((1,), (1,)))
        inner = jnp.sum(probs * d_probs, axis=0, keepdims=True)
        d_scores = (probs * (d_probs - inner)).astype(half)
        dv_acc[:, cols] += dot(probs.astype(half), grad, ((1,), (0,)))
        dk_acc[:, cols] += dot(d_scores, q_ref[0, :, cols], ((1,), (0,)))
        dq = dot(k_ref[0, :, cols], d_scores, ((0,), (0,)))
        dq_ref[:, cols] = (dq.T * factor).astype(half)

    if final:

        @pl.when(step == pl.num_programs(0) - 1)
        def _():
            dk_ref[...] = dk_acc[...].astype(half)
            dv_ref[...] = dv_acc[...].astype(half)


def attend_back_call(qkv, qcode, kcode, lse, w_out, d_attn, first, sums):
    _, rows, local = qkv.shape
    _, heads, chunk = lse.shape
    count = len(d_attn)
    final = sums is not None
    whole = (rows, local)
    return pl.pallas_call(
        lambda *refs: attend_back_kernel(final, [len(pieces) for pieces in d_attn], *refs),
        grid=(count,),
        in_specs=[
            spec((1, chunk, local), lambda i: (0, first + i, 0)),
            spec((1, rows, local), lambda i: (1, 0, 0)),
            spec((1, rows, local), lambda i: (2, 0, 0)),
            spec((chunk, HEAD_DIM), lambda i: (first + i, 0)),
            fixed((rows, HEAD_DIM)),
            spec((1, heads, chunk), lambda i: (first + i, 0, 0)),
            held(w_out.shape),
        ]
        + [held(piece.shape) for piece in flat(d_attn)]
        + ([held(whole)] * 2 if final else []),
        out_specs=[spec((chunk, local), lambda i: (i, 0))] + [fixed(whole)] * 2,
        out_shape=[shaped((count * chunk, local), half)] + [shaped(whole, half if final else f32)] * 2,
        scratch_shapes=([pltpu.VMEM(whole, f32)] * 2 if final else []) + [pltpu.VMEM((chunk, local), half)],
        compiler_params=params(36),
        cost_estimate=cost(2 if final else 130),
        name="attend_back",
    )(qkv, qkv, qkv, qcode, kcode, lse, w_out, *flat(d_attn), *(sums if final else []))


def project_back_kernel(q_ref, k_ref, v_ref, w_ref, out_ref):
    total = None
    for i, ref in enumerate((q_ref, k_ref, v_ref)):
        part = dot(ref[...], w_ref[i], ((1,), (1,)))
        total = part if total is None else total + part
    out_ref[...] = total.astype(half)


def project_back_call(d_query, d_key, d_value, w_qkv, chunk, first, count, first_query):
    _, width, local = w_qkv.shape
    there = lambda i: (first + i, 0)
    return pl.pallas_call(
        project_back_kernel,
        grid=(count,),
        in_specs=[
            spec((chunk, local), lambda i: (first - first_query + i, 0)),
            spec((chunk, local), there),
            spec((chunk, local), there),
            held(w_qkv.shape),
        ],
        out_specs=spec((chunk, width), lambda i: (i, 0)),
        out_shape=shaped((count * chunk, width), half),
        compiler_params=params(32),
        cost_estimate=cost(2),
        name="project_back",
    )(d_query, d_key, d_value, w_qkv)


def total_of(terms):
    return jnp.sum(terms, axis=0, keepdims=True)


def mlp_kernel(count, *refs):
    x_refs = refs[:count]
    up_ref, b_ref, d_ref = refs[count : count + 3]
    hidden_ref, d_pre_ref, dx_ref, b_sum_ref, acc_ref = refs[-5:]
    step = pl.program_id(0)
    mixed = jnp.concatenate([ref[...] for ref in x_refs], axis=0) if count > 1 else x_refs[0][...]
    pre = jnp.dot(mixed, up_ref[...], preferred_element_type=f32) + b_ref[...]
    cumul = 0.5 * (1.0 + lax.erf(pre * 0.7071067811865476))
    density = jnp.exp(-0.5 * pre * pre) * 0.3989422804014327
    hidden_ref[...] = (pre * cumul).astype(half)
    d_pre = (d_ref[...].astype(f32) * (cumul + pre * density)).astype(half)
    d_pre_ref[...] = d_pre
    b_sum_ref[...] = total_of(d_pre.astype(f32))
    part = dot(d_pre, up_ref[...], ((1,), (1,)))

    @pl.when(step == 0)
    def _():
        acc_ref[...] = part

    @pl.when(step > 0)
    def _():
        acc_ref[...] += part

    @pl.when(step == pl.num_programs(0) - 1)
    def _():
        dx_ref[...] = acc_ref[...].astype(half)


def mlp_call(pieces, w_up, b_up, d_hidden, chunk, before):
    rows = sum(piece.shape[0] for piece in pieces)
    width, ff = w_up.shape
    block = min(1024, ff)
    here = lambda j: (chunk, j)
    operands = [*pieces, w_up, b_up[None, :], d_hidden]
    in_specs = [held(piece.shape) for piece in pieces] + [
        spec((width, block), lambda j: (0, j)),
        spec((1, block), lambda j: (0, j)),
        spec((rows, block), here),
    ]
    aliases = {}
    if before is not None:
        aliases = {len(operands): 0, len(operands) + 1: 1}
        operands += before
        in_specs += [pl.BlockSpec(memory_space=pl.ANY)] * 2
    return pl.pallas_call(
        lambda *refs: mlp_kernel(len(pieces), *refs),
        grid=(ff // block,),
        in_specs=in_specs,
        out_specs=[
            spec((rows, block), here),
            spec((rows, block), here),
            fixed((rows, width)),
            spec((1, block), lambda j: (0, j)),
        ],
        out_shape=[
            shaped((d_hidden.shape[0], ff), half),
            shaped((d_hidden.shape[0], ff), half),
            shaped((rows, width), half),
            shaped((1, ff), f32),
        ],
        scratch_shapes=[pltpu.VMEM((rows, width), f32)],
        input_output_aliases=aliases,
        compiler_params=params(28),
        cost_estimate=cost(3),
        name="mlp",
    )(*operands)


def summed(refs):
    total = refs[0][...].astype(f32)
    for ref in refs[1:]:
        total = total + ref[...].astype(f32)
    return total


def middle_kernel(count, first_ref, slot_ref, *refs):
    tok_ref, gate_ref, shift_ref, scale_ref, mixed_ref, attended_ref = refs[count:]
    slot = slot_ref[pl.program_id(0)]
    attended = summed(refs[:count])
    attended_ref[...] = attended
    normed, _ = normalize(tok_ref[...].astype(f32) + row_of(gate_ref, slot) * attended)
    mixed_ref[...] = (normed * (1.0 + row_of(scale_ref, slot)) + row_of(shift_ref, slot)).astype(half)


def back_b_kernel(count, first_ref, slot_ref, *refs):
    tok_ref, grad_ref, attended_ref, gate_ref, scale_ref, d_attn_ref, d_middle_ref, sums_ref = refs[count:]
    slot = slot_ref[pl.program_id(0)]
    gate = row_of(gate_ref, slot)
    attended = attended_ref[...]
    normed, recip = normalize(tok_ref[...].astype(f32) + gate * attended)
    d_mixed = summed(refs[:count])
    back = norm_back(d_mixed * (1.0 + row_of(scale_ref, slot)), normed, recip)
    d_middle = grad_ref[...].astype(f32) + back
    d_middle_ref[...] = d_middle
    d_attn_ref[...] = (d_middle * gate).astype(half)
    sums_ref[0, 0:1, :] = total_of(d_middle * attended)
    sums_ref[0, 1:2, :] = total_of(d_mixed)
    sums_ref[0, 2:3, :] = total_of(d_mixed * normed)


def back_a_kernel(count, first_ref, slot_ref, *refs):
    tok_ref, d_middle_ref, scale_ref, out_ref, sums_ref = refs[count:]
    slot = slot_ref[pl.program_id(0)]
    normed, recip = normalize(tok_ref[...].astype(f32))
    d_mixed = summed(refs[:count])
    back = norm_back(d_mixed * (1.0 + row_of(scale_ref, slot)), normed, recip)
    out_ref[...] = (d_middle_ref[...] + back).astype(half)
    sums_ref[0, 0:1, :] = total_of(d_mixed)
    sums_ref[0, 1:2, :] = total_of(d_mixed * normed)


def result_kernel(count, first_ref, slot_ref, *refs):
    tok_ref, grad_ref, attended_ref, gate_a_ref, gate_b_ref, out_ref, sums_ref = refs[count:]
    slot = slot_ref[pl.program_id(0)]
    middle = tok_ref[...].astype(f32) + row_of(gate_a_ref, slot) * attended_ref[...]
    mlp_out = summed(refs[:count])
    out_ref[...] = (middle + row_of(gate_b_ref, slot) * mlp_out).astype(half)
    sums_ref[0, 0:1, :] = total_of(grad_ref[...].astype(f32) * mlp_out)


def on_own(kernel, name, first, slots, parts, whole, own, modes, columns, outs, terms):
    rows, width = own[0].shape if own else (slots.shape[0] * SPAN, whole[0].shape[1])
    spans = rows // SPAN
    block = (SPAN, width)
    here = spec(block, lambda i, m, s: (i, 0))
    return pl.pallas_call(
        lambda *refs: kernel(len(parts), *refs),
        grid_spec=pltpu.PrefetchScalarGridSpec(
            num_scalar_prefetch=2,
            grid=(spans,),
            in_specs=[here] * len(parts)
            + [spec(block, lambda i, m, s: (m[0] + i, 0))] * len(whole)
            + [here] * len(own)
            + mode_specs(modes, columns),
            out_specs=[here] * len(outs) + ([spec((1, terms, width), lambda i, m, s: (i, 0, 0))] if terms else []),
        ),
        out_shape=[shaped((rows, width), kind) for kind in outs]
        + ([shaped((spans, terms, width), f32)] if terms else []),
        compiler_params=params(24),
        cost_estimate=cost(0 if name in ("result", "back_a") else 5),
        name=name,
    )(first[None], slots, *parts, *[in_hbm(array) for array in whole], *own, *([modes] * len(columns)))


def make_body(n_wide, n_narrow):
    def body(
        tokens,
        cotangent,
        noise_emb,
        offsets,
        lengths,
        group_ids,
        group_table,
        w_qkv,
        w_out,
        w_up,
        b_up,
        w_down,
        w_mod,
        b_mod,
    ):
        tok_dev, width = tokens.shape
        slots = offsets.shape[1]
        local = w_qkv.shape[2]
        groups = group_table.shape[0]
        rows = tok_dev // n_narrow
        spans = rows // SPAN
        last = n_narrow - 1
        me = lax.axis_index("narrow")
        place = lax.axis_index("wide")
        order = me ^ jnp.arange(n_narrow, dtype=jnp.int32)
        first_own = me * spans

        starts = (order[:, None] * spans + jnp.arange(spans, dtype=jnp.int32)[None, :]).reshape(-1, 1) * SPAN
        inside = (starts >= offsets) & (starts < offsets + lengths)
        slot_hot = inside.astype(f32)
        slot_of = jnp.sum(inside * jnp.arange(slots, dtype=jnp.int32)[None, :], axis=1).astype(jnp.int32)
        slot_own = slot_of[:spans]
        lanes = jnp.arange(HEAD_DIM, dtype=jnp.int32)
        same = jnp.repeat(slot_of, SPAN)[:, None] == lanes[None, :]
        kcode = same.astype(half)
        qcode = jnp.where(same, 0.0, MASKED).astype(half)

        group_hot = (group_ids[0][:, None] == jnp.arange(groups, dtype=jnp.int32)[None, :]).astype(f32)
        cond = noise_emb + jnp.dot(group_hot, group_table, precision=highest)
        silu_low = jax.nn.silu(cond).astype(half)
        w_mod_t = w_mod.transpose(1, 0, 2)

        silu_all = lax.all_gather(jnp.concatenate([silu_low, silu_low], axis=0), "wide", axis=0)

        own_a = modes_call(silu_low, w_mod_t, b_mod, 0, 2)
        got_a = exchange([own_a] * n_narrow, n_narrow)
        own_b = modes_call(after(silu_low, own_a), w_mod_t, b_mod, 2, 4)
        got_b = exchange([after(own_b, *got_a)] * n_narrow, n_narrow)
        modes_a = in_order(got_a, me, 2)
        mixed_a = by_chunk(mix_kernel, "mix_a", after(order, own_b), slot_of, tokens, modes_a, (0, 1))
        qkv = project_call(mixed_a, w_qkv, HEAD_DIM ** (-0.5))

        far = attend_call(qkv, after(qcode, *got_b), kcode, w_out, rows, last, 1)
        via = collect_far(far[2], n_narrow)
        near = attend_call(qkv, after(qcode, far[0], silu_all), kcode, w_out, rows, 0, last)
        modes = jnp.concatenate([modes_a, in_order(got_b, me, 2)], axis=0)
        heads_out = jnp.concatenate([near[0], far[0]], axis=0)
        lse = jnp.concatenate([near[1], far[1]], axis=0)
        sent = [near[2][d * rows : (d + 1) * rows] for d in range(last)] + [far[2]]
        attended_parts = collect(sent, n_narrow, via)

        d_mlp = by_chunk(gate_kernel, "d_mlp", after(order, near[0]), slot_of, cotangent, modes, (5,))
        d_hidden = product(d_mlp, w_down, ((1,), (1,)), "d_hidden")
        mixed_own, attended = on_own(
            middle_kernel, "middle", first_own, after(slot_own, d_hidden), attended_parts, [tokens], [],
            modes, (2, 3, 4), [half, f32], 0,
        )
        mixed_near = spread_near(mixed_own, n_narrow)

        pair, d_mixed, b_sums, due = None, [], [], []
        for d in range(n_narrow):
            pieces = mixed_pieces[d] if d else [mixed_own]
            outs = mlp_call(pieces, w_up, after(b_up, *due), d_hidden, d, pair)
            pair = list(outs[:2])
            d_mixed.append(outs[2])
            b_sums.append(outs[3])
            due = [outs[2]]
            if d == 0:
                mixed_pieces = spread(mixed_near, n_narrow, *due)
        hidden, d_pre = pair
        d_mixed_parts = exchange(d_mixed, n_narrow)
        grad_b_up = after(sum(b_sums)[0], hidden)
        mixed_b = jnp.concatenate(flat(mixed_pieces), axis=0)

        grad_w_up = product(mixed_b, d_pre, ((0,), (0,)), "grad_w_up", out=pltpu.HBM)
        sum_w_up = lax.psum_scatter(grad_w_up, "wide", scatter_dimension=0, tiled=True)
        grad_w_down = product(d_mlp, after(hidden, grad_w_up), ((0,), (0,)), "grad_w_down", out=pltpu.HBM)

        d_attn_own, d_middle, sums_b = on_own(
            back_b_kernel, "back_b", first_own, after(slot_own, grad_w_down), d_mixed_parts, [tokens, cotangent],
            [attended], modes, (2, 4), [half, f32], 3,
        )

        def to_modes(sums):
            sent = [lax.dynamic_slice_in_dim(sums, (me ^ d) * local, local, 2) for d in range(n_narrow)]
            got = exchange(sent, n_narrow)
            modes_back = jnp.einsum("bs,bgv->gsv", slot_hot, jnp.concatenate(got, axis=0), precision=highest)
            return sent, modes_back.astype(half)

        sums_sent, d_modes_early = to_modes(sums_b)
        d_attn_near = spread_near(after(d_attn_own, *sums_sent), n_narrow)

        mlp_sent = product(after(hidden, *sums_sent), w_down, ((1,), (0,)), "mlp_out")
        d_attn_pieces = spread(d_attn_near, n_narrow, mlp_sent)
        mlp_sent = after(mlp_sent, *d_attn_near[1:])
        mlp_parts = exchange([mlp_sent[d * rows : (d + 1) * rows] for d in range(n_narrow)], n_narrow)
        back = attend_back_call(qkv, after(qcode, d_modes_early), kcode, lse, w_out, d_attn_pieces[:last], 0, None)
        back_far = attend_back_call(
            qkv, after(qcode, back[0]), kcode, lse, w_out, d_attn_pieces[last:], last, back[1:]
        )
        d_key, d_value = back_far[1:]
        far_a = project_back_call(back_far[0], d_key, d_value, w_qkv, rows, last, 1, last)
        via_a = collect_far(far_a, n_narrow)
        near_a = project_back_call(back[0], after(d_key, far_a), d_value, w_qkv, rows, 0, last, 0)
        sent_a = [near_a[d * rows : (d + 1) * rows] for d in range(last)] + [far_a]
        d_mixed_a_parts = collect(sent_a, n_narrow, via_a)
        sum_w_down = lax.psum_scatter(after(grad_w_down, back_far[0]), "wide", scatter_dimension=0, tiled=True)

        d_query = jnp.concatenate([back[0], back_far[0]], axis=0)
        d_proj = jnp.concatenate([after(d_query, near_a), d_key, d_value], axis=1)
        wide_cols = d_proj.shape[1] + local
        grads = product(
            after(mixed_a, *mlp_parts), d_proj, ((0,), (0,)), "grad_w_qkv", block=local, out=pltpu.HBM, micros=0,
            columns=wide_cols,
        )
        d_attn = jnp.concatenate([joined(pieces) for pieces in d_attn_pieces], axis=0)
        grads = product(
            after(d_attn, grads, *via_a), heads_out, ((0,), (0,)), "grad_w_out", block=local, out=pltpu.HBM, micros=0,
            columns=wide_cols, first=d_proj.shape[1], before=grads,
        )
        sum_rest = lax.psum_scatter(grads, "wide", scatter_dimension=0, tiled=True)
        result_own, sums_out = on_own(
            result_kernel, "result", first_own, after(slot_own, grads), mlp_parts, [tokens, cotangent],
            [attended], modes, (2, 5), [half], 1,
        )
        result_near = spread_near(result_own, n_narrow)
        silu_part = silu_back_call(after(d_modes_early, d_mlp), w_mod_t, lambda g: g + 2)

        grad_tok_own, sums_a = on_own(
            back_a_kernel, "back_a", first_own, after(slot_own, silu_part, sum_w_up, sum_w_down), d_mixed_a_parts, [tokens],
            [d_middle], modes, (1,), [half], 2,
        )
        sums_sent, d_modes_late = to_modes(jnp.concatenate([sums_a, sums_out], axis=1))
        silu_part = silu_part + silu_back_call(d_modes_late, w_mod_t, lambda g: jnp.where(g < 2, g, 5))
        d_silu_part = silu_part.astype(half)
        d_silu = sum(part.astype(f32) for part in exchange([d_silu_part] * n_narrow, n_narrow))
        sigma = jax.nn.sigmoid(cond)
        grad_noise = d_silu * sigma * (1.0 + cond * (1.0 - sigma))
        table_part = jnp.dot(group_hot.T, grad_noise, precision=highest).astype(half)

        grad_tok_near = spread_near(after(grad_tok_own, d_silu_part), n_narrow)
        result = settle(spread(result_near, n_narrow, *sums_sent), after(order, sum_w_down))
        ff = w_up.shape[1]
        small = jnp.pad(grad_b_up.astype(half), (0, -ff % width)).reshape(-1, width)
        d_modes = jnp.concatenate([d_modes_late[:2], d_modes_early, d_modes_late[2:]], axis=0)
        late = lax.all_gather(
            jnp.concatenate([d_modes.reshape(-1, width), small, table_part], axis=0), "wide", axis=0
        )
        grad_tokens = settle(spread(grad_tok_near, n_narrow), after(order, result))

        col = width // n_wide
        ff_part = ff // n_wide
        part_b = local // n_wide
        silu_cols = lax.dynamic_slice_in_dim(silu_all[:, :slots], place * col, col, 2).reshape(-1, col)
        mode_rows = 6 * slots * local // width
        small_rows = mode_rows + small.shape[0]
        b_up_all = late[:, mode_rows:small_rows].reshape(n_wide, -1)[:, :ff]
        sum_b_up = jnp.sum(
            lax.dynamic_slice_in_dim(b_up_all, place * ff_part, ff_part, 1).astype(f32), axis=0
        )
        d_modes_all = late[:, :mode_rows].reshape(n_wide, 6, slots, local)
        d_modes_all = d_modes_all.transpose(1, 0, 2, 3).reshape(6, n_wide * slots, local)
        grad_w_mod = jnp.einsum("sd,gsv->gdv", silu_cols, d_modes_all, preferred_element_type=f32).transpose(1, 0, 2)
        sum_b_mod = jnp.sum(
            lax.dynamic_slice_in_dim(d_modes_all, place * part_b, part_b, 2).astype(f32), axis=1
        )
        sum_table = jnp.sum(
            lax.dynamic_slice_in_dim(late[:, small_rows:], place * col, col, 2).astype(f32), axis=0
        )

        out_qkv = sum_rest[:, : 3 * local].astype(f32).reshape(col, 3, local).transpose(1, 0, 2)
        return (
            result,
            grad_tokens,
            grad_noise,
            sum_table,
            out_qkv,
            sum_rest[:, 3 * local :].astype(f32).T,
            sum_w_up.astype(f32),
            sum_b_up,
            sum_w_down.astype(f32).T,
            grad_w_mod,
            sum_b_mod,
        )

    return body


def solution(mesh):
    in_specs = (
        P("wide", None),
        P("wide", None),
        P("wide", None),
        P("wide", None),
        P("wide", None),
        P("wide", None),
        P(),
        P(None, None, "narrow"),
        P("narrow", None),
        P(None, "narrow"),
        P("narrow"),
        P("narrow", None),
        P(None, None, "narrow"),
        P(None, "narrow"),
    )
    out_specs = (
        P("wide", None),
        P("wide", None),
        P("wide", None),
        P(None, "wide"),
        P(None, "wide", "narrow"),
        P("narrow", "wide"),
        P("wide", "narrow"),
        P(("narrow", "wide")),
        P("narrow", "wide"),
        P("wide", None, "narrow"),
        P(None, ("narrow", "wide")),
    )
    body = make_body(mesh.shape["wide"], mesh.shape["narrow"])
    return jax.shard_map(body, mesh=mesh, in_specs=in_specs, out_specs=out_specs, check_vma=False)
```

```python
import jax
import jax.numpy as jnp
from jax import lax
from jax.experimental import pallas as pl
from jax.experimental.pallas import tpu as pltpu
from jax.sharding import PartitionSpec as P

HEAD_DIM = 128
SPAN = 64
MASKED = -1e30

f32 = jnp.float32
half = jnp.bfloat16
highest = lax.Precision.HIGHEST
MIB = 1 << 20


def dot(left, right, dims):
    return lax.dot_general(left, right, (dims, ((), ())), preferred_element_type=f32)


def normalize(values):
    centred = values - jnp.mean(values, axis=-1, keepdims=True)
    recip = lax.rsqrt(jnp.mean(centred * centred, axis=-1, keepdims=True) + 1e-06)
    return (centred * recip, recip)


def norm_back(grad, normed, recip):
    first = jnp.mean(grad, axis=-1, keepdims=True)
    second = jnp.mean(grad * normed, axis=-1, keepdims=True)
    return recip * (grad - first - normed * second)


def spec(shape, index):
    return pl.BlockSpec(shape, index)


def fixed(shape):
    zeros = (0,) * len(shape)
    return pl.BlockSpec(shape, lambda *_: zeros)


def held(shape):
    zeros = (0,) * len(shape)
    return pl.BlockSpec(shape, lambda *_: zeros, pipeline_mode=pl.Buffered(1))


def in_hbm(array):
    return pltpu.with_memory_space_constraint(array, pltpu.HBM)


def params(mib):
    return pltpu.CompilerParams(vmem_limit_bytes=mib * MIB)


def cost(micros):
    return pl.CostEstimate(flops=int(micros * 1.15e+09), transcendentals=0, bytes_accessed=0)


def shaped(shape, kind):
    return jax.ShapeDtypeStruct(shape, kind)


def after(values, *others):
    return lax.optimization_barrier((values, *others))[0]


def hop(values, distance, size):
    return lax.ppermute(values, "narrow", [(i, i ^ distance) for i in range(size)])


def exchange(chunks, size):
    return [chunks[0]] + [hop(chunks[d], d, size) for d in range(1, len(chunks))]


def spread_near(shard, size):
    return [shard] + [hop(shard, d, size) for d in range(1, size if size != 4 else 3)]


def spread(near, size, *gates):
    if size != 4:
        return [[piece] for piece in near]
    one, two = near[1:]
    mid = one.shape[0] // 2
    two, one = after(two[:mid], *gates), after(one[mid:], *gates)
    return [[piece] for piece in near] + [[hop(two, 1, size), hop(one, 2, size)]]


def joined(pieces):
    return jnp.concatenate(pieces, axis=0) if len(pieces) > 1 else pieces[0]


def flat(lists):
    return [piece for pieces in lists for piece in pieces]


def collect_far(far, size):
    if size != 4:
        return []
    mid = far.shape[0] // 2
    return [hop(far[:mid], 2, size), hop(far[mid:], 1, size)]


def collect_near(chunks, size, via):
    if size != 4:
        return chunks[1:]
    _, one, two, _ = chunks
    mid = one.shape[0] // 2
    via_two, via_one = via
    one = joined([(one[:mid].astype(f32) + via_two.astype(f32)).astype(half), one[mid:]])
    two = joined([two[:mid], (two[mid:].astype(f32) + via_one.astype(f32)).astype(half)])
    return [one, two]


def collect(chunks, size, via):
    return exchange(chunks[:1] + collect_near(chunks, size, via), size)


def in_order(pieces, index, axis):
    return jnp.concatenate([lax.select_n(index ^ k, *pieces) for k in range(len(pieces))], axis=axis)


def settle_kernel(layout, order_ref, *refs):
    out_ref = refs[-1]
    for d, count in enumerate(layout):

        @pl.when(pl.program_id(0) == d)
        def _(pieces=refs[sum(layout[:d]) :][:count]):
            at = 0
            for piece in pieces:
                out_ref[at : at + piece.shape[0], :] = piece[...]
                at += piece.shape[0]


def settle(chunks, order):
    rows = sum(piece.shape[0] for piece in chunks[0])
    width = chunks[0][0].shape[1]
    return pl.pallas_call(
        lambda *refs: settle_kernel([len(pieces) for pieces in chunks], *refs),
        grid_spec=pltpu.PrefetchScalarGridSpec(
            num_scalar_prefetch=1,
            grid=(len(chunks),),
            in_specs=[held(piece.shape) for piece in flat(chunks)],
            out_specs=spec((rows, width), lambda i, o: (o[i], 0)),
        ),
        out_shape=pltpu.HBM((rows * len(chunks), width), chunks[0][0].dtype),
        compiler_params=params(16),
        cost_estimate=cost(20),
        name="settle",
    )(order, *flat(chunks))


def modes_kernel(silu_ref, w_ref, b_ref, out_ref):
    out_ref[0] = (
        jnp.dot(silu_ref[...], w_ref[0], preferred_element_type=f32) + b_ref[0]
    )


def modes_call(silu_low, w_mod, b_mod, first, count):
    slots, width = silu_low.shape
    local = w_mod.shape[2]
    return pl.pallas_call(
        modes_kernel,
        grid=(count,),
        in_specs=[
            spec((slots, width), lambda g: (0, 0)),
            spec((1, width, local), lambda g: (first + g, 0, 0)),
            spec((1, 1, local), lambda g: (first + g, 0, 0)),
        ],
        out_specs=spec((1, slots, local), lambda g: (g, 0, 0)),
        out_shape=shaped((count, slots, local), f32),
        cost_estimate=cost(5),
        compiler_params=params(24),
        name="modes",
    )(silu_low, in_hbm(w_mod), b_mod[:, None, :])


def silu_back_kernel(d_ref, w_ref, out_ref):
    part = dot(d_ref[0], w_ref[0], ((1,), (1,)))

    @pl.when(pl.program_id(0) == 0)
    def _():
        out_ref[...] = part

    @pl.when(pl.program_id(0) > 0)
    def _():
        out_ref[...] = out_ref[...] + part


def silu_back_call(d_modes, w_mod):
    groups, slots, local = d_modes.shape
    width = w_mod.shape[1]
    return pl.pallas_call(
        silu_back_kernel,
        grid=(groups,),
        in_specs=[
            spec((1, slots, local), lambda g: (g, 0, 0)),
            spec((1, width, local), lambda g: (g, 0, 0)),
        ],
        out_specs=fixed((slots, width)),
        out_shape=shaped((slots, width), f32),
        compiler_params=params(16),
        cost_estimate=cost(0),
        name="silu_back",
    )(d_modes, in_hbm(w_mod))


def row_of(ref, slot):
    return ref[0, pl.ds(slot, 1), :]


def mix_kernel(order_ref, slot_ref, tok_ref, shift_ref, scale_ref, out_ref):
    step = pl.program_id(0)
    spans = tok_ref.shape[0] // SPAN
    for i in range(spans):
        rows = slice(i * SPAN, (i + 1) * SPAN)
        slot = slot_ref[step * spans + i]
        normed, _ = normalize(tok_ref[rows, :].astype(f32))
        out_ref[rows, :] = (normed * (1.0 + row_of(scale_ref, slot)) + row_of(shift_ref, slot)).astype(half)


def gate_kernel(order_ref, slot_ref, grad_ref, gate_ref, out_ref):
    step = pl.program_id(0)
    spans = grad_ref.shape[0] // SPAN
    for i in range(spans):
        rows = slice(i * SPAN, (i + 1) * SPAN)
        gate = row_of(gate_ref, slot_ref[step * spans + i])
        out_ref[rows, :] = (grad_ref[rows, :].astype(f32) * gate).astype(half)


def mode_specs(modes, columns):
    _, count, width = modes.shape
    return [spec((1, count, width), lambda i, *_, column=column: (column, 0, 0)) for column in columns]


def by_chunk(kernel, name, order, slots, values, modes, columns):
    rows, width = values.shape
    chunk = rows // order.shape[0]
    return pl.pallas_call(
        kernel,
        grid_spec=pltpu.PrefetchScalarGridSpec(
            num_scalar_prefetch=2,
            grid=(order.shape[0],),
            in_specs=[spec((chunk, width), lambda i, o, s: (o[i], 0))] + mode_specs(modes, columns),
            out_specs=spec((chunk, width), lambda i, o, s: (i, 0)),
        ),
        out_shape=shaped((rows, width), half),
        compiler_params=params(24),
        cost_estimate=cost(5),
        name=name,
    )(order, slots, values, *([modes] * len(columns)))


def product_kernel(dims, scales, left_ref, right_ref, out_ref):
    total = dot(left_ref[...], right_ref[...].reshape(right_ref.shape[-2:]), dims)
    if scales is not None:
        total = total * jnp.where(pl.program_id(0) == 0, scales, 1.0)
    out_ref[...] = total.astype(half).reshape(out_ref.shape)


def product(left, right, dims, name, block=512, out=shaped, micros=4, columns=None, first=0, before=None):
    free = 1 - dims[1][0]
    count = right.shape[free]
    rows = left.shape[1 - dims[0][0]]
    block = min(block, count)
    shape = (block, right.shape[1]) if free == 0 else (right.shape[0], block)
    index = (lambda j: (j, 0)) if free == 0 else (lambda j: (0, j))
    given = [] if before is None else [before]
    return pl.pallas_call(
        lambda left_ref, right_ref, *refs: product_kernel(dims, None, left_ref, right_ref, refs[-1]),
        grid=(count // block,),
        in_specs=[held(left.shape), spec(shape, index)] + [pl.BlockSpec(memory_space=pl.ANY)] * len(given),
        out_specs=spec((rows, block), lambda j: (0, first // block + j)),
        out_shape=out((rows, columns or count), half),
        input_output_aliases={2: 0} if given else {},
        compiler_params=params(28),
        cost_estimate=cost(micros),
        name=name,
    )(left, right, *given)


def project_call(mixed, w_qkv, factor):
    count, width, local = w_qkv.shape
    rows = mixed.shape[0]
    return pl.pallas_call(
        lambda *refs: product_kernel(((1,), (0,)), factor, *refs),
        grid=(count,),
        in_specs=[held(mixed.shape), spec((1, width, local), lambda i: (i, 0, 0))],
        out_specs=spec((1, rows, local), lambda i: (i, 0, 0)),
        out_shape=shaped((count, rows, local), half),
        compiler_params=params(28),
        cost_estimate=cost(9),
        name="project",
    )(mixed, w_qkv)


def attend_kernel(q_ref, k_ref, v_ref, qcode_ref, kcode_ref, w_ref, heads_ref, lse_ref, out_ref):
    heads = q_ref.shape[2] // HEAD_DIM
    for h in range(heads):
        cols = slice(h * HEAD_DIM, (h + 1) * HEAD_DIM)
        keys = jnp.concatenate([k_ref[0, :, cols], kcode_ref[...]], axis=1)
        query = jnp.concatenate([q_ref[0, :, cols], qcode_ref[...]], axis=1)
        scores = dot(keys, query, ((1,), (1,)))
        top = jnp.max(scores, axis=0, keepdims=True)
        expo = jnp.exp(scores - top)
        total = jnp.sum(expo, axis=0, keepdims=True)
        out = dot(v_ref[0, :, cols], expo.astype(half), ((0,), (0,)))
        heads_ref[:, cols] = (out / total).T.astype(half)
        lse_ref[0, h : h + 1, :] = top + jnp.log(total)
    out_ref[...] = jnp.dot(heads_ref[...], w_ref[...], preferred_element_type=f32).astype(half)


def attend_call(qkv, qcode, kcode, w_out, chunk, first, count):
    _, rows, local = qkv.shape
    width = w_out.shape[1]
    heads = local // HEAD_DIM
    return pl.pallas_call(
        attend_kernel,
        grid=(count,),
        in_specs=[
            spec((1, chunk, local), lambda i: (0, first + i, 0)),
            spec((1, rows, local), lambda i: (1, 0, 0)),
            spec((1, rows, local), lambda i: (2, 0, 0)),
            spec((chunk, HEAD_DIM), lambda i: (first + i, 0)),
            fixed((rows, HEAD_DIM)),
            held(w_out.shape),
        ],
        out_specs=[
            spec((chunk, local), lambda i: (i, 0)),
            spec((1, heads, chunk), lambda i: (i, 0, 0)),
            spec((chunk, width), lambda i: (i, 0)),
        ],
        out_shape=[
            shaped((count * chunk, local), half),
            shaped((count, heads, chunk), f32),
            shaped((count * chunk, width), half),
        ],
        compiler_params=params(32),
        cost_estimate=cost(2 + 3.3 * count),
        name="attend",
    )(qkv, qkv, qkv, qcode, kcode, w_out)


def attend_back_kernel(final, layout, q_ref, k_ref, v_ref, qcode_ref, kcode_ref, lse_ref, w_ref, *refs):
    chunk, local = q_ref.shape[1:]
    pieces, refs, d_heads_ref = refs[: sum(layout)], refs[sum(layout) : -1], refs[-1]
    heads = local // HEAD_DIM
    step = pl.program_id(0)
    factor = HEAD_DIM ** (-0.5)
    if final:
        dk_old, dv_old, dq_ref, dk_ref, dv_ref, dk_acc, dv_acc = refs
    else:
        dq_ref, dk_acc, dv_acc = refs

    @pl.when(step == 0)
    def _():
        dk_acc[...] = dk_old[...] if final else jnp.zeros_like(dk_acc)
        dv_acc[...] = dv_old[...] if final else jnp.zeros_like(dv_acc)

    for d, count in enumerate(layout):

        @pl.when(step == d)
        def _(refs=pieces[sum(layout[:d]) :][:count]):
            at = 0
            for ref in refs:
                d_heads_ref[at : at + ref.shape[0], :] = dot(ref[...], w_ref[...], ((1,), (1,))).astype(half)
                at += ref.shape[0]

    for h in range(heads):
        cols = slice(h * HEAD_DIM, (h + 1) * HEAD_DIM)
        keys = jnp.concatenate([k_ref[0, :, cols], kcode_ref[...]], axis=1)
        query = jnp.concatenate([q_ref[0, :, cols], qcode_ref[...]], axis=1)
        grad = d_heads_ref[:, cols]
        scores = dot(keys, query, ((1,), (1,)))
        probs = jnp.exp(scores - lse_ref[0, h : h + 1, :])
        d_probs = dot(v_ref[0, :, cols], grad, ((1,), (1,)))
        inner = jnp.sum(probs * d_probs, axis=0, keepdims=True)
        d_scores = (probs * (d_probs - inner)).astype(half)
        dv_acc[:, cols] += dot(probs.astype(half), grad, ((1,), (0,)))
        dk_acc[:, cols] += dot(d_scores, q_ref[0, :, cols], ((1,), (0,)))
        dq = dot(k_ref[0, :, cols], d_scores, ((0,), (0,)))
        dq_ref[:, cols] = (dq.T * factor).astype(half)

    if final:

        @pl.when(step == pl.num_programs(0) - 1)
        def _():
            dk_ref[...] = dk_acc[...].astype(half)
            dv_ref[...] = dv_acc[...].astype(half)


def attend_back_call(qkv, qcode, kcode, lse, w_out, d_attn, first, sums):
    _, rows, local = qkv.shape
    _, heads, chunk = lse.shape
    count = len(d_attn)
    final = sums is not None
    whole = (rows, local)
    return pl.pallas_call(
        lambda *refs: attend_back_kernel(final, [len(pieces) for pieces in d_attn], *refs),
        grid=(count,),
        in_specs=[
            spec((1, chunk, local), lambda i: (0, first + i, 0)),
            spec((1, rows, local), lambda i: (1, 0, 0)),
            spec((1, rows, local), lambda i: (2, 0, 0)),
            spec((chunk, HEAD_DIM), lambda i: (first + i, 0)),
            fixed((rows, HEAD_DIM)),
            spec((1, heads, chunk), lambda i: (first + i, 0, 0)),
            held(w_out.shape),
        ]
        + [held(piece.shape) for piece in flat(d_attn)]
        + ([held(whole)] * 2 if final else []),
        out_specs=[spec((chunk, local), lambda i: (i, 0))] + [fixed(whole)] * 2,
        out_shape=[shaped((count * chunk, local), half)] + [shaped(whole, half if final else f32)] * 2,
        scratch_shapes=([pltpu.VMEM(whole, f32)] * 2 if final else []) + [pltpu.VMEM((chunk, local), half)],
        compiler_params=params(36),
        cost_estimate=cost(0 if final else 130),
        name="attend_back",
    )(qkv, qkv, qkv, qcode, kcode, lse, w_out, *flat(d_attn), *(sums if final else []))


def project_back_kernel(q_ref, k_ref, v_ref, w_ref, out_ref):
    total = None
    for i, ref in enumerate((q_ref, k_ref, v_ref)):
        part = dot(ref[...], w_ref[i], ((1,), (1,)))
        total = part if total is None else total + part
    out_ref[...] = total.astype(half)


def project_back_call(d_query, d_key, d_value, w_qkv, chunk, first, count, first_query):
    _, width, local = w_qkv.shape
    there = lambda i: (first + i, 0)
    return pl.pallas_call(
        project_back_kernel,
        grid=(count,),
        in_specs=[
            spec((chunk, local), lambda i: (first - first_query + i, 0)),
            spec((chunk, local), there),
            spec((chunk, local), there),
            held(w_qkv.shape),
        ],
        out_specs=spec((chunk, width), lambda i: (i, 0)),
        out_shape=shaped((count * chunk, width), half),
        compiler_params=params(32),
        cost_estimate=cost(0),
        name="project_back",
    )(d_query, d_key, d_value, w_qkv)


def total_of(terms):
    return jnp.sum(terms, axis=0, keepdims=True)


def mlp_kernel(count, *refs):
    x_refs = refs[:count]
    up_ref, b_ref, d_ref = refs[count : count + 3]
    hidden_ref, d_pre_ref, dx_ref, b_sum_ref, acc_ref = refs[-5:]
    step = pl.program_id(0)
    mixed = jnp.concatenate([ref[...] for ref in x_refs], axis=0) if count > 1 else x_refs[0][...]
    pre = jnp.dot(mixed, up_ref[...], preferred_element_type=f32) + b_ref[...]
    cumul = 0.5 * (1.0 + lax.erf(pre * 0.7071067811865476))
    density = jnp.exp(-0.5 * pre * pre) * 0.3989422804014327
    hidden_ref[...] = (pre * cumul).astype(half)
    d_pre = (d_ref[...].astype(f32) * (cumul + pre * density)).astype(half)
    d_pre_ref[...] = d_pre
    b_sum_ref[...] = total_of(d_pre.astype(f32))
    part = dot(d_pre, up_ref[...], ((1,), (1,)))

    @pl.when(step == 0)
    def _():
        acc_ref[...] = part

    @pl.when(step > 0)
    def _():
        acc_ref[...] += part

    @pl.when(step == pl.num_programs(0) - 1)
    def _():
        dx_ref[...] = acc_ref[...].astype(half)


def mlp_call(pieces, w_up, b_up, d_hidden, chunk, before):
    rows = sum(piece.shape[0] for piece in pieces)
    width, ff = w_up.shape
    block = min(1024, ff)
    here = lambda j: (chunk, j)
    operands = [*pieces, w_up, b_up[None, :], d_hidden]
    in_specs = [held(piece.shape) for piece in pieces] + [
        spec((width, block), lambda j: (0, j)),
        spec((1, block), lambda j: (0, j)),
        spec((rows, block), here),
    ]
    aliases = {}
    if before is not None:
        aliases = {len(operands): 0, len(operands) + 1: 1}
        operands += before
        in_specs += [pl.BlockSpec(memory_space=pl.ANY)] * 2
    return pl.pallas_call(
        lambda *refs: mlp_kernel(len(pieces), *refs),
        grid=(ff // block,),
        in_specs=in_specs,
        out_specs=[
            spec((rows, block), here),
            spec((rows, block), here),
            fixed((rows, width)),
            spec((1, block), lambda j: (0, j)),
        ],
        out_shape=[
            shaped((d_hidden.shape[0], ff), half),
            shaped((d_hidden.shape[0], ff), half),
            pltpu.VMEM((rows, width), half),
            shaped((1, ff), f32),
        ],
        scratch_shapes=[pltpu.VMEM((rows, width), f32)],
        input_output_aliases=aliases,
        compiler_params=params(24),
        cost_estimate=cost(3),
        name="mlp",
    )(*operands)


def summed(refs):
    total = refs[0][...].astype(f32)
    for ref in refs[1:]:
        total = total + ref[...].astype(f32)
    return total


def middle_kernel(count, first_ref, slot_ref, *refs):
    tok_ref, gate_ref, shift_ref, scale_ref, mixed_ref, attended_ref = refs[count:]
    slot = slot_ref[pl.program_id(0)]
    attended = summed(refs[:count])
    attended_ref[...] = attended
    normed, _ = normalize(tok_ref[...].astype(f32) + row_of(gate_ref, slot) * attended)
    mixed_ref[...] = (normed * (1.0 + row_of(scale_ref, slot)) + row_of(shift_ref, slot)).astype(half)


def back_b_kernel(count, first_ref, slot_ref, *refs):
    tok_ref, grad_ref, attended_ref, gate_ref, scale_ref, d_attn_ref, d_middle_ref, sums_ref = refs[count:]
    slot = slot_ref[pl.program_id(0)]
    gate = row_of(gate_ref, slot)
    attended = attended_ref[...]
    normed, recip = normalize(tok_ref[...].astype(f32) + gate * attended)
    d_mixed = summed(refs[:count])
    back = norm_back(d_mixed * (1.0 + row_of(scale_ref, slot)), normed, recip)
    d_middle = grad_ref[...].astype(f32) + back
    d_middle_ref[...] = d_middle
    d_attn_ref[...] = (d_middle * gate).astype(half)
    sums_ref[0, 0:1, :] = total_of(d_middle * attended)
    sums_ref[0, 1:2, :] = total_of(d_mixed)
    sums_ref[0, 2:3, :] = total_of(d_mixed * normed)


def back_a_kernel(count, first_ref, slot_ref, *refs):
    tok_ref, d_middle_ref, scale_ref, out_ref, sums_ref = refs[count:]
    slot = slot_ref[pl.program_id(0)]
    normed, recip = normalize(tok_ref[...].astype(f32))
    d_mixed = summed(refs[:count])
    back = norm_back(d_mixed * (1.0 + row_of(scale_ref, slot)), normed, recip)
    out_ref[...] = (d_middle_ref[...] + back).astype(half)
    sums_ref[0, 0:1, :] = total_of(d_mixed)
    sums_ref[0, 1:2, :] = total_of(d_mixed * normed)


def result_kernel(count, first_ref, slot_ref, *refs):
    tok_ref, grad_ref, attended_ref, gate_a_ref, gate_b_ref, out_ref, sums_ref = refs[count:]
    slot = slot_ref[pl.program_id(0)]
    middle = tok_ref[...].astype(f32) + row_of(gate_a_ref, slot) * attended_ref[...]
    mlp_out = summed(refs[:count])
    out_ref[...] = (middle + row_of(gate_b_ref, slot) * mlp_out).astype(half)
    sums_ref[0, 0:1, :] = total_of(grad_ref[...].astype(f32) * mlp_out)


def on_own(kernel, name, first, slots, parts, whole, own, modes, columns, outs, terms):
    rows, width = own[0].shape if own else (slots.shape[0] * SPAN, whole[0].shape[1])
    spans = rows // SPAN
    block = (SPAN, width)
    here = spec(block, lambda i, m, s: (i, 0))
    return pl.pallas_call(
        lambda *refs: kernel(len(parts), *refs),
        grid_spec=pltpu.PrefetchScalarGridSpec(
            num_scalar_prefetch=2,
            grid=(spans,),
            in_specs=[here] * len(parts)
            + [spec(block, lambda i, m, s: (m[0] + i, 0))] * len(whole)
            + [here] * len(own)
            + mode_specs(modes, columns),
            out_specs=[here] * len(outs) + ([spec((1, terms, width), lambda i, m, s: (i, 0, 0))] if terms else []),
        ),
        out_shape=[shaped((rows, width), kind) for kind in outs]
        + ([shaped((spans, terms, width), f32)] if terms else []),
        compiler_params=params(24),
        cost_estimate=cost(0 if name in ("result", "back_a") else 5),
        name=name,
    )(first[None], slots, *parts, *[in_hbm(array) for array in whole], *own, *([modes] * len(columns)))


def unpack_kernel(sum_ref, qkv_ref, out_ref):
    step = pl.program_id(0)

    @pl.when(step < 3)
    def _():
        qkv_ref[0] = sum_ref[...].astype(f32)

    @pl.when(step == 3)
    def _():
        out_ref[...] = sum_ref[...].astype(f32).T


def unpack_call(sums, local):
    rows = sums.shape[0]
    return pl.pallas_call(
        unpack_kernel,
        grid=(4,),
        in_specs=[spec((rows, local), lambda i: (0, i))],
        out_specs=[
            spec((1, rows, local), lambda i: (jnp.minimum(i, 2), 0, 0)),
            fixed((local, rows)),
        ],
        out_shape=[pltpu.HBM((3, rows, local), f32), pltpu.HBM((local, rows), f32)],
        compiler_params=params(16),
        cost_estimate=cost(2),
        name="unpack",
    )(sums)


def make_body(n_wide, n_narrow):
    def body(
        tokens,
        cotangent,
        noise_emb,
        offsets,
        lengths,
        group_ids,
        group_table,
        w_qkv,
        w_out,
        w_up,
        b_up,
        w_down,
        w_mod,
        b_mod,
    ):
        tok_dev, width = tokens.shape
        slots = offsets.shape[1]
        local = w_qkv.shape[2]
        groups = group_table.shape[0]
        rows = tok_dev // n_narrow
        spans = rows // SPAN
        last = n_narrow - 1
        me = lax.axis_index("narrow")
        place = lax.axis_index("wide")
        order = me ^ jnp.arange(n_narrow, dtype=jnp.int32)
        first_own = me * spans

        starts = (order[:, None] * spans + jnp.arange(spans, dtype=jnp.int32)[None, :]).reshape(-1, 1) * SPAN
        inside = (starts >= offsets) & (starts < offsets + lengths)
        slot_hot = inside.astype(f32)
        slot_of = jnp.sum(inside * jnp.arange(slots, dtype=jnp.int32)[None, :], axis=1).astype(jnp.int32)
        slot_own = slot_of[:spans]
        lanes = jnp.arange(HEAD_DIM, dtype=jnp.int32)
        same = jnp.repeat(slot_of, SPAN)[:, None] == lanes[None, :]
        kcode = same.astype(half)
        qcode = jnp.where(same, 0.0, MASKED).astype(half)

        group_hot = (group_ids[0][:, None] == jnp.arange(groups, dtype=jnp.int32)[None, :]).astype(f32)
        cond = noise_emb + jnp.dot(group_hot, group_table, precision=highest)
        silu_low = jax.nn.silu(cond).astype(half)
        w_mod_t = w_mod.transpose(1, 0, 2)

        silu_all = lax.all_gather(jnp.concatenate([silu_low, silu_low], axis=0), "wide", axis=0)

        own_a = modes_call(silu_low, w_mod_t, b_mod, 0, 2)
        got_a = exchange([own_a] * n_narrow, n_narrow)
        own_b = modes_call(after(silu_low, own_a), w_mod_t, b_mod, 2, 4)
        modes_a = in_order(got_a, me, 2)
        mixed_a = by_chunk(mix_kernel, "mix_a", after(order, own_b), slot_of, tokens, modes_a, (0, 1))
        qkv = project_call(mixed_a, w_qkv, HEAD_DIM ** (-0.5))

        far = attend_call(qkv, qcode, kcode, w_out, rows, last, 1)
        via = collect_far(far[2], n_narrow)
        got_b = exchange([after(own_b, far[0])] * n_narrow, n_narrow)
        near = attend_call(qkv, after(qcode, far[0], silu_all), kcode, w_out, rows, 0, last)
        modes = jnp.concatenate([modes_a, in_order([after(got, near[0]) for got in got_b], me, 2)], axis=0)
        heads_out = jnp.concatenate([near[0], far[0]], axis=0)
        lse = jnp.concatenate([near[1], far[1]], axis=0)
        sent = [near[2][d * rows : (d + 1) * rows] for d in range(last)] + [far[2]]
        attended_parts = collect(sent, n_narrow, via)

        d_mlp = by_chunk(gate_kernel, "d_mlp", after(order, near[0]), slot_of, cotangent, modes, (5,))
        d_hidden = product(d_mlp, w_down, ((1,), (1,)), "d_hidden")
        mixed_own, attended = on_own(
            middle_kernel, "middle", first_own, after(slot_own, d_hidden), attended_parts, [tokens], [],
            modes, (2, 3, 4), [half, f32], 0,
        )
        mixed_near = spread_near(mixed_own, n_narrow)

        pair, d_mixed, b_sums, due = None, [], [], []
        for d in range(n_narrow):
            pieces = mixed_pieces[d] if d else [mixed_own]
            outs = mlp_call(pieces, w_up, after(b_up, *due), d_hidden, d, pair)
            pair = list(outs[:2])
            d_mixed.append(outs[2])
            b_sums.append(outs[3])
            due = [outs[2]]
            if d == 0:
                mixed_pieces = spread(mixed_near, n_narrow, *due)
        hidden, d_pre = pair
        d_mixed_parts = exchange(d_mixed, n_narrow)
        grad_b_up = after(sum(b_sums)[0], hidden)
        mixed_b = jnp.concatenate(flat(mixed_pieces), axis=0)

        grad_w_up = product(mixed_b, d_pre, ((0,), (0,)), "grad_w_up", out=pltpu.HBM)
        sum_w_up = lax.psum_scatter(grad_w_up, "wide", scatter_dimension=0, tiled=True)
        grad_w_down = product(d_mlp, after(hidden, grad_w_up), ((0,), (0,)), "grad_w_down", out=pltpu.HBM)

        d_attn_own, d_middle, sums_b = on_own(
            back_b_kernel, "back_b", first_own, after(slot_own, grad_w_down), d_mixed_parts, [tokens, cotangent],
            [attended], modes, (2, 4), [half, f32], 3,
        )

        def to_modes(sums):
            sent = [lax.dynamic_slice_in_dim(sums, (me ^ d) * local, local, 2) for d in range(n_narrow)]
            got = exchange(sent, n_narrow)
            modes_back = jnp.einsum("bs,bgv->gsv", slot_hot, jnp.concatenate(got, axis=0), precision=highest)
            return sent, modes_back.astype(half)

        d_attn_near = spread_near(d_attn_own, n_narrow)

        mlp_sent = product(after(hidden, d_attn_own), w_down, ((1,), (0,)), "mlp_out", micros=200)
        d_attn_pieces = spread(d_attn_near, n_narrow, mlp_sent)
        mlp_sent = after(mlp_sent, *d_attn_near[1:])
        mlp_parts = exchange([mlp_sent[d * rows : (d + 1) * rows] for d in range(n_narrow)], n_narrow)
        back = attend_back_call(qkv, qcode, kcode, lse, w_out, d_attn_pieces[:last], 0, None)
        back_far = attend_back_call(
            qkv, after(qcode, back[0]), kcode, lse, w_out, d_attn_pieces[last:], last, back[1:]
        )
        d_key, d_value = back_far[1:]
        far_a = project_back_call(back_far[0], d_key, d_value, w_qkv, rows, last, 1, last)
        via_a = collect_far(far_a, n_narrow)
        near_a = project_back_call(back[0], after(d_key, far_a), d_value, w_qkv, rows, 0, last, 0)
        sent_a = [near_a[d * rows : (d + 1) * rows] for d in range(last)] + [far_a]
        near_sent = collect_near(sent_a, n_narrow, via_a)
        d_mixed_a_parts = exchange(sent_a[:1] + near_sent, n_narrow)
        sum_w_down = lax.psum_scatter(after(grad_w_down, *d_attn_near[1:]), "wide", scatter_dimension=0, tiled=True)

        d_query = jnp.concatenate([back[0], back_far[0]], axis=0)
        d_proj = jnp.concatenate([after(d_query, near_a), d_key, d_value], axis=1)
        wide_cols = d_proj.shape[1] + local
        grads = product(
            after(mixed_a, *mlp_parts), d_proj, ((0,), (0,)), "grad_w_qkv", block=local, out=pltpu.HBM, micros=0,
            columns=wide_cols,
        )
        d_attn = jnp.concatenate([joined(pieces) for pieces in d_attn_pieces], axis=0)
        grads = product(
            after(d_attn, grads, *via_a), heads_out, ((0,), (0,)), "grad_w_out", block=local, out=pltpu.HBM, micros=0,
            columns=wide_cols, first=d_proj.shape[1], before=grads,
        )
        sum_rest = lax.psum_scatter(grads, "wide", scatter_dimension=0, tiled=True)
        result_own, sums_out = on_own(
            result_kernel, "result", first_own, after(slot_own, grads, *near_sent), mlp_parts, [tokens, cotangent],
            [attended], modes, (2, 5), [half], 1,
        )
        grad_tok_own, sums_a = on_own(
            back_a_kernel, "back_a", first_own, after(slot_own, result_own, sum_w_up), d_mixed_a_parts, [tokens],
            [d_middle], modes, (1,), [half], 2,
        )
        sums_sent, d_modes = to_modes(jnp.concatenate([sums_a, sums_b, sums_out], axis=1))
        d_silu_part = silu_back_call(after(d_modes, sum_w_down), w_mod_t).astype(half)
        d_silu = sum(part.astype(f32) for part in exchange([d_silu_part] * n_narrow, n_narrow))
        sigma = jax.nn.sigmoid(cond)
        grad_noise = d_silu * sigma * (1.0 + cond * (1.0 - sigma))
        table_part = jnp.dot(group_hot.T, grad_noise, precision=highest).astype(half)

        grad_tok_near = spread_near(after(grad_tok_own, d_silu_part), n_narrow)
        result_near = spread_near(after(result_own, d_silu_part), n_narrow)
        result = settle(spread(result_near, n_narrow), after(order, sum_w_down))
        ff = w_up.shape[1]
        small = jnp.pad(grad_b_up.astype(half), (0, -ff % width)).reshape(-1, width)
        late = lax.all_gather(
            jnp.concatenate([d_modes.reshape(-1, width), small, table_part], axis=0), "wide", axis=0
        )
        grad_tokens = settle(spread(grad_tok_near, n_narrow), after(order, result))

        col = width // n_wide
        ff_part = ff // n_wide
        part_b = local // n_wide
        silu_cols = lax.dynamic_slice_in_dim(silu_all[:, :slots], place * col, col, 2).reshape(-1, col)
        mode_rows = 6 * slots * local // width
        small_rows = mode_rows + small.shape[0]
        b_up_all = late[:, mode_rows:small_rows].reshape(n_wide, -1)[:, :ff]
        sum_b_up = jnp.sum(
            lax.dynamic_slice_in_dim(b_up_all, place * ff_part, ff_part, 1).astype(f32), axis=0
        )
        d_modes_all = late[:, :mode_rows].reshape(n_wide, 6, slots, local)
        d_modes_all = d_modes_all.transpose(1, 0, 2, 3).reshape(6, n_wide * slots, local)
        grad_w_mod = jnp.einsum("sd,gsv->gdv", silu_cols, d_modes_all, preferred_element_type=f32).transpose(1, 0, 2)
        sum_b_mod = jnp.sum(
            lax.dynamic_slice_in_dim(d_modes_all, place * part_b, part_b, 2).astype(f32), axis=1
        )
        sum_table = jnp.sum(
            lax.dynamic_slice_in_dim(late[:, small_rows:], place * col, col, 2).astype(f32), axis=0
        )

        out_qkv, out_w_out = unpack_call(after(sum_rest, result, grad_tokens), local)
        return (
            result,
            grad_tokens,
            grad_noise,
            sum_table,
            out_qkv,
            out_w_out,
            sum_w_up.astype(f32),
            sum_b_up,
            sum_w_down.astype(f32).T,
            grad_w_mod,
            sum_b_mod,
        )

    return body


def solution(mesh):
    in_specs = (
        P("wide", None),
        P("wide", None),
        P("wide", None),
        P("wide", None),
        P("wide", None),
        P("wide", None),
        P(),
        P(None, None, "narrow"),
        P("narrow", None),
        P(None, "narrow"),
        P("narrow"),
        P("narrow", None),
        P(None, None, "narrow"),
        P(None, "narrow"),
    )
    out_specs = (
        P("wide", None),
        P("wide", None),
        P("wide", None),
        P(None, "wide"),
        P(None, "wide", "narrow"),
        P("narrow", "wide"),
        P("wide", "narrow"),
        P(("narrow", "wide")),
        P("narrow", "wide"),
        P("wide", None, "narrow"),
        P(None, ("narrow", "wide")),
    )
    body = make_body(mesh.shape["wide"], mesh.shape["narrow"])
    return jax.shard_map(body, mesh=mesh, in_specs=in_specs, out_specs=out_specs, check_vma=False)
```

```python
import jax
import jax.numpy as jnp
from jax import lax
from jax.experimental import pallas as pl
from jax.experimental.pallas import tpu as pltpu
from jax.sharding import PartitionSpec as P

HEAD_DIM = 128
SPAN = 64
MASKED = -1e30

f32 = jnp.float32
half = jnp.bfloat16
highest = lax.Precision.HIGHEST
MIB = 1 << 20


def dot(left, right, dims):
    return lax.dot_general(left, right, (dims, ((), ())), preferred_element_type=f32)


def normalize(values):
    centred = values - jnp.mean(values, axis=-1, keepdims=True)
    recip = lax.rsqrt(jnp.mean(centred * centred, axis=-1, keepdims=True) + 1e-06)
    return (centred * recip, recip)


def norm_back(grad, normed, recip):
    first = jnp.mean(grad, axis=-1, keepdims=True)
    second = jnp.mean(grad * normed, axis=-1, keepdims=True)
    return recip * (grad - first - normed * second)


def spec(shape, index):
    return pl.BlockSpec(shape, index)


def fixed(shape):
    zeros = (0,) * len(shape)
    return pl.BlockSpec(shape, lambda *_: zeros)


def held(shape):
    zeros = (0,) * len(shape)
    return pl.BlockSpec(shape, lambda *_: zeros, pipeline_mode=pl.Buffered(1))


def in_hbm(array):
    return pltpu.with_memory_space_constraint(array, pltpu.HBM)


def params(mib):
    return pltpu.CompilerParams(vmem_limit_bytes=mib * MIB)


def cost(micros):
    return pl.CostEstimate(flops=int(micros * 1.15e+09), transcendentals=0, bytes_accessed=0)


def shaped(shape, kind):
    return jax.ShapeDtypeStruct(shape, kind)


def after(values, *others):
    return lax.optimization_barrier((values, *others))[0]


def hop(values, distance, size):
    return lax.ppermute(values, "narrow", [(i, i ^ distance) for i in range(size)])


def exchange(chunks, size):
    return [chunks[0]] + [hop(chunks[d], d, size) for d in range(1, len(chunks))]


def spread_near(shard, size):
    return [shard] + [hop(shard, d, size) for d in range(1, size if size != 4 else 3)]


def spread(near, size, *gates):
    if size != 4:
        return [[piece] for piece in near]
    one, two = near[1:]
    mid = one.shape[0] // 2
    two, one = after(two[:mid], *gates), after(one[mid:], *gates)
    return [[piece] for piece in near] + [[hop(two, 1, size), hop(one, 2, size)]]


def joined(pieces):
    return jnp.concatenate(pieces, axis=0) if len(pieces) > 1 else pieces[0]


def flat(lists):
    return [piece for pieces in lists for piece in pieces]


def collect_far(far, size):
    if size != 4:
        return []
    mid = far.shape[0] // 2
    return [hop(far[:mid], 2, size), hop(far[mid:], 1, size)]


def collect_near(chunks, size, via):
    if size != 4:
        return chunks[1:]
    _, one, two, _ = chunks
    mid = one.shape[0] // 2
    via_two, via_one = via
    one = joined([(one[:mid].astype(f32) + via_two.astype(f32)).astype(half), one[mid:]])
    two = joined([two[:mid], (two[mid:].astype(f32) + via_one.astype(f32)).astype(half)])
    return [one, two]


def collect(chunks, size, via):
    return exchange(chunks[:1] + collect_near(chunks, size, via), size)


def in_order(pieces, index, axis):
    return jnp.concatenate([lax.select_n(index ^ k, *pieces) for k in range(len(pieces))], axis=axis)


def settle_kernel(layout, order_ref, *refs):
    out_ref = refs[-1]
    for d, count in enumerate(layout):

        @pl.when(pl.program_id(0) == d)
        def _(pieces=refs[sum(layout[:d]) :][:count]):
            at = 0
            for piece in pieces:
                out_ref[at : at + piece.shape[0], :] = piece[...]
                at += piece.shape[0]


def settle(chunks, order):
    rows = sum(piece.shape[0] for piece in chunks[0])
    width = chunks[0][0].shape[1]
    return pl.pallas_call(
        lambda *refs: settle_kernel([len(pieces) for pieces in chunks], *refs),
        grid_spec=pltpu.PrefetchScalarGridSpec(
            num_scalar_prefetch=1,
            grid=(len(chunks),),
            in_specs=[held(piece.shape) for piece in flat(chunks)],
            out_specs=spec((rows, width), lambda i, o: (o[i], 0)),
        ),
        out_shape=pltpu.HBM((rows * len(chunks), width), chunks[0][0].dtype),
        compiler_params=params(16),
        cost_estimate=cost(20),
        name="settle",
    )(order, *flat(chunks))


def modes_kernel(silu_ref, w_ref, b_ref, out_ref):
    out_ref[0] = (
        jnp.dot(silu_ref[...], w_ref[0], preferred_element_type=f32) + b_ref[0]
    )


def modes_call(silu_low, w_mod, b_mod, first, count):
    slots, width = silu_low.shape
    local = w_mod.shape[2]
    return pl.pallas_call(
        modes_kernel,
        grid=(count,),
        in_specs=[
            spec((slots, width), lambda g: (0, 0)),
            spec((1, width, local), lambda g: (first + g, 0, 0)),
            spec((1, 1, local), lambda g: (first + g, 0, 0)),
        ],
        out_specs=spec((1, slots, local), lambda g: (g, 0, 0)),
        out_shape=shaped((count, slots, local), f32),
        cost_estimate=cost(5),
        compiler_params=params(24),
        name="modes",
    )(silu_low, in_hbm(w_mod), b_mod[:, None, :])


def silu_back_kernel(d_ref, w_ref, out_ref):
    part = dot(d_ref[0], w_ref[0], ((1,), (1,)))

    @pl.when(pl.program_id(0) == 0)
    def _():
        out_ref[...] = part

    @pl.when(pl.program_id(0) > 0)
    def _():
        out_ref[...] = out_ref[...] + part


def silu_back_call(d_modes, w_mod):
    groups, slots, local = d_modes.shape
    width = w_mod.shape[1]
    return pl.pallas_call(
        silu_back_kernel,
        grid=(groups,),
        in_specs=[
            spec((1, slots, local), lambda g: (g, 0, 0)),
            spec((1, width, local), lambda g: (g, 0, 0)),
        ],
        out_specs=fixed((slots, width)),
        out_shape=shaped((slots, width), f32),
        compiler_params=params(16),
        cost_estimate=cost(0),
        name="silu_back",
    )(d_modes, in_hbm(w_mod))


def row_of(ref, slot):
    return ref[0, pl.ds(slot, 1), :]


def mix_kernel(order_ref, slot_ref, tok_ref, shift_ref, scale_ref, out_ref):
    step = pl.program_id(0)
    spans = tok_ref.shape[0] // SPAN
    for i in range(spans):
        rows = slice(i * SPAN, (i + 1) * SPAN)
        slot = slot_ref[step * spans + i]
        normed, _ = normalize(tok_ref[rows, :].astype(f32))
        out_ref[rows, :] = (normed * (1.0 + row_of(scale_ref, slot)) + row_of(shift_ref, slot)).astype(half)


def gate_kernel(order_ref, slot_ref, grad_ref, gate_ref, out_ref):
    step = pl.program_id(0)
    spans = grad_ref.shape[0] // SPAN
    for i in range(spans):
        rows = slice(i * SPAN, (i + 1) * SPAN)
        gate = row_of(gate_ref, slot_ref[step * spans + i])
        out_ref[rows, :] = (grad_ref[rows, :].astype(f32) * gate).astype(half)


def mode_specs(modes, columns):
    _, count, width = modes.shape
    return [spec((1, count, width), lambda i, *_, column=column: (column, 0, 0)) for column in columns]


def by_chunk(kernel, name, order, slots, values, modes, columns):
    rows, width = values.shape
    chunk = rows // order.shape[0]
    return pl.pallas_call(
        kernel,
        grid_spec=pltpu.PrefetchScalarGridSpec(
            num_scalar_prefetch=2,
            grid=(order.shape[0],),
            in_specs=[spec((chunk, width), lambda i, o, s: (o[i], 0))] + mode_specs(modes, columns),
            out_specs=spec((chunk, width), lambda i, o, s: (i, 0)),
        ),
        out_shape=shaped((rows, width), half),
        compiler_params=params(24),
        cost_estimate=cost(5),
        name=name,
    )(order, slots, values, *([modes] * len(columns)))


def product_kernel(dims, scales, left_ref, right_ref, out_ref):
    total = dot(left_ref[...], right_ref[...].reshape(right_ref.shape[-2:]), dims)
    if scales is not None:
        total = total * jnp.where(pl.program_id(0) == 0, scales, 1.0)
    out_ref[...] = total.astype(half).reshape(out_ref.shape)


def product(left, right, dims, name, block=512, out=shaped, micros=4, columns=None, first=0, before=None):
    free = 1 - dims[1][0]
    count = right.shape[free]
    rows = left.shape[1 - dims[0][0]]
    block = min(block, count)
    shape = (block, right.shape[1]) if free == 0 else (right.shape[0], block)
    index = (lambda j: (j, 0)) if free == 0 else (lambda j: (0, j))
    given = [] if before is None else [before]
    return pl.pallas_call(
        lambda left_ref, right_ref, *refs: product_kernel(dims, None, left_ref, right_ref, refs[-1]),
        grid=(count // block,),
        in_specs=[held(left.shape), spec(shape, index)] + [pl.BlockSpec(memory_space=pl.ANY)] * len(given),
        out_specs=spec((rows, block), lambda j: (0, first // block + j)),
        out_shape=out((rows, columns or count), half),
        input_output_aliases={2: 0} if given else {},
        compiler_params=params(28),
        cost_estimate=cost(micros),
        name=name,
    )(left, right, *given)


def project_call(mixed, w_qkv, factor):
    count, width, local = w_qkv.shape
    rows = mixed.shape[0]
    return pl.pallas_call(
        lambda *refs: product_kernel(((1,), (0,)), factor, *refs),
        grid=(count,),
        in_specs=[held(mixed.shape), spec((1, width, local), lambda i: (i, 0, 0))],
        out_specs=spec((1, rows, local), lambda i: (i, 0, 0)),
        out_shape=shaped((count, rows, local), half),
        compiler_params=params(28),
        cost_estimate=cost(9),
        name="project",
    )(mixed, w_qkv)


def attend_kernel(q_ref, k_ref, v_ref, qcode_ref, kcode_ref, w_ref, heads_ref, lse_ref, out_ref):
    heads = q_ref.shape[2] // HEAD_DIM
    for h in range(heads):
        cols = slice(h * HEAD_DIM, (h + 1) * HEAD_DIM)
        keys = jnp.concatenate([k_ref[0, :, cols], kcode_ref[...]], axis=1)
        query = jnp.concatenate([q_ref[0, :, cols], qcode_ref[...]], axis=1)
        scores = dot(keys, query, ((1,), (1,)))
        top = jnp.max(scores, axis=0, keepdims=True)
        expo = jnp.exp(scores - top)
        total = jnp.sum(expo, axis=0, keepdims=True)
        out = dot(v_ref[0, :, cols], expo.astype(half), ((0,), (0,)))
        heads_ref[:, cols] = (out / total).T.astype(half)
        lse_ref[0, h : h + 1, :] = top + jnp.log(total)
    out_ref[...] = jnp.dot(heads_ref[...], w_ref[...], preferred_element_type=f32).astype(half)


def attend_call(qkv, qcode, kcode, w_out, chunk, first, count):
    _, rows, local = qkv.shape
    width = w_out.shape[1]
    heads = local // HEAD_DIM
    return pl.pallas_call(
        attend_kernel,
        grid=(count,),
        in_specs=[
            spec((1, chunk, local), lambda i: (0, first + i, 0)),
            spec((1, rows, local), lambda i: (1, 0, 0)),
            spec((1, rows, local), lambda i: (2, 0, 0)),
            spec((chunk, HEAD_DIM), lambda i: (first + i, 0)),
            fixed((rows, HEAD_DIM)),
            held(w_out.shape),
        ],
        out_specs=[
            spec((chunk, local), lambda i: (i, 0)),
            spec((1, heads, chunk), lambda i: (i, 0, 0)),
            spec((chunk, width), lambda i: (i, 0)),
        ],
        out_shape=[
            shaped((count * chunk, local), half),
            shaped((count, heads, chunk), f32),
            shaped((count * chunk, width), half),
        ],
        compiler_params=params(32),
        cost_estimate=cost(2 + 3.3 * count),
        name="attend",
    )(qkv, qkv, qkv, qcode, kcode, w_out)


def attend_back_kernel(final, layout, q_ref, k_ref, v_ref, qcode_ref, kcode_ref, lse_ref, w_ref, *refs):
    chunk, local = q_ref.shape[1:]
    pieces, refs, d_heads_ref = refs[: sum(layout)], refs[sum(layout) : -1], refs[-1]
    heads = local // HEAD_DIM
    step = pl.program_id(0)
    factor = HEAD_DIM ** (-0.5)
    if final:
        dk_old, dv_old, dq_ref, dk_ref, dv_ref, dk_acc, dv_acc = refs
    else:
        dq_ref, dk_acc, dv_acc = refs

    @pl.when(step == 0)
    def _():
        dk_acc[...] = dk_old[...] if final else jnp.zeros_like(dk_acc)
        dv_acc[...] = dv_old[...] if final else jnp.zeros_like(dv_acc)

    for d, count in enumerate(layout):

        @pl.when(step == d)
        def _(refs=pieces[sum(layout[:d]) :][:count]):
            at = 0
            for ref in refs:
                d_heads_ref[at : at + ref.shape[0], :] = dot(ref[...], w_ref[...], ((1,), (1,))).astype(half)
                at += ref.shape[0]

    for h in range(heads):
        cols = slice(h * HEAD_DIM, (h + 1) * HEAD_DIM)
        keys = jnp.concatenate([k_ref[0, :, cols], kcode_ref[...]], axis=1)
        query = jnp.concatenate([q_ref[0, :, cols], qcode_ref[...]], axis=1)
        grad = d_heads_ref[:, cols]
        scores = dot(keys, query, ((1,), (1,)))
        probs = jnp.exp(scores - lse_ref[0, h : h + 1, :])
        d_probs = dot(v_ref[0, :, cols], grad, ((1,), (1,)))
        inner = jnp.sum(probs * d_probs, axis=0, keepdims=True)
        d_scores = (probs * (d_probs - inner)).astype(half)
        dv_acc[:, cols] += dot(probs.astype(half), grad, ((1,), (0,)))
        dk_acc[:, cols] += dot(d_scores, q_ref[0, :, cols], ((1,), (0,)))
        dq = dot(k_ref[0, :, cols], d_scores, ((0,), (0,)))
        dq_ref[:, cols] = (dq.T * factor).astype(half)

    if final:

        @pl.when(step == pl.num_programs(0) - 1)
        def _():
            dk_ref[...] = dk_acc[...].astype(half)
            dv_ref[...] = dv_acc[...].astype(half)


def attend_back_call(qkv, qcode, kcode, lse, w_out, d_attn, first, sums):
    _, rows, local = qkv.shape
    _, heads, chunk = lse.shape
    count = len(d_attn)
    final = sums is not None
    whole = (rows, local)
    return pl.pallas_call(
        lambda *refs: attend_back_kernel(final, [len(pieces) for pieces in d_attn], *refs),
        grid=(count,),
        in_specs=[
            spec((1, chunk, local), lambda i: (0, first + i, 0)),
            spec((1, rows, local), lambda i: (1, 0, 0)),
            spec((1, rows, local), lambda i: (2, 0, 0)),
            spec((chunk, HEAD_DIM), lambda i: (first + i, 0)),
            fixed((rows, HEAD_DIM)),
            spec((1, heads, chunk), lambda i: (first + i, 0, 0)),
            held(w_out.shape),
        ]
        + [held(piece.shape) for piece in flat(d_attn)]
        + ([held(whole)] * 2 if final else []),
        out_specs=[spec((chunk, local), lambda i: (i, 0))] + [fixed(whole)] * 2,
        out_shape=[shaped((count * chunk, local), half)] + [shaped(whole, half if final else f32)] * 2,
        scratch_shapes=([pltpu.VMEM(whole, f32)] * 2 if final else []) + [pltpu.VMEM((chunk, local), half)],
        compiler_params=params(36),
        cost_estimate=cost(0 if final else 130),
        name="attend_back",
    )(qkv, qkv, qkv, qcode, kcode, lse, w_out, *flat(d_attn), *(sums if final else []))


def project_back_kernel(q_ref, k_ref, v_ref, w_ref, out_ref):
    total = None
    for i, ref in enumerate((q_ref, k_ref, v_ref)):
        part = dot(ref[...], w_ref[i], ((1,), (1,)))
        total = part if total is None else total + part
    out_ref[...] = total.astype(half)


def project_back_call(d_query, d_key, d_value, w_qkv, chunk, first, count, first_query):
    _, width, local = w_qkv.shape
    there = lambda i: (first + i, 0)
    return pl.pallas_call(
        project_back_kernel,
        grid=(count,),
        in_specs=[
            spec((chunk, local), lambda i: (first - first_query + i, 0)),
            spec((chunk, local), there),
            spec((chunk, local), there),
            held(w_qkv.shape),
        ],
        out_specs=spec((chunk, width), lambda i: (i, 0)),
        out_shape=shaped((count * chunk, width), half),
        compiler_params=params(32),
        cost_estimate=cost(0),
        name="project_back",
    )(d_query, d_key, d_value, w_qkv)


def total_of(terms):
    return jnp.sum(terms, axis=0, keepdims=True)


def mlp_kernel(count, *refs):
    x_refs = refs[:count]
    up_ref, b_ref, d_ref = refs[count : count + 3]
    hidden_ref, d_pre_ref, dx_ref, b_sum_ref, acc_ref = refs[-5:]
    step = pl.program_id(0)
    mixed = jnp.concatenate([ref[...] for ref in x_refs], axis=0) if count > 1 else x_refs[0][...]
    pre = jnp.dot(mixed, up_ref[...], preferred_element_type=f32) + b_ref[...]
    cumul = 0.5 * (1.0 + lax.erf(pre * 0.7071067811865476))
    density = jnp.exp(-0.5 * pre * pre) * 0.3989422804014327
    hidden_ref[...] = (pre * cumul).astype(half)
    d_pre = (d_ref[...].astype(f32) * (cumul + pre * density)).astype(half)
    d_pre_ref[...] = d_pre
    b_sum_ref[...] = total_of(d_pre.astype(f32))
    part = dot(d_pre, up_ref[...], ((1,), (1,)))

    @pl.when(step == 0)
    def _():
        acc_ref[...] = part

    @pl.when(step > 0)
    def _():
        acc_ref[...] += part

    @pl.when(step == pl.num_programs(0) - 1)
    def _():
        dx_ref[...] = acc_ref[...].astype(half)


def mlp_call(pieces, w_up, b_up, d_hidden, chunk, before):
    rows = sum(piece.shape[0] for piece in pieces)
    width, ff = w_up.shape
    block = min(1024, ff)
    here = lambda j: (chunk, j)
    operands = [*pieces, w_up, b_up[None, :], d_hidden]
    in_specs = [held(piece.shape) for piece in pieces] + [
        spec((width, block), lambda j: (0, j)),
        spec((1, block), lambda j: (0, j)),
        spec((rows, block), here),
    ]
    aliases = {}
    if before is not None:
        aliases = {len(operands): 0, len(operands) + 1: 1}
        operands += before
        in_specs += [pl.BlockSpec(memory_space=pl.ANY)] * 2
    return pl.pallas_call(
        lambda *refs: mlp_kernel(len(pieces), *refs),
        grid=(ff // block,),
        in_specs=in_specs,
        out_specs=[
            spec((rows, block), here),
            spec((rows, block), here),
            fixed((rows, width)),
            spec((1, block), lambda j: (0, j)),
        ],
        out_shape=[
            shaped((d_hidden.shape[0], ff), half),
            shaped((d_hidden.shape[0], ff), half),
            pltpu.VMEM((rows, width), half),
            shaped((1, ff), f32),
        ],
        scratch_shapes=[pltpu.VMEM((rows, width), f32)],
        input_output_aliases=aliases,
        compiler_params=params(24),
        cost_estimate=cost(3),
        name="mlp",
    )(*operands)


def summed(refs):
    total = refs[0][...].astype(f32)
    for ref in refs[1:]:
        total = total + ref[...].astype(f32)
    return total


def middle_kernel(count, first_ref, slot_ref, *refs):
    tok_ref, gate_ref, shift_ref, scale_ref, mixed_ref, attended_ref = refs[count:]
    slot = slot_ref[pl.program_id(0)]
    attended = summed(refs[:count])
    attended_ref[...] = attended
    normed, _ = normalize(tok_ref[...].astype(f32) + row_of(gate_ref, slot) * attended)
    mixed_ref[...] = (normed * (1.0 + row_of(scale_ref, slot)) + row_of(shift_ref, slot)).astype(half)


def back_b_kernel(count, first_ref, slot_ref, *refs):
    tok_ref, grad_ref, attended_ref, gate_ref, scale_ref, d_attn_ref, d_middle_ref, sums_ref = refs[count:]
    slot = slot_ref[pl.program_id(0)]
    gate = row_of(gate_ref, slot)
    attended = attended_ref[...]
    normed, recip = normalize(tok_ref[...].astype(f32) + gate * attended)
    d_mixed = summed(refs[:count])
    back = norm_back(d_mixed * (1.0 + row_of(scale_ref, slot)), normed, recip)
    d_middle = grad_ref[...].astype(f32) + back
    d_middle_ref[...] = d_middle
    d_attn_ref[...] = (d_middle * gate).astype(half)
    sums_ref[0, 0:1, :] = total_of(d_middle * attended)
    sums_ref[0, 1:2, :] = total_of(d_mixed)
    sums_ref[0, 2:3, :] = total_of(d_mixed * normed)


def back_a_kernel(count, first_ref, slot_ref, *refs):
    tok_ref, d_middle_ref, scale_ref, out_ref, sums_ref = refs[count:]
    slot = slot_ref[pl.program_id(0)]
    normed, recip = normalize(tok_ref[...].astype(f32))
    d_mixed = summed(refs[:count])
    back = norm_back(d_mixed * (1.0 + row_of(scale_ref, slot)), normed, recip)
    out_ref[...] = (d_middle_ref[...] + back).astype(half)
    sums_ref[0, 0:1, :] = total_of(d_mixed)
    sums_ref[0, 1:2, :] = total_of(d_mixed * normed)


def result_kernel(count, first_ref, slot_ref, *refs):
    tok_ref, grad_ref, attended_ref, gate_a_ref, gate_b_ref, out_ref, sums_ref = refs[count:]
    slot = slot_ref[pl.program_id(0)]
    middle = tok_ref[...].astype(f32) + row_of(gate_a_ref, slot) * attended_ref[...]
    mlp_out = summed(refs[:count])
    out_ref[...] = (middle + row_of(gate_b_ref, slot) * mlp_out).astype(half)
    sums_ref[0, 0:1, :] = total_of(grad_ref[...].astype(f32) * mlp_out)


def on_own(kernel, name, first, slots, parts, whole, own, modes, columns, outs, terms):
    rows, width = own[0].shape if own else (slots.shape[0] * SPAN, whole[0].shape[1])
    spans = rows // SPAN
    block = (SPAN, width)
    here = spec(block, lambda i, m, s: (i, 0))
    return pl.pallas_call(
        lambda *refs: kernel(len(parts), *refs),
        grid_spec=pltpu.PrefetchScalarGridSpec(
            num_scalar_prefetch=2,
            grid=(spans,),
            in_specs=[here] * len(parts)
            + [spec(block, lambda i, m, s: (m[0] + i, 0))] * len(whole)
            + [here] * len(own)
            + mode_specs(modes, columns),
            out_specs=[here] * len(outs) + ([spec((1, terms, width), lambda i, m, s: (i, 0, 0))] if terms else []),
        ),
        out_shape=[shaped((rows, width), kind) for kind in outs]
        + ([shaped((spans, terms, width), f32)] if terms else []),
        compiler_params=params(24),
        cost_estimate=cost(0 if name in ("result", "back_a") else 5),
        name=name,
    )(first[None], slots, *parts, *[in_hbm(array) for array in whole], *own, *([modes] * len(columns)))


def unpack_kernel(sum_ref, qkv_ref, out_ref):
    step = pl.program_id(0)

    @pl.when(step < 3)
    def _():
        qkv_ref[0] = sum_ref[...].astype(f32)

    @pl.when(step == 3)
    def _():
        out_ref[...] = sum_ref[...].astype(f32).T


def unpack_call(sums, local):
    rows = sums.shape[0]
    return pl.pallas_call(
        unpack_kernel,
        grid=(4,),
        in_specs=[spec((rows, local), lambda i: (0, i))],
        out_specs=[
            spec((1, rows, local), lambda i: (jnp.minimum(i, 2), 0, 0)),
            fixed((local, rows)),
        ],
        out_shape=[pltpu.HBM((3, rows, local), f32), pltpu.HBM((local, rows), f32)],
        compiler_params=params(16),
        cost_estimate=cost(2),
        name="unpack",
    )(in_hbm(sums))


def make_body(n_wide, n_narrow):
    def body(
        tokens,
        cotangent,
        noise_emb,
        offsets,
        lengths,
        group_ids,
        group_table,
        w_qkv,
        w_out,
        w_up,
        b_up,
        w_down,
        w_mod,
        b_mod,
    ):
        tok_dev, width = tokens.shape
        slots = offsets.shape[1]
        local = w_qkv.shape[2]
        groups = group_table.shape[0]
        rows = tok_dev // n_narrow
        spans = rows // SPAN
        last = n_narrow - 1
        me = lax.axis_index("narrow")
        place = lax.axis_index("wide")
        order = me ^ jnp.arange(n_narrow, dtype=jnp.int32)
        first_own = me * spans

        starts = (order[:, None] * spans + jnp.arange(spans, dtype=jnp.int32)[None, :]).reshape(-1, 1) * SPAN
        inside = (starts >= offsets) & (starts < offsets + lengths)
        slot_hot = inside.astype(f32)
        slot_of = jnp.sum(inside * jnp.arange(slots, dtype=jnp.int32)[None, :], axis=1).astype(jnp.int32)
        slot_own = slot_of[:spans]
        lanes = jnp.arange(HEAD_DIM, dtype=jnp.int32)
        same = jnp.repeat(slot_of, SPAN)[:, None] == lanes[None, :]
        kcode = same.astype(half)
        qcode = jnp.where(same, 0.0, MASKED).astype(half)

        group_hot = (group_ids[0][:, None] == jnp.arange(groups, dtype=jnp.int32)[None, :]).astype(f32)
        cond = noise_emb + jnp.dot(group_hot, group_table, precision=highest)
        silu_low = jax.nn.silu(cond).astype(half)
        w_mod_t = w_mod.transpose(1, 0, 2)

        silu_all = lax.all_gather(jnp.concatenate([silu_low, silu_low], axis=0), "wide", axis=0)

        own_a = modes_call(silu_low, w_mod_t, b_mod, 0, 2)
        got_a = exchange([own_a] * n_narrow, n_narrow)
        own_b = modes_call(after(silu_low, own_a), w_mod_t, b_mod, 2, 4)
        modes_a = in_order(got_a, me, 2)
        mixed_a = by_chunk(mix_kernel, "mix_a", after(order, own_b), slot_of, tokens, modes_a, (0, 1))
        qkv = project_call(mixed_a, w_qkv, HEAD_DIM ** (-0.5))

        far = attend_call(qkv, qcode, kcode, w_out, rows, last, 1)
        via = collect_far(far[2], n_narrow)
        got_b = exchange([after(own_b, far[0])] * n_narrow, n_narrow)
        near = attend_call(qkv, after(qcode, far[0], silu_all), kcode, w_out, rows, 0, last)
        modes = jnp.concatenate([modes_a, in_order([after(got, near[0]) for got in got_b], me, 2)], axis=0)
        heads_out = jnp.concatenate([near[0], far[0]], axis=0)
        lse = jnp.concatenate([near[1], far[1]], axis=0)
        sent = [near[2][d * rows : (d + 1) * rows] for d in range(last)] + [far[2]]
        attended_parts = collect(sent, n_narrow, via)

        calls = [[(d, 0), (d, 1)] for d in range(n_narrow)]
        if n_narrow == 4:
            calls[1:3] = [[(1, 0), (2, 0)], [(1, 1), (2, 1)]]
        halves = flat(calls)
        block = rows // 2
        order_mlp = jnp.stack([2 * (me ^ d) + h for d, h in halves])
        slot_mlp = slot_of.reshape(2 * n_narrow, -1)[jnp.array([2 * d + h for d, h in halves])].reshape(-1)
        d_mlp = by_chunk(gate_kernel, "d_mlp", after(order_mlp, near[0]), slot_mlp, cotangent, modes, (5,))
        d_hidden = product(d_mlp, w_down, ((1,), (1,)), "d_hidden")
        mixed_own, attended = on_own(
            middle_kernel, "middle", first_own, after(slot_own, d_hidden), attended_parts, [tokens], [],
            modes, (2, 3, 4), [half, f32], 0,
        )
        pieces = {(0, h): mixed_own[h * block : (h + 1) * block] for h in range(2)}

        def send(half):
            for d in range(1, n_narrow if n_narrow != 4 else 3):
                pieces[d, half] = hop(pieces[0, half], d, n_narrow)

        send(0)
        pair, d_mixed, b_sums, due = None, {}, [], []
        for k, call in enumerate(calls):
            given = [pieces[half_chunk] for half_chunk in call] if k else [mixed_own]
            if k == 3 and n_narrow == 4:
                given = [pieces[half_chunk] for half_chunk in call]
            outs = mlp_call(given, w_up, after(b_up, *due), d_hidden, k, pair)
            pair = list(outs[:2])
            for i, half_chunk in enumerate(call):
                d_mixed[half_chunk] = outs[2][i * block : (i + 1) * block] if call[0][0] != call[1][0] else outs[2]
            b_sums.append(outs[3])
            due = [outs[2]]
            if k == 1 and n_narrow == 4:
                pieces[3, 0] = hop(after(pieces[2, 0], outs[2]), 1, n_narrow)
                pieces[3, 1] = hop(after(pieces[1, 1], outs[2]), 2, n_narrow)
            if not k:
                pieces[0, 1] = after(pieces[0, 1], outs[2])
                send(1)
        hidden, d_pre = pair

        def of_distance(d):
            first, second = d_mixed[d, 0], d_mixed[d, 1]
            if first is second:
                return first
            return after(joined([first, second]), pieces[last, 0], pieces[last, 1])

        d_mixed_parts = exchange([of_distance(d) for d in range(n_narrow)], n_narrow)
        mixed_b = jnp.concatenate([mixed_own] + [pieces[half_chunk] for half_chunk in halves[2:]], axis=0)

        def mlp_chunks(array):
            at = {half_chunk: k * block for k, half_chunk in enumerate(halves)}
            return [
                joined([array[at[d, h] : at[d, h] + block] for h in range(2)]) for d in range(n_narrow)
            ]

        grad_b_up = after(sum(b_sums)[0], hidden)

        grad_w_up = product(mixed_b, d_pre, ((0,), (0,)), "grad_w_up", out=pltpu.HBM, micros=4)
        sum_w_up = lax.psum_scatter(grad_w_up, "wide", scatter_dimension=0, tiled=True)
        grad_w_down = product(d_mlp, after(hidden, grad_w_up), ((0,), (0,)), "grad_w_down", out=pltpu.HBM, micros=4)

        d_attn_own, d_middle, sums_b = on_own(
            back_b_kernel, "back_b", first_own, after(slot_own, grad_w_down), d_mixed_parts, [tokens, cotangent],
            [attended], modes, (2, 4), [half, f32], 3,
        )

        def to_modes(sums):
            sent = [lax.dynamic_slice_in_dim(sums, (me ^ d) * local, local, 2) for d in range(n_narrow)]
            got = exchange(sent, n_narrow)
            modes_back = jnp.einsum("bs,bgv->gsv", slot_hot, jnp.concatenate(got, axis=0), precision=highest)
            return sent, modes_back.astype(half)

        d_attn_near = spread_near(d_attn_own, n_narrow)

        mlp_sent = product(after(hidden, d_attn_own), w_down, ((1,), (0,)), "mlp_out", micros=200)
        d_attn_pieces = spread(d_attn_near, n_narrow, mlp_sent)
        mlp_sent = after(mlp_sent, *d_attn_near[1:])
        mlp_parts = exchange(mlp_chunks(mlp_sent), n_narrow)
        back = attend_back_call(qkv, qcode, kcode, lse, w_out, d_attn_pieces[:last], 0, None)
        back_far = attend_back_call(
            qkv, after(qcode, back[0]), kcode, lse, w_out, d_attn_pieces[last:], last, back[1:]
        )
        d_key, d_value = back_far[1:]
        far_a = project_back_call(back_far[0], d_key, d_value, w_qkv, rows, last, 1, last)
        via_a = collect_far(far_a, n_narrow)
        near_a = project_back_call(back[0], after(d_key, far_a), d_value, w_qkv, rows, 0, last, 0)
        sent_a = [near_a[d * rows : (d + 1) * rows] for d in range(last)] + [far_a]
        near_sent = collect_near(sent_a, n_narrow, via_a)
        d_mixed_a_parts = exchange(sent_a[:1] + near_sent, n_narrow)
        sum_w_down = lax.psum_scatter(after(grad_w_down, *d_attn_near[1:]), "wide", scatter_dimension=0, tiled=True)

        d_query = jnp.concatenate([back[0], back_far[0]], axis=0)
        d_proj = jnp.concatenate([after(d_query, near_a), d_key, d_value], axis=1)
        wide_cols = d_proj.shape[1] + local
        grads = product(
            after(mixed_a, *mlp_parts), d_proj, ((0,), (0,)), "grad_w_qkv", block=local, out=pltpu.HBM, micros=0,
            columns=wide_cols,
        )
        d_attn = jnp.concatenate([joined(pieces) for pieces in d_attn_pieces], axis=0)
        grads = product(
            after(d_attn, grads, *via_a), heads_out, ((0,), (0,)), "grad_w_out", block=local, out=pltpu.HBM, micros=0,
            columns=wide_cols, first=d_proj.shape[1], before=grads,
        )
        sum_rest = lax.psum_scatter(grads, "wide", scatter_dimension=0, tiled=True)
        result_own, sums_out = on_own(
            result_kernel, "result", first_own, after(slot_own, grads, *near_sent), mlp_parts, [tokens, cotangent],
            [attended], modes, (2, 5), [half], 1,
        )
        grad_tok_own, sums_a = on_own(
            back_a_kernel, "back_a", first_own, after(slot_own, result_own, sum_w_up), d_mixed_a_parts, [tokens],
            [d_middle], modes, (1,), [half], 2,
        )
        sums_sent, d_modes = to_modes(jnp.concatenate([sums_a, sums_b, sums_out], axis=1))
        d_silu_part = silu_back_call(after(d_modes, sum_w_down), w_mod_t).astype(half)
        d_silu = sum(part.astype(f32) for part in exchange([d_silu_part] * n_narrow, n_narrow))
        sigma = jax.nn.sigmoid(cond)
        grad_noise = d_silu * sigma * (1.0 + cond * (1.0 - sigma))
        table_part = jnp.dot(group_hot.T, grad_noise, precision=highest).astype(half)

        grad_tok_near = spread_near(after(grad_tok_own, d_silu_part), n_narrow)
        result_near = spread_near(after(result_own, d_silu_part), n_narrow)
        ff = w_up.shape[1]
        small = jnp.pad(grad_b_up.astype(half), (0, -ff % width)).reshape(-1, width)
        late = lax.all_gather(
            jnp.concatenate([d_modes.reshape(-1, width), small, table_part], axis=0), "wide", axis=0
        )
        result = settle(spread(result_near, n_narrow, late), after(order, sum_w_down))
        grad_tokens = settle(spread(grad_tok_near, n_narrow, late), after(order, result))

        col = width // n_wide
        ff_part = ff // n_wide
        part_b = local // n_wide
        silu_cols = lax.dynamic_slice_in_dim(silu_all[:, :slots], place * col, col, 2).reshape(-1, col)
        mode_rows = 6 * slots * local // width
        small_rows = mode_rows + small.shape[0]
        b_up_all = late[:, mode_rows:small_rows].reshape(n_wide, -1)[:, :ff]
        sum_b_up = jnp.sum(
            lax.dynamic_slice_in_dim(b_up_all, place * ff_part, ff_part, 1).astype(f32), axis=0
        )
        d_modes_all = late[:, :mode_rows].reshape(n_wide, 6, slots, local)
        d_modes_all = d_modes_all.transpose(1, 0, 2, 3).reshape(6, n_wide * slots, local)
        grad_w_mod = jnp.einsum("sd,gsv->gdv", silu_cols, d_modes_all, preferred_element_type=f32).transpose(1, 0, 2)
        sum_b_mod = jnp.sum(
            lax.dynamic_slice_in_dim(d_modes_all, place * part_b, part_b, 2).astype(f32), axis=1
        )
        sum_table = jnp.sum(
            lax.dynamic_slice_in_dim(late[:, small_rows:], place * col, col, 2).astype(f32), axis=0
        )

        out_qkv, out_w_out = unpack_call(after(sum_rest, result, grad_tokens), local)
        return (
            result,
            grad_tokens,
            grad_noise,
            sum_table,
            out_qkv,
            out_w_out,
            sum_w_up.astype(f32),
            sum_b_up,
            sum_w_down.astype(f32).T,
            grad_w_mod,
            sum_b_mod,
        )

    return body


def solution(mesh):
    in_specs = (
        P("wide", None),
        P("wide", None),
        P("wide", None),
        P("wide", None),
        P("wide", None),
        P("wide", None),
        P(),
        P(None, None, "narrow"),
        P("narrow", None),
        P(None, "narrow"),
        P("narrow"),
        P("narrow", None),
        P(None, None, "narrow"),
        P(None, "narrow"),
    )
    out_specs = (
        P("wide", None),
        P("wide", None),
        P("wide", None),
        P(None, "wide"),
        P(None, "wide", "narrow"),
        P("narrow", "wide"),
        P("wide", "narrow"),
        P(("narrow", "wide")),
        P("narrow", "wide"),
        P("wide", None, "narrow"),
        P(None, ("narrow", "wide")),
    )
    body = make_body(mesh.shape["wide"], mesh.shape["narrow"])
    return jax.shard_map(body, mesh=mesh, in_specs=in_specs, out_specs=out_specs, check_vma=False)
```

```python
import jax
import jax.numpy as jnp
from jax import lax
from jax.experimental import pallas as pl
from jax.experimental.pallas import tpu as pltpu
from jax.sharding import PartitionSpec as P

HEAD_DIM = 128
SPAN = 64
MASKED = -1e30

f32 = jnp.float32
half = jnp.bfloat16
highest = lax.Precision.HIGHEST
MIB = 1 << 20


def dot(left, right, dims):
    return lax.dot_general(left, right, (dims, ((), ())), preferred_element_type=f32)


def normalize(values):
    centred = values - jnp.mean(values, axis=-1, keepdims=True)
    recip = lax.rsqrt(jnp.mean(centred * centred, axis=-1, keepdims=True) + 1e-06)
    return (centred * recip, recip)


def norm_back(grad, normed, recip):
    first = jnp.mean(grad, axis=-1, keepdims=True)
    second = jnp.mean(grad * normed, axis=-1, keepdims=True)
    return recip * (grad - first - normed * second)


def spec(shape, index):
    return pl.BlockSpec(shape, index)


def fixed(shape):
    zeros = (0,) * len(shape)
    return pl.BlockSpec(shape, lambda *_: zeros)


def held(shape):
    zeros = (0,) * len(shape)
    return pl.BlockSpec(shape, lambda *_: zeros, pipeline_mode=pl.Buffered(1))


def in_hbm(array):
    return pltpu.with_memory_space_constraint(array, pltpu.HBM)


def params(mib):
    return pltpu.CompilerParams(vmem_limit_bytes=mib * MIB)


def cost(micros):
    return pl.CostEstimate(flops=int(micros * 1.15e+09), transcendentals=0, bytes_accessed=0)


def shaped(shape, kind):
    return jax.ShapeDtypeStruct(shape, kind)


def after(values, *others):
    return lax.optimization_barrier((values, *others))[0]


def hop(values, distance, size):
    return lax.ppermute(values, "narrow", [(i, i ^ distance) for i in range(size)])


def exchange(chunks, size):
    return [chunks[0]] + [hop(chunks[d], d, size) for d in range(1, len(chunks))]


def spread_near(shard, size):
    return [shard] + [hop(shard, d, size) for d in range(1, size if size != 4 else 3)]


def spread(near, size, *gates):
    if size != 4:
        return [[piece] for piece in near]
    one, two = near[1:]
    mid = one.shape[0] // 2
    two, one = after(two[:mid], *gates), after(one[mid:], *gates)
    return [[piece] for piece in near] + [[hop(two, 1, size), hop(one, 2, size)]]


def joined(pieces):
    return jnp.concatenate(pieces, axis=0) if len(pieces) > 1 else pieces[0]


def flat(lists):
    return [piece for pieces in lists for piece in pieces]


def collect_far(far, size):
    if size != 4:
        return []
    mid = far.shape[0] // 2
    return [hop(far[:mid], 2, size), hop(far[mid:], 1, size)]


def collect_near(chunks, size, via):
    if size != 4:
        return chunks[1:]
    _, one, two, _ = chunks
    mid = one.shape[0] // 2
    via_two, via_one = via
    one = joined([(one[:mid].astype(f32) + via_two.astype(f32)).astype(half), one[mid:]])
    two = joined([two[:mid], (two[mid:].astype(f32) + via_one.astype(f32)).astype(half)])
    return [one, two]


def collect(chunks, size, via):
    return exchange(chunks[:1] + collect_near(chunks, size, via), size)


def in_order(pieces, index, axis):
    return jnp.concatenate([lax.select_n(index ^ k, *pieces) for k in range(len(pieces))], axis=axis)


def settle_kernel(layout, order_ref, *refs):
    out_ref = refs[-1]
    for d, count in enumerate(layout):

        @pl.when(pl.program_id(0) == d)
        def _(pieces=refs[sum(layout[:d]) :][:count]):
            at = 0
            for piece in pieces:
                out_ref[at : at + piece.shape[0], :] = piece[...]
                at += piece.shape[0]


def settle(chunks, order):
    rows = sum(piece.shape[0] for piece in chunks[0])
    width = chunks[0][0].shape[1]
    return pl.pallas_call(
        lambda *refs: settle_kernel([len(pieces) for pieces in chunks], *refs),
        grid_spec=pltpu.PrefetchScalarGridSpec(
            num_scalar_prefetch=1,
            grid=(len(chunks),),
            in_specs=[held(piece.shape) for piece in flat(chunks)],
            out_specs=spec((rows, width), lambda i, o: (o[i], 0)),
        ),
        out_shape=pltpu.HBM((rows * len(chunks), width), chunks[0][0].dtype),
        compiler_params=params(16),
        cost_estimate=cost(20),
        name="settle",
    )(order, *flat(chunks))


def modes_kernel(silu_ref, w_ref, b_ref, out_ref):
    for g in range(w_ref.shape[0]):
        out_ref[g] = jnp.dot(silu_ref[...], w_ref[g], preferred_element_type=f32) + b_ref[g]


def modes_call(silu_low, w_mod, b_mod, first, count):
    slots, width = silu_low.shape
    local = w_mod.shape[2]
    there = lambda i: (first // 2 + i, 0, 0)
    return pl.pallas_call(
        modes_kernel,
        grid=(count // 2,),
        in_specs=[
            fixed((slots, width)),
            spec((2, width, local), there),
            spec((2, 1, local), there),
        ],
        out_specs=spec((2, slots, local), lambda i: (i, 0, 0)),
        out_shape=shaped((count, slots, local), f32),
        cost_estimate=cost(1.5 * count),
        compiler_params=params(24),
        name="modes",
    )(silu_low, in_hbm(w_mod), b_mod[:, None, :])


def silu_back_kernel(d_ref, w_ref, out_ref):
    part = dot(d_ref[0], w_ref[0], ((1,), (1,)))

    @pl.when(pl.program_id(0) == 0)
    def _():
        out_ref[...] = part

    @pl.when(pl.program_id(0) > 0)
    def _():
        out_ref[...] = out_ref[...] + part


def silu_back_call(d_modes, w_mod):
    groups, slots, local = d_modes.shape
    width = w_mod.shape[1]
    return pl.pallas_call(
        silu_back_kernel,
        grid=(groups,),
        in_specs=[
            spec((1, slots, local), lambda g: (g, 0, 0)),
            spec((1, width, local), lambda g: (g, 0, 0)),
        ],
        out_specs=fixed((slots, width)),
        out_shape=shaped((slots, width), f32),
        compiler_params=params(16),
        cost_estimate=cost(0),
        name="silu_back",
    )(d_modes, in_hbm(w_mod))


def row_of(ref, slot):
    return ref[0, pl.ds(slot, 1), :]


def mix_kernel(order_ref, slot_ref, tok_ref, shift_ref, scale_ref, out_ref):
    step = pl.program_id(0)
    spans = tok_ref.shape[0] // SPAN
    for i in range(spans):
        rows = slice(i * SPAN, (i + 1) * SPAN)
        slot = slot_ref[step * spans + i]
        normed, _ = normalize(tok_ref[rows, :].astype(f32))
        out_ref[rows, :] = (normed * (1.0 + row_of(scale_ref, slot)) + row_of(shift_ref, slot)).astype(half)


def gate_kernel(order_ref, slot_ref, grad_ref, gate_ref, out_ref):
    step = pl.program_id(0)
    spans = grad_ref.shape[0] // SPAN
    for i in range(spans):
        rows = slice(i * SPAN, (i + 1) * SPAN)
        gate = row_of(gate_ref, slot_ref[step * spans + i])
        out_ref[rows, :] = (grad_ref[rows, :].astype(f32) * gate).astype(half)


def mode_specs(modes, columns):
    _, count, width = modes.shape
    return [spec((1, count, width), lambda i, *_, column=column: (column, 0, 0)) for column in columns]


def by_chunk(kernel, name, order, slots, values, modes, columns):
    rows, width = values.shape
    chunk = rows // order.shape[0]
    return pl.pallas_call(
        kernel,
        grid_spec=pltpu.PrefetchScalarGridSpec(
            num_scalar_prefetch=2,
            grid=(order.shape[0],),
            in_specs=[spec((chunk, width), lambda i, o, s: (o[i], 0))] + mode_specs(modes, columns),
            out_specs=spec((chunk, width), lambda i, o, s: (i, 0)),
        ),
        out_shape=shaped((rows, width), half),
        compiler_params=params(24),
        cost_estimate=cost(5),
        name=name,
    )(order, slots, values, *([modes] * len(columns)))


def product_kernel(dims, scales, left_ref, right_ref, out_ref):
    total = dot(left_ref[...], right_ref[...].reshape(right_ref.shape[-2:]), dims)
    if scales is not None:
        total = total * jnp.where(pl.program_id(0) == 0, scales, 1.0)
    out_ref[...] = total.astype(half).reshape(out_ref.shape)


def product(left, right, dims, name, block=512, out=shaped, micros=4, columns=None, first=0, before=None, gate=None):
    free = 1 - dims[1][0]
    count = right.shape[free]
    rows = left.shape[1 - dims[0][0]]
    block = min(block, count)
    shape = (block, right.shape[1]) if free == 0 else (right.shape[0], block)
    index = (lambda j: (j, 0)) if free == 0 else (lambda j: (0, j))
    given = ([] if before is None else [before]) + ([] if gate is None else [gate])
    return pl.pallas_call(
        lambda left_ref, right_ref, *refs: product_kernel(dims, None, left_ref, right_ref, refs[-1]),
        grid=(count // block,),
        in_specs=[held(left.shape), spec(shape, index)] + [pl.BlockSpec(memory_space=pl.ANY)] * len(given),
        out_specs=spec((rows, block), lambda j: (0, first // block + j)),
        out_shape=out((rows, columns or count), half),
        input_output_aliases={} if before is None else {2: 0},
        compiler_params=params(28),
        cost_estimate=cost(micros),
        name=name,
    )(left, right, *given)


def project_call(mixed, w_qkv, factor):
    count, width, local = w_qkv.shape
    rows = mixed.shape[0]
    return pl.pallas_call(
        lambda *refs: product_kernel(((1,), (0,)), factor, *refs),
        grid=(count,),
        in_specs=[held(mixed.shape), spec((1, width, local), lambda i: (i, 0, 0))],
        out_specs=spec((1, rows, local), lambda i: (i, 0, 0)),
        out_shape=shaped((count, rows, local), half),
        compiler_params=params(28),
        cost_estimate=cost(9),
        name="project",
    )(mixed, w_qkv)


def attend_kernel(q_ref, k_ref, v_ref, qcode_ref, kcode_ref, w_ref, heads_ref, lse_ref, out_ref):
    heads = q_ref.shape[2] // HEAD_DIM
    for h in range(heads):
        cols = slice(h * HEAD_DIM, (h + 1) * HEAD_DIM)
        keys = jnp.concatenate([k_ref[0, :, cols], kcode_ref[...]], axis=1)
        query = jnp.concatenate([q_ref[0, :, cols], qcode_ref[...]], axis=1)
        scores = dot(keys, query, ((1,), (1,)))
        top = jnp.max(scores, axis=0, keepdims=True)
        expo = jnp.exp(scores - top)
        total = jnp.sum(expo, axis=0, keepdims=True)
        out = dot(v_ref[0, :, cols], expo.astype(half), ((0,), (0,)))
        heads_ref[:, cols] = (out / total).T.astype(half)
        lse_ref[0, h : h + 1, :] = top + jnp.log(total)
    out_ref[...] = jnp.dot(heads_ref[...], w_ref[...], preferred_element_type=f32).astype(half)


def attend_call(qkv, qcode, kcode, w_out, chunk, first, count):
    _, rows, local = qkv.shape
    width = w_out.shape[1]
    heads = local // HEAD_DIM
    return pl.pallas_call(
        attend_kernel,
        grid=(count,),
        in_specs=[
            spec((1, chunk, local), lambda i: (0, first + i, 0)),
            spec((1, rows, local), lambda i: (1, 0, 0)),
            spec((1, rows, local), lambda i: (2, 0, 0)),
            spec((chunk, HEAD_DIM), lambda i: (first + i, 0)),
            fixed((rows, HEAD_DIM)),
            held(w_out.shape),
        ],
        out_specs=[
            spec((chunk, local), lambda i: (i, 0)),
            spec((1, heads, chunk), lambda i: (i, 0, 0)),
            spec((chunk, width), lambda i: (i, 0)),
        ],
        out_shape=[
            shaped((count * chunk, local), half),
            shaped((count, heads, chunk), f32),
            shaped((count * chunk, width), half),
        ],
        compiler_params=params(32),
        cost_estimate=cost(2 + 3.3 * count),
        name="attend",
    )(qkv, qkv, qkv, qcode, kcode, w_out)


def attend_back_kernel(final, layout, q_ref, k_ref, v_ref, qcode_ref, kcode_ref, lse_ref, w_ref, *refs):
    chunk, local = q_ref.shape[1:]
    pieces, refs, d_heads_ref = refs[: sum(layout)], refs[sum(layout) : -1], refs[-1]
    heads = local // HEAD_DIM
    step = pl.program_id(0)
    factor = HEAD_DIM ** (-0.5)
    if final:
        dk_old, dv_old, dq_ref, dk_ref, dv_ref, dk_acc, dv_acc = refs
    else:
        dq_ref, dk_acc, dv_acc = refs

    @pl.when(step == 0)
    def _():
        dk_acc[...] = dk_old[...] if final else jnp.zeros_like(dk_acc)
        dv_acc[...] = dv_old[...] if final else jnp.zeros_like(dv_acc)

    for d, count in enumerate(layout):

        @pl.when(step == d)
        def _(refs=pieces[sum(layout[:d]) :][:count]):
            at = 0
            for ref in refs:
                d_heads_ref[at : at + ref.shape[0], :] = dot(ref[...], w_ref[...], ((1,), (1,))).astype(half)
                at += ref.shape[0]

    for h in range(heads):
        cols = slice(h * HEAD_DIM, (h + 1) * HEAD_DIM)
        keys = jnp.concatenate([k_ref[0, :, cols], kcode_ref[...]], axis=1)
        query = jnp.concatenate([q_ref[0, :, cols], qcode_ref[...]], axis=1)
        grad = d_heads_ref[:, cols]
        scores = dot(keys, query, ((1,), (1,)))
        probs = jnp.exp(scores - lse_ref[0, h : h + 1, :])
        d_probs = dot(v_ref[0, :, cols], grad, ((1,), (1,)))
        inner = jnp.sum(probs * d_probs, axis=0, keepdims=True)
        d_scores = (probs * (d_probs - inner)).astype(half)
        dv_acc[:, cols] += dot(probs.astype(half), grad, ((1,), (0,)))
        dk_acc[:, cols] += dot(d_scores, q_ref[0, :, cols], ((1,), (0,)))
        dq = dot(k_ref[0, :, cols], d_scores, ((0,), (0,)))
        dq_ref[:, cols] = (dq.T * factor).astype(half)

    if final:

        @pl.when(step == pl.num_programs(0) - 1)
        def _():
            dk_ref[...] = dk_acc[...].astype(half)
            dv_ref[...] = dv_acc[...].astype(half)


def attend_back_call(qkv, qcode, kcode, lse, w_out, d_attn, first, sums):
    _, rows, local = qkv.shape
    _, heads, chunk = lse.shape
    count = len(d_attn)
    final = sums is not None
    whole = (rows, local)
    return pl.pallas_call(
        lambda *refs: attend_back_kernel(final, [len(pieces) for pieces in d_attn], *refs),
        grid=(count,),
        in_specs=[
            spec((1, chunk, local), lambda i: (0, first + i, 0)),
            spec((1, rows, local), lambda i: (1, 0, 0)),
            spec((1, rows, local), lambda i: (2, 0, 0)),
            spec((chunk, HEAD_DIM), lambda i: (first + i, 0)),
            fixed((rows, HEAD_DIM)),
            spec((1, heads, chunk), lambda i: (first + i, 0, 0)),
            held(w_out.shape),
        ]
        + [held(piece.shape) for piece in flat(d_attn)]
        + ([held(whole)] * 2 if final else []),
        out_specs=[spec((chunk, local), lambda i: (i, 0))] + [fixed(whole)] * 2,
        out_shape=[shaped((count * chunk, local), half)] + [shaped(whole, half if final else f32)] * 2,
        scratch_shapes=([pltpu.VMEM(whole, f32)] * 2 if final else []) + [pltpu.VMEM((chunk, local), half)],
        compiler_params=params(36),
        cost_estimate=cost(0 if final else 130),
        name="attend_back",
    )(qkv, qkv, qkv, qcode, kcode, lse, w_out, *flat(d_attn), *(sums if final else []))


def project_back_kernel(q_ref, k_ref, v_ref, w_ref, out_ref):
    total = None
    for i, ref in enumerate((q_ref, k_ref, v_ref)):
        part = dot(ref[...], w_ref[i], ((1,), (1,)))
        total = part if total is None else total + part
    out_ref[...] = total.astype(half)


def project_back_call(d_query, d_key, d_value, w_qkv, chunk, first, count, first_query):
    _, width, local = w_qkv.shape
    there = lambda i: (first + i, 0)
    return pl.pallas_call(
        project_back_kernel,
        grid=(count,),
        in_specs=[
            spec((chunk, local), lambda i: (first - first_query + i, 0)),
            spec((chunk, local), there),
            spec((chunk, local), there),
            held(w_qkv.shape),
        ],
        out_specs=spec((chunk, width), lambda i: (i, 0)),
        out_shape=shaped((count * chunk, width), half),
        compiler_params=params(32),
        cost_estimate=cost(0),
        name="project_back",
    )(d_query, d_key, d_value, w_qkv)


def total_of(terms):
    return jnp.sum(terms, axis=0, keepdims=True)


def mlp_kernel(count, *refs):
    x_refs = refs[:count]
    up_ref, b_ref, d_ref = refs[count : count + 3]
    hidden_ref, d_pre_ref, dx_ref, b_sum_ref, acc_ref = refs[-5:]
    step = pl.program_id(0)
    mixed = jnp.concatenate([ref[...] for ref in x_refs], axis=0) if count > 1 else x_refs[0][...]
    pre = jnp.dot(mixed, up_ref[...], preferred_element_type=f32) + b_ref[...]
    cumul = 0.5 * (1.0 + lax.erf(pre * 0.7071067811865476))
    density = jnp.exp(-0.5 * pre * pre) * 0.3989422804014327
    hidden_ref[...] = (pre * cumul).astype(half)
    d_pre = (d_ref[...].astype(f32) * (cumul + pre * density)).astype(half)
    d_pre_ref[...] = d_pre
    b_sum_ref[...] = total_of(d_pre.astype(f32))
    part = dot(d_pre, up_ref[...], ((1,), (1,)))

    @pl.when(step == 0)
    def _():
        acc_ref[...] = part

    @pl.when(step > 0)
    def _():
        acc_ref[...] += part

    @pl.when(step == pl.num_programs(0) - 1)
    def _():
        dx_ref[...] = acc_ref[...].astype(half)


def mlp_call(pieces, w_up, b_up, d_hidden, chunk, before):
    rows = sum(piece.shape[0] for piece in pieces)
    width, ff = w_up.shape
    block = min(1024, ff)
    here = lambda j: (chunk, j)
    operands = [*pieces, w_up, b_up[None, :], d_hidden]
    in_specs = [held(piece.shape) for piece in pieces] + [
        spec((width, block), lambda j: (0, j)),
        spec((1, block), lambda j: (0, j)),
        spec((rows, block), here),
    ]
    aliases = {}
    if before is not None:
        aliases = {len(operands): 0, len(operands) + 1: 1}
        operands += before
        in_specs += [pl.BlockSpec(memory_space=pl.ANY)] * 2
    return pl.pallas_call(
        lambda *refs: mlp_kernel(len(pieces), *refs),
        grid=(ff // block,),
        in_specs=in_specs,
        out_specs=[
            spec((rows, block), here),
            spec((rows, block), here),
            fixed((rows, width)),
            spec((1, block), lambda j: (0, j)),
        ],
        out_shape=[
            shaped((d_hidden.shape[0], ff), half),
            shaped((d_hidden.shape[0], ff), half),
            pltpu.VMEM((rows, width), half),
            shaped((1, ff), f32),
        ],
        scratch_shapes=[pltpu.VMEM((rows, width), f32)],
        input_output_aliases=aliases,
        compiler_params=params(24),
        cost_estimate=cost(3),
        name="mlp",
    )(*operands)


def summed(refs):
    total = None
    for ref in refs:
        part = ref[...].astype(f32)
        total = part if total is None else total + part
    return total


def middle_kernel(parts, span, slot_ref, *refs):
    tok_ref, gate_ref, shift_ref, scale_ref, mixed_ref, attended_ref = refs
    slot = slot_ref[span]
    attended = summed(parts)
    attended_ref[...] = attended
    normed, _ = normalize(tok_ref[...].astype(f32) + row_of(gate_ref, slot) * attended)
    mixed_ref[...] = (normed * (1.0 + row_of(scale_ref, slot)) + row_of(shift_ref, slot)).astype(half)


def back_b_kernel(parts, span, slot_ref, *refs):
    tok_ref, grad_ref, attended_ref, gate_ref, scale_ref, d_attn_ref, d_middle_ref, sums_ref = refs
    slot = slot_ref[span]
    gate = row_of(gate_ref, slot)
    attended = attended_ref[...]
    normed, recip = normalize(tok_ref[...].astype(f32) + gate * attended)
    d_mixed = summed(parts)
    back = norm_back(d_mixed * (1.0 + row_of(scale_ref, slot)), normed, recip)
    d_middle = grad_ref[...].astype(f32) + back
    d_middle_ref[...] = d_middle
    d_attn_ref[...] = (d_middle * gate).astype(half)
    sums_ref[0, 0:1, :] = total_of(d_middle * attended)
    sums_ref[0, 1:2, :] = total_of(d_mixed)
    sums_ref[0, 2:3, :] = total_of(d_mixed * normed)


def back_a_kernel(parts, span, slot_ref, *refs):
    tok_ref, d_middle_ref, scale_ref, out_ref, sums_ref = refs
    slot = slot_ref[span]
    normed, recip = normalize(tok_ref[...].astype(f32))
    d_mixed = summed(parts)
    back = norm_back(d_mixed * (1.0 + row_of(scale_ref, slot)), normed, recip)
    out_ref[...] = (d_middle_ref[...] + back).astype(half)
    sums_ref[0, 0:1, :] = total_of(d_mixed)
    sums_ref[0, 1:2, :] = total_of(d_mixed * normed)


def result_kernel(parts, span, slot_ref, *refs):
    tok_ref, grad_ref, attended_ref, gate_a_ref, gate_b_ref, out_ref, sums_ref = refs
    slot = slot_ref[span]
    middle = tok_ref[...].astype(f32) + row_of(gate_a_ref, slot) * attended_ref[...]
    mlp_out = summed(parts)
    out_ref[...] = (middle + row_of(gate_b_ref, slot) * mlp_out).astype(half)
    sums_ref[0, 0:1, :] = total_of(grad_ref[...].astype(f32) * mlp_out)


def on_own(kernel, name, me, slots, parts, whole, own, modes, columns, outs, terms):
    width = whole[0].shape[1]
    spans = slots.shape[0]
    rows = spans * SPAN
    parts = [part if isinstance(part, tuple) else (part,) for part in parts]
    arrays = [*flat(parts), *own]

    def call(me_ref, slot_ref, *refs):
        ins = refs[: len(arrays) + len(whole)]
        mode_refs = refs[len(ins) : len(ins) + len(columns)]
        out_refs = refs[len(ins) + len(columns) :]
        for span in range(spans):

            def view(ref, count=1):
                at = span % (spans // count) * SPAN
                return ref.at[at : at + SPAN, :]

            given, at = [], 0
            for part in parts:
                count = len(part)
                given.append(view(ins[at + span // (spans // count)], count))
                at += count
            own_refs = [view(ref) for ref in ins[at : at + len(own)]]
            whole_refs = [view(ref) for ref in ins[at + len(own) :]]
            targets = [view(ref) for ref in out_refs[: len(outs)]]
            sums = [ref.at[span : span + 1] for ref in out_refs[len(outs) :]]
            kernel(given, span, slot_ref, *whole_refs, *own_refs, *mode_refs, *targets, *sums)

    return pl.pallas_call(
        call,
        grid_spec=pltpu.PrefetchScalarGridSpec(
            num_scalar_prefetch=2,
            grid=(1,),
            in_specs=[held(array.shape) for array in arrays]
            + [spec((rows, width), lambda i, m, s: (m[0], 0))] * len(whole)
            + mode_specs(modes, columns),
            out_specs=[fixed((rows, width))] * len(outs) + ([fixed((spans, terms, width))] if terms else []),
        ),
        out_shape=[shaped((rows, width), kind) for kind in outs]
        + ([shaped((spans, terms, width), f32)] if terms else []),
        compiler_params=params(24),
        cost_estimate=cost(0 if name in ("result", "back_a") else 5),
        name=name,
    )(me[None], slots, *arrays, *[in_hbm(array) for array in whole], *([modes] * len(columns)))


def unpack_kernel(sum_ref, qkv_ref, out_ref):
    step = pl.program_id(0)

    @pl.when(step < 3)
    def _():
        qkv_ref[0] = sum_ref[...].astype(f32)

    @pl.when(step == 3)
    def _():
        out_ref[...] = sum_ref[...].astype(f32).T


def unpack_call(sums, local):
    rows = sums.shape[0]
    return pl.pallas_call(
        unpack_kernel,
        grid=(4,),
        in_specs=[spec((rows, local), lambda i: (0, i))],
        out_specs=[
            spec((1, rows, local), lambda i: (jnp.minimum(i, 2), 0, 0)),
            fixed((local, rows)),
        ],
        out_shape=[pltpu.HBM((3, rows, local), f32), pltpu.HBM((local, rows), f32)],
        compiler_params=params(16),
        cost_estimate=cost(2),
        name="unpack",
    )(in_hbm(sums))


def make_body(n_wide, n_narrow):
    def body(
        tokens,
        cotangent,
        noise_emb,
        offsets,
        lengths,
        group_ids,
        group_table,
        w_qkv,
        w_out,
        w_up,
        b_up,
        w_down,
        w_mod,
        b_mod,
    ):
        tok_dev, width = tokens.shape
        slots = offsets.shape[1]
        local = w_qkv.shape[2]
        groups = group_table.shape[0]
        rows = tok_dev // n_narrow
        spans = rows // SPAN
        last = n_narrow - 1
        me = lax.axis_index("narrow")
        place = lax.axis_index("wide")
        order = me ^ jnp.arange(n_narrow, dtype=jnp.int32)

        starts = (order[:, None] * spans + jnp.arange(spans, dtype=jnp.int32)[None, :]).reshape(-1, 1) * SPAN
        inside = (starts >= offsets) & (starts < offsets + lengths)
        slot_hot = inside.astype(f32)
        slot_of = jnp.sum(inside * jnp.arange(slots, dtype=jnp.int32)[None, :], axis=1).astype(jnp.int32)
        slot_own = slot_of[:spans]
        lanes = jnp.arange(HEAD_DIM, dtype=jnp.int32)
        same = jnp.repeat(slot_of, SPAN)[:, None] == lanes[None, :]
        kcode = same.astype(half)
        qcode = jnp.where(same, 0.0, MASKED).astype(half)

        group_hot = (group_ids[0][:, None] == jnp.arange(groups, dtype=jnp.int32)[None, :]).astype(f32)
        cond = noise_emb + jnp.dot(group_hot, group_table, precision=highest)
        silu_low = jax.nn.silu(cond).astype(half)
        w_mod_t = w_mod.transpose(1, 0, 2)

        silu_all = lax.all_gather(jnp.concatenate([silu_low, silu_low], axis=0), "wide", axis=0)

        own_a = modes_call(silu_low, w_mod_t, b_mod, 0, 2)
        got_a = exchange([own_a] * n_narrow, n_narrow)
        own_b = modes_call(after(silu_low, own_a), w_mod_t, b_mod, 2, 4)
        modes_a = in_order(got_a, me, 2)
        mixed_a = by_chunk(mix_kernel, "mix_a", after(order, own_b), slot_of, tokens, modes_a, (0, 1))
        qkv = project_call(mixed_a, w_qkv, HEAD_DIM ** (-0.5))

        far = attend_call(qkv, qcode, kcode, w_out, rows, last, 1)
        via = collect_far(far[2], n_narrow)
        got_b = exchange([after(own_b, far[1])] * n_narrow, n_narrow)
        near = far
        if last > 1:
            near = attend_call(qkv, after(qcode, far[1], silu_all), kcode, w_out, rows, 1, last - 1)
        own = attend_call(qkv, after(qcode, near[1]), kcode, w_out, rows, 0, 1)
        modes = jnp.concatenate([modes_a, in_order([after(got, near[1]) for got in got_b], me, 2)], axis=0)
        in_turn = [own, near, far] if last > 1 else [own, far]
        heads_out = jnp.concatenate([outs[0] for outs in in_turn], axis=0)
        lse = jnp.concatenate([outs[1] for outs in in_turn], axis=0)
        sent = [near[2][(d - 1) * rows : d * rows] for d in range(1, last)]
        mid = rows // 2
        if n_narrow == 4:
            via_two, via_one = [after(got, own[1]) for got in via]
            second = hop(sent[0][mid:], 1, n_narrow)
            first = hop(sent[1][:mid], 2, n_narrow)
            merged = [
                (half_chunk.astype(f32) + got.astype(f32)).astype(half)
                for half_chunk, got in ((sent[0][:mid], via_two), (sent[1][mid:], via_one))
            ]
            attended_parts = [
                own[2],
                (hop(merged[0], 1, n_narrow), second),
                (first, hop(merged[1], 2, n_narrow)),
            ]
        else:
            attended_parts = exchange([own[2]] + sent + [far[2]], n_narrow)

        calls = [[(d, 0), (d, 1)] for d in range(n_narrow)]
        if n_narrow == 4:
            calls[1:3] = [[(1, 0), (2, 0)], [(1, 1), (2, 1)]]
        halves = flat(calls)
        block = rows // 2
        order_mlp = jnp.stack([2 * (me ^ d) + h for d, h in halves])
        slot_mlp = slot_of.reshape(2 * n_narrow, -1)[jnp.array([2 * d + h for d, h in halves])].reshape(-1)
        d_mlp = by_chunk(gate_kernel, "d_mlp", after(order_mlp, own[1]), slot_mlp, cotangent, modes, (5,))
        d_hidden = product(d_mlp, w_down, ((1,), (1,)), "d_hidden")
        mixed_own, attended = on_own(
            middle_kernel, "middle", me, after(slot_own, d_hidden), attended_parts, [tokens], [],
            modes, (2, 3, 4), [half, f32], 0,
        )
        pieces = {(0, h): mixed_own[h * block : (h + 1) * block] for h in range(2)}

        def send(half):
            for d in range(1, n_narrow if n_narrow != 4 else 3):
                pieces[d, half] = hop(pieces[0, half], d, n_narrow)

        send(0)
        pair, d_mixed, b_sums, due = None, {}, [], []
        for k, call in enumerate(calls):
            given = [pieces[half_chunk] for half_chunk in call] if k else [mixed_own]
            if k == 3 and n_narrow == 4:
                given = [pieces[half_chunk] for half_chunk in call]
            outs = mlp_call(given, w_up, after(b_up, *due), d_hidden, k, pair)
            pair = list(outs[:2])
            for i, half_chunk in enumerate(call):
                d_mixed[half_chunk] = outs[2][i * block : (i + 1) * block] if call[0][0] != call[1][0] else outs[2]
            b_sums.append(outs[3])
            due = [outs[3]]
            if k == 1 and n_narrow == 4:
                pieces[3, 0] = hop(after(pieces[2, 0], outs[3]), 1, n_narrow)
                pieces[3, 1] = hop(after(pieces[1, 1], outs[3]), 2, n_narrow)
            if not k:
                pieces[0, 1] = after(pieces[0, 1], outs[3])
                send(1)
        hidden, d_pre = pair

        def of_distance(d):
            first, second = d_mixed[d, 0], d_mixed[d, 1]
            if first is second:
                return first
            return after(joined([first, second]), pieces[last, 0], pieces[last, 1])

        d_mixed_parts = exchange([of_distance(d) for d in range(n_narrow)], n_narrow)
        mixed_b = jnp.concatenate([mixed_own] + [pieces[half_chunk] for half_chunk in halves[2:]], axis=0)

        def mlp_chunks(array):
            at = {half_chunk: k * block for k, half_chunk in enumerate(halves)}
            return [
                joined([array[at[d, h] : at[d, h] + block] for h in range(2)]) for d in range(n_narrow)
            ]

        grad_b_up = after(sum(b_sums)[0], hidden)

        grad_w_up = product(mixed_b, d_pre, ((0,), (0,)), "grad_w_up", out=pltpu.HBM, micros=4)
        sum_w_up = lax.psum_scatter(grad_w_up, "wide", scatter_dimension=0, tiled=True)
        grad_w_down = product(
            d_mlp, hidden, ((0,), (0,)), "grad_w_down", out=pltpu.HBM, micros=4, gate=after(order, grad_w_up)
        )

        d_attn_own, d_middle, sums_b = on_own(
            back_b_kernel, "back_b", me, after(slot_own, grad_w_down), d_mixed_parts, [tokens, cotangent],
            [attended], modes, (2, 4), [half, f32], 3,
        )

        def to_modes(sums):
            sent = [lax.dynamic_slice_in_dim(sums, (me ^ d) * local, local, 2) for d in range(n_narrow)]
            got = exchange(sent, n_narrow)
            modes_back = jnp.einsum("bs,bgv->gsv", slot_hot, jnp.concatenate(got, axis=0), precision=highest)
            return sent, modes_back.astype(half)

        d_attn_near = spread_near(d_attn_own, n_narrow)

        mlp_sent = product(hidden, w_down, ((1,), (0,)), "mlp_out", micros=200, gate=after(order, sums_b))
        d_attn_pieces = spread(d_attn_near, n_narrow, mlp_sent)
        mlp_sent = after(mlp_sent, *d_attn_near[1:])
        mlp_parts = exchange(mlp_chunks(mlp_sent), n_narrow)
        back = attend_back_call(qkv, qcode, kcode, lse, w_out, d_attn_pieces[:last], 0, None)
        back_far = attend_back_call(
            qkv, after(qcode, back[0]), kcode, lse, w_out, d_attn_pieces[last:], last, back[1:]
        )
        d_key, d_value = back_far[1:]
        far_a = project_back_call(back_far[0], d_key, d_value, w_qkv, rows, last, 1, last)
        via_a = collect_far(far_a, n_narrow)
        near_a = project_back_call(back[0], after(d_key, far_a), d_value, w_qkv, rows, 0, last, 0)
        sent_a = [near_a[d * rows : (d + 1) * rows] for d in range(last)] + [far_a]
        near_sent = collect_near(sent_a, n_narrow, via_a)
        d_mixed_a_parts = exchange(sent_a[:1] + near_sent, n_narrow)
        sum_w_down = lax.psum_scatter(after(grad_w_down, *d_attn_near[1:]), "wide", scatter_dimension=0, tiled=True)

        d_query = jnp.concatenate([back[0], back_far[0]], axis=0)
        d_proj = jnp.concatenate([after(d_query, near_a), d_key, d_value], axis=1)
        wide_cols = d_proj.shape[1] + local
        grads = product(
            mixed_a, d_proj, ((0,), (0,)), "grad_w_qkv", block=local, out=pltpu.HBM, micros=0,
            columns=wide_cols, gate=after(order, *mlp_parts),
        )
        d_attn = jnp.concatenate([joined(pieces) for pieces in d_attn_pieces], axis=0)
        grads = product(
            d_attn, heads_out, ((0,), (0,)), "grad_w_out", block=local, out=pltpu.HBM, micros=0,
            columns=wide_cols, first=d_proj.shape[1], before=grads, gate=after(order, *via_a),
        )
        sum_rest = lax.psum_scatter(grads, "wide", scatter_dimension=0, tiled=True)
        result_own, sums_out = on_own(
            result_kernel, "result", me, after(slot_own, grads, *near_sent), mlp_parts, [tokens, cotangent],
            [attended], modes, (2, 5), [half], 1,
        )
        grad_tok_own, sums_a = on_own(
            back_a_kernel, "back_a", me, after(slot_own, result_own, sum_w_up), d_mixed_a_parts, [tokens],
            [d_middle], modes, (1,), [half], 2,
        )
        sums_sent, d_modes = to_modes(jnp.concatenate([sums_a, sums_b, sums_out], axis=1))
        d_silu_part = silu_back_call(after(d_modes, sum_w_down), w_mod_t).astype(half)
        d_silu = sum(part.astype(f32) for part in exchange([d_silu_part] * n_narrow, n_narrow))
        sigma = jax.nn.sigmoid(cond)
        grad_noise = d_silu * sigma * (1.0 + cond * (1.0 - sigma))
        table_part = jnp.dot(group_hot.T, grad_noise, precision=highest).astype(half)

        grad_tok_near = spread_near(after(grad_tok_own, d_silu_part), n_narrow)
        result_near = spread_near(after(result_own, d_silu_part), n_narrow)
        ff = w_up.shape[1]
        small = jnp.pad(grad_b_up.astype(half), (0, -ff % width)).reshape(-1, width)
        late = lax.all_gather(
            jnp.concatenate([d_modes.reshape(-1, width), small, table_part], axis=0), "wide", axis=0
        )
        result = settle(spread(result_near, n_narrow, late), after(order, sum_w_down))
        grad_tokens = settle(spread(grad_tok_near, n_narrow, late), after(order, result))

        col = width // n_wide
        ff_part = ff // n_wide
        part_b = local // n_wide
        silu_cols = lax.dynamic_slice_in_dim(silu_all[:, :slots], place * col, col, 2).reshape(-1, col)
        mode_rows = 6 * slots * local // width
        small_rows = mode_rows + small.shape[0]
        b_up_all = late[:, mode_rows:small_rows].reshape(n_wide, -1)[:, :ff]
        sum_b_up = jnp.sum(
            lax.dynamic_slice_in_dim(b_up_all, place * ff_part, ff_part, 1).astype(f32), axis=0
        )
        d_modes_all = late[:, :mode_rows].reshape(n_wide, 6, slots, local)
        d_modes_all = d_modes_all.transpose(1, 0, 2, 3).reshape(6, n_wide * slots, local)
        grad_w_mod = jnp.einsum("sd,gsv->gdv", silu_cols, d_modes_all, preferred_element_type=f32).transpose(1, 0, 2)
        sum_b_mod = jnp.sum(
            lax.dynamic_slice_in_dim(d_modes_all, place * part_b, part_b, 2).astype(f32), axis=1
        )
        sum_table = jnp.sum(
            lax.dynamic_slice_in_dim(late[:, small_rows:], place * col, col, 2).astype(f32), axis=0
        )

        out_qkv, out_w_out = unpack_call(after(sum_rest, result, grad_tokens), local)
        return (
            result,
            grad_tokens,
            grad_noise,
            sum_table,
            out_qkv,
            out_w_out,
            sum_w_up.astype(f32),
            sum_b_up,
            sum_w_down.astype(f32).T,
            grad_w_mod,
            sum_b_mod,
        )

    return body


def solution(mesh):
    in_specs = (
        P("wide", None),
        P("wide", None),
        P("wide", None),
        P("wide", None),
        P("wide", None),
        P("wide", None),
        P(),
        P(None, None, "narrow"),
        P("narrow", None),
        P(None, "narrow"),
        P("narrow"),
        P("narrow", None),
        P(None, None, "narrow"),
        P(None, "narrow"),
    )
    out_specs = (
        P("wide", None),
        P("wide", None),
        P("wide", None),
        P(None, "wide"),
        P(None, "wide", "narrow"),
        P("narrow", "wide"),
        P("wide", "narrow"),
        P(("narrow", "wide")),
        P("narrow", "wide"),
        P("wide", None, "narrow"),
        P(None, ("narrow", "wide")),
    )
    body = make_body(mesh.shape["wide"], mesh.shape["narrow"])
    return jax.shard_map(body, mesh=mesh, in_specs=in_specs, out_specs=out_specs, check_vma=False)
```

```python
import jax
import jax.numpy as jnp
from jax import lax
from jax.experimental import pallas as pl
from jax.experimental.pallas import tpu as pltpu
from jax.sharding import PartitionSpec as P

HEAD_DIM = 128
SPAN = 64
MASKED = -1e30

f32 = jnp.float32
half = jnp.bfloat16
highest = lax.Precision.HIGHEST
MIB = 1 << 20


def dot(left, right, dims):
    return lax.dot_general(left, right, (dims, ((), ())), preferred_element_type=f32)


def normalize(values):
    centred = values - jnp.mean(values, axis=-1, keepdims=True)
    recip = lax.rsqrt(jnp.mean(centred * centred, axis=-1, keepdims=True) + 1e-06)
    return (centred * recip, recip)


def norm_back(grad, normed, recip):
    first = jnp.mean(grad, axis=-1, keepdims=True)
    second = jnp.mean(grad * normed, axis=-1, keepdims=True)
    return recip * (grad - first - normed * second)


def spec(shape, index):
    return pl.BlockSpec(shape, index)


def fixed(shape):
    zeros = (0,) * len(shape)
    return pl.BlockSpec(shape, lambda *_: zeros)


def held(shape):
    zeros = (0,) * len(shape)
    return pl.BlockSpec(shape, lambda *_: zeros, pipeline_mode=pl.Buffered(1))


def in_hbm(array):
    return pltpu.with_memory_space_constraint(array, pltpu.HBM)


def params(mib):
    return pltpu.CompilerParams(vmem_limit_bytes=mib * MIB)


def cost(micros):
    return pl.CostEstimate(flops=int(micros * 1.15e+09), transcendentals=0, bytes_accessed=0)


def shaped(shape, kind):
    return jax.ShapeDtypeStruct(shape, kind)


def after(values, *others):
    return lax.optimization_barrier((values, *others))[0]


def hop(values, distance, size):
    return lax.ppermute(values, "narrow", [(i, i ^ distance) for i in range(size)])


def exchange(chunks, size):
    return [chunks[0]] + [hop(chunks[d], d, size) for d in range(1, len(chunks))]


def spread_near(shard, size):
    return [shard] + [hop(shard, d, size) for d in range(1, size if size != 4 else 3)]


def spread(near, size, *gates):
    if size != 4:
        return [[piece] for piece in near]
    one, two = near[1:]
    mid = one.shape[0] // 2
    two, one = after(two[:mid], *gates), after(one[mid:], *gates)
    return [[piece] for piece in near] + [[hop(two, 1, size), hop(one, 2, size)]]


def joined(pieces):
    return jnp.concatenate(pieces, axis=0) if len(pieces) > 1 else pieces[0]


def flat(lists):
    return [piece for pieces in lists for piece in pieces]


def collect_far(far, size):
    if size != 4:
        return []
    mid = far.shape[0] // 2
    return [hop(far[:mid], 2, size), hop(far[mid:], 1, size)]


def collect_near(chunks, size, via):
    if size != 4:
        return chunks[1:]
    _, one, two, _ = chunks
    mid = one.shape[0] // 2
    via_two, via_one = via
    one = joined([(one[:mid].astype(f32) + via_two.astype(f32)).astype(half), one[mid:]])
    two = joined([two[:mid], (two[mid:].astype(f32) + via_one.astype(f32)).astype(half)])
    return [one, two]


def collect(chunks, size, via):
    return exchange(chunks[:1] + collect_near(chunks, size, via), size)


def in_order(pieces, index, axis):
    return jnp.concatenate([lax.select_n(index ^ k, *pieces) for k in range(len(pieces))], axis=axis)


def settle_kernel(layout, order_ref, *refs):
    out_ref = refs[-1]
    for d, count in enumerate(layout):

        @pl.when(pl.program_id(0) == d)
        def _(pieces=refs[sum(layout[:d]) :][:count]):
            at = 0
            for piece in pieces:
                out_ref[at : at + piece.shape[0], :] = piece[...]
                at += piece.shape[0]


def settle(chunks, order):
    rows = sum(piece.shape[0] for piece in chunks[0])
    width = chunks[0][0].shape[1]
    return pl.pallas_call(
        lambda *refs: settle_kernel([len(pieces) for pieces in chunks], *refs),
        grid_spec=pltpu.PrefetchScalarGridSpec(
            num_scalar_prefetch=1,
            grid=(len(chunks),),
            in_specs=[held(piece.shape) for piece in flat(chunks)],
            out_specs=spec((rows, width), lambda i, o: (o[i], 0)),
        ),
        out_shape=pltpu.HBM((rows * len(chunks), width), chunks[0][0].dtype),
        compiler_params=params(16),
        cost_estimate=cost(20),
        name="settle",
    )(order, *flat(chunks))


def modes_kernel(silu_ref, w_ref, b_ref, out_ref):
    for g in range(w_ref.shape[0]):
        out_ref[g] = jnp.dot(silu_ref[...], w_ref[g], preferred_element_type=f32) + b_ref[g]


def modes_call(silu_low, w_mod, b_mod, first, count):
    slots, width = silu_low.shape
    local = w_mod.shape[2]
    there = lambda i: (first // 2 + i, 0, 0)
    return pl.pallas_call(
        modes_kernel,
        grid=(count // 2,),
        in_specs=[
            fixed((slots, width)),
            spec((2, width, local), there),
            spec((2, 1, local), there),
        ],
        out_specs=spec((2, slots, local), lambda i: (i, 0, 0)),
        out_shape=shaped((count, slots, local), f32),
        cost_estimate=cost(1.5 * count),
        compiler_params=params(24),
        name="modes",
    )(silu_low, in_hbm(w_mod), b_mod[:, None, :])


def silu_back_kernel(d_ref, w_ref, out_ref):
    part = dot(d_ref[0], w_ref[0], ((1,), (1,)))

    @pl.when(pl.program_id(0) == 0)
    def _():
        out_ref[...] = part

    @pl.when(pl.program_id(0) > 0)
    def _():
        out_ref[...] = out_ref[...] + part


def silu_back_call(d_modes, w_mod):
    groups, slots, local = d_modes.shape
    width = w_mod.shape[1]
    return pl.pallas_call(
        silu_back_kernel,
        grid=(groups,),
        in_specs=[
            spec((1, slots, local), lambda g: (g, 0, 0)),
            spec((1, width, local), lambda g: (g, 0, 0)),
        ],
        out_specs=fixed((slots, width)),
        out_shape=shaped((slots, width), f32),
        compiler_params=params(16),
        cost_estimate=cost(0),
        name="silu_back",
    )(d_modes, in_hbm(w_mod))


def row_of(ref, slot):
    return ref[0, pl.ds(slot, 1), :]


def mix_kernel(order_ref, slot_ref, tok_ref, shift_ref, scale_ref, out_ref):
    step = pl.program_id(0)
    spans = tok_ref.shape[0] // SPAN
    for i in range(spans):
        rows = slice(i * SPAN, (i + 1) * SPAN)
        slot = slot_ref[step * spans + i]
        normed, _ = normalize(tok_ref[rows, :].astype(f32))
        out_ref[rows, :] = (normed * (1.0 + row_of(scale_ref, slot)) + row_of(shift_ref, slot)).astype(half)


def gate_kernel(order_ref, slot_ref, grad_ref, gate_ref, out_ref):
    step = pl.program_id(0)
    spans = grad_ref.shape[0] // SPAN
    for i in range(spans):
        rows = slice(i * SPAN, (i + 1) * SPAN)
        gate = row_of(gate_ref, slot_ref[step * spans + i])
        out_ref[rows, :] = (grad_ref[rows, :].astype(f32) * gate).astype(half)


def mode_specs(modes, columns):
    _, count, width = modes.shape
    return [spec((1, count, width), lambda i, *_, column=column: (column, 0, 0)) for column in columns]


def by_chunk(kernel, name, order, slots, values, modes, columns):
    rows, width = values.shape
    chunk = rows // order.shape[0]
    return pl.pallas_call(
        kernel,
        grid_spec=pltpu.PrefetchScalarGridSpec(
            num_scalar_prefetch=2,
            grid=(order.shape[0],),
            in_specs=[spec((chunk, width), lambda i, o, s: (o[i], 0))] + mode_specs(modes, columns),
            out_specs=spec((chunk, width), lambda i, o, s: (i, 0)),
        ),
        out_shape=shaped((rows, width), half),
        compiler_params=params(24),
        cost_estimate=cost(5),
        name=name,
    )(order, slots, values, *([modes] * len(columns)))


def product_kernel(dims, scales, left_ref, right_ref, out_ref):
    total = dot(left_ref[...], right_ref[...].reshape(right_ref.shape[-2:]), dims)
    if scales is not None:
        total = total * jnp.where(pl.program_id(0) == 0, scales, 1.0)
    out_ref[...] = total.astype(half).reshape(out_ref.shape)


def product(left, right, dims, name, block=512, out=shaped, micros=4, columns=None, first=0, before=None, gate=None):
    free = 1 - dims[1][0]
    count = right.shape[free]
    rows = left.shape[1 - dims[0][0]]
    block = min(block, count)
    shape = (block, right.shape[1]) if free == 0 else (right.shape[0], block)
    index = (lambda j: (j, 0)) if free == 0 else (lambda j: (0, j))
    given = ([] if before is None else [before]) + ([] if gate is None else [gate])
    return pl.pallas_call(
        lambda left_ref, right_ref, *refs: product_kernel(dims, None, left_ref, right_ref, refs[-1]),
        grid=(count // block,),
        in_specs=[held(left.shape), spec(shape, index)] + [pl.BlockSpec(memory_space=pl.ANY)] * len(given),
        out_specs=spec((rows, block), lambda j: (0, first // block + j)),
        out_shape=out((rows, columns or count), half),
        input_output_aliases={} if before is None else {2: 0},
        compiler_params=params(28),
        cost_estimate=cost(micros),
        name=name,
    )(left, right, *given)


def project_call(mixed, w_qkv, factor):
    count, width, local = w_qkv.shape
    rows = mixed.shape[0]
    return pl.pallas_call(
        lambda *refs: product_kernel(((1,), (0,)), factor, *refs),
        grid=(count,),
        in_specs=[held(mixed.shape), spec((1, width, local), lambda i: (i, 0, 0))],
        out_specs=spec((1, rows, local), lambda i: (i, 0, 0)),
        out_shape=shaped((count, rows, local), half),
        compiler_params=params(28),
        cost_estimate=cost(9),
        name="project",
    )(mixed, w_qkv)


def attend_kernel(q_ref, k_ref, v_ref, qcode_ref, kcode_ref, w_all_ref, heads_ref, lse_ref, out_ref, w_ref, sem):
    fetch = pltpu.make_async_copy(w_all_ref, w_ref, sem)

    @pl.when(pl.program_id(0) == 0)
    def _():
        fetch.start()

    heads = q_ref.shape[2] // HEAD_DIM
    for h in range(heads):
        cols = slice(h * HEAD_DIM, (h + 1) * HEAD_DIM)
        keys = jnp.concatenate([k_ref[0, :, cols], kcode_ref[...]], axis=1)
        query = jnp.concatenate([q_ref[0, :, cols], qcode_ref[...]], axis=1)
        scores = dot(keys, query, ((1,), (1,)))
        top = jnp.max(scores, axis=0, keepdims=True)
        expo = jnp.exp(scores - top)
        total = jnp.sum(expo, axis=0, keepdims=True)
        out = dot(v_ref[0, :, cols], expo.astype(half), ((0,), (0,)))
        heads_ref[:, cols] = (out / total).T.astype(half)
        lse_ref[0, h : h + 1, :] = top + jnp.log(total)

    @pl.when(pl.program_id(0) == 0)
    def _():
        fetch.wait()

    out_ref[...] = jnp.dot(heads_ref[...], w_ref[...], preferred_element_type=f32).astype(half)


def attend_call(qkv, qcode, kcode, w_out, chunk, first, count):
    _, rows, local = qkv.shape
    width = w_out.shape[1]
    heads = local // HEAD_DIM
    return pl.pallas_call(
        attend_kernel,
        grid=(count,),
        in_specs=[
            spec((1, chunk, local), lambda i: (0, first + i, 0)),
            spec((1, rows, local), lambda i: (1, 0, 0)),
            spec((1, rows, local), lambda i: (2, 0, 0)),
            spec((chunk, HEAD_DIM), lambda i: (first + i, 0)),
            fixed((rows, HEAD_DIM)),
            pl.BlockSpec(memory_space=pl.ANY),
        ],
        out_specs=[
            spec((chunk, local), lambda i: (i, 0)),
            spec((1, heads, chunk), lambda i: (i, 0, 0)),
            spec((chunk, width), lambda i: (i, 0)),
        ],
        out_shape=[
            shaped((count * chunk, local), half),
            shaped((count, heads, chunk), f32),
            shaped((count * chunk, width), half),
        ],
        scratch_shapes=[pltpu.VMEM(w_out.shape, half), pltpu.SemaphoreType.DMA],
        compiler_params=params(32),
        cost_estimate=cost(2 + 3.3 * count),
        name="attend",
    )(qkv, qkv, qkv, qcode, kcode, in_hbm(w_out))


def attend_back_kernel(final, layout, q_ref, k_ref, v_ref, qcode_ref, kcode_ref, lse_ref, w_ref, *refs):
    chunk, local = q_ref.shape[1:]
    pieces, refs, d_heads_ref = refs[: sum(layout)], refs[sum(layout) : -1], refs[-1]
    heads = local // HEAD_DIM
    step = pl.program_id(0)
    factor = HEAD_DIM ** (-0.5)
    if final:
        dk_old, dv_old, dq_ref, dk_ref, dv_ref, dk_acc, dv_acc = refs
    else:
        dq_ref, dk_acc, dv_acc = refs

    @pl.when(step == 0)
    def _():
        dk_acc[...] = dk_old[...] if final else jnp.zeros_like(dk_acc)
        dv_acc[...] = dv_old[...] if final else jnp.zeros_like(dv_acc)

    for d, count in enumerate(layout):

        @pl.when(step == d)
        def _(refs=pieces[sum(layout[:d]) :][:count]):
            at = 0
            for ref in refs:
                d_heads_ref[at : at + ref.shape[0], :] = dot(ref[...], w_ref[...], ((1,), (1,))).astype(half)
                at += ref.shape[0]

    for h in range(heads):
        cols = slice(h * HEAD_DIM, (h + 1) * HEAD_DIM)
        keys = jnp.concatenate([k_ref[0, :, cols], kcode_ref[...]], axis=1)
        query = jnp.concatenate([q_ref[0, :, cols], qcode_ref[...]], axis=1)
        grad = d_heads_ref[:, cols]
        scores = dot(keys, query, ((1,), (1,)))
        probs = jnp.exp(scores - lse_ref[0, h : h + 1, :])
        d_probs = dot(v_ref[0, :, cols], grad, ((1,), (1,)))
        inner = jnp.sum(probs * d_probs, axis=0, keepdims=True)
        d_scores = (probs * (d_probs - inner)).astype(half)
        dv_acc[:, cols] += dot(probs.astype(half), grad, ((1,), (0,)))
        dk_acc[:, cols] += dot(d_scores, q_ref[0, :, cols], ((1,), (0,)))
        dq = dot(k_ref[0, :, cols], d_scores, ((0,), (0,)))
        dq_ref[:, cols] = (dq.T * factor).astype(half)

    if final:

        @pl.when(step == pl.num_programs(0) - 1)
        def _():
            dk_ref[...] = dk_acc[...].astype(half)
            dv_ref[...] = dv_acc[...].astype(half)


def attend_back_call(qkv, qcode, kcode, lse, w_out, d_attn, first, sums):
    _, rows, local = qkv.shape
    _, heads, chunk = lse.shape
    count = len(d_attn)
    final = sums is not None
    whole = (rows, local)
    return pl.pallas_call(
        lambda *refs: attend_back_kernel(final, [len(pieces) for pieces in d_attn], *refs),
        grid=(count,),
        in_specs=[
            spec((1, chunk, local), lambda i: (0, first + i, 0)),
            spec((1, rows, local), lambda i: (1, 0, 0)),
            spec((1, rows, local), lambda i: (2, 0, 0)),
            spec((chunk, HEAD_DIM), lambda i: (first + i, 0)),
            fixed((rows, HEAD_DIM)),
            spec((1, heads, chunk), lambda i: (first + i, 0, 0)),
            held(w_out.shape),
        ]
        + [held(piece.shape) for piece in flat(d_attn)]
        + ([held(whole)] * 2 if final else []),
        out_specs=[spec((chunk, local), lambda i: (i, 0))] + [fixed(whole)] * 2,
        out_shape=[shaped((count * chunk, local), half)] + [shaped(whole, half if final else f32)] * 2,
        scratch_shapes=([pltpu.VMEM(whole, f32)] * 2 if final else []) + [pltpu.VMEM((chunk, local), half)],
        compiler_params=params(36),
        cost_estimate=cost(0 if final else 130),
        name="attend_back",
    )(qkv, qkv, qkv, qcode, kcode, lse, w_out, *flat(d_attn), *(sums if final else []))


def project_back_kernel(q_ref, k_ref, v_ref, w_ref, out_ref):
    total = None
    for i, ref in enumerate((q_ref, k_ref, v_ref)):
        part = dot(ref[...], w_ref[i], ((1,), (1,)))
        total = part if total is None else total + part
    out_ref[...] = total.astype(half)


def project_back_call(d_query, d_key, d_value, w_qkv, chunk, first, count, first_query):
    _, width, local = w_qkv.shape
    there = lambda i: (first + i, 0)
    return pl.pallas_call(
        project_back_kernel,
        grid=(count,),
        in_specs=[
            spec((chunk, local), lambda i: (first - first_query + i, 0)),
            spec((chunk, local), there),
            spec((chunk, local), there),
            held(w_qkv.shape),
        ],
        out_specs=spec((chunk, width), lambda i: (i, 0)),
        out_shape=shaped((count * chunk, width), half),
        compiler_params=params(32),
        cost_estimate=cost(0),
        name="project_back",
    )(d_query, d_key, d_value, w_qkv)


def total_of(terms):
    return jnp.sum(terms, axis=0, keepdims=True)


def mlp_kernel(count, *refs):
    x_refs = refs[:count]
    up_ref, b_ref, d_ref = refs[count : count + 3]
    hidden_ref, d_pre_ref, dx_ref, b_sum_ref, acc_ref = refs[-5:]
    step = pl.program_id(0)
    mixed = jnp.concatenate([ref[...] for ref in x_refs], axis=0) if count > 1 else x_refs[0][...]
    pre = jnp.dot(mixed, up_ref[...], preferred_element_type=f32) + b_ref[...]
    cumul = 0.5 * (1.0 + lax.erf(pre * 0.7071067811865476))
    density = jnp.exp(-0.5 * pre * pre) * 0.3989422804014327
    hidden_ref[...] = (pre * cumul).astype(half)
    d_pre = (d_ref[...].astype(f32) * (cumul + pre * density)).astype(half)
    d_pre_ref[...] = d_pre
    b_sum_ref[...] = total_of(d_pre.astype(f32))
    part = dot(d_pre, up_ref[...], ((1,), (1,)))

    @pl.when(step == 0)
    def _():
        acc_ref[...] = part

    @pl.when(step > 0)
    def _():
        acc_ref[...] += part

    @pl.when(step == pl.num_programs(0) - 1)
    def _():
        dx_ref[...] = acc_ref[...].astype(half)


def mlp_call(pieces, w_up, b_up, d_hidden, chunk, before):
    rows = sum(piece.shape[0] for piece in pieces)
    width, ff = w_up.shape
    block = min(1024, ff)
    here = lambda j: (chunk, j)
    operands = [*pieces, w_up, b_up[None, :], d_hidden]
    in_specs = [held(piece.shape) for piece in pieces] + [
        spec((width, block), lambda j: (0, j)),
        spec((1, block), lambda j: (0, j)),
        spec((rows, block), here),
    ]
    aliases = {}
    if before is not None:
        aliases = {len(operands): 0, len(operands) + 1: 1}
        operands += before
        in_specs += [pl.BlockSpec(memory_space=pl.ANY)] * 2
    return pl.pallas_call(
        lambda *refs: mlp_kernel(len(pieces), *refs),
        grid=(ff // block,),
        in_specs=in_specs,
        out_specs=[
            spec((rows, block), here),
            spec((rows, block), here),
            fixed((rows, width)),
            spec((1, block), lambda j: (0, j)),
        ],
        out_shape=[
            shaped((d_hidden.shape[0], ff), half),
            shaped((d_hidden.shape[0], ff), half),
            pltpu.VMEM((rows, width), half),
            shaped((1, ff), f32),
        ],
        scratch_shapes=[pltpu.VMEM((rows, width), f32)],
        input_output_aliases=aliases,
        compiler_params=params(24),
        cost_estimate=cost(3),
        name="mlp",
    )(*operands)


def summed(refs):
    total = None
    for ref in refs:
        part = ref[...].astype(f32)
        total = part if total is None else total + part
    return total


def middle_kernel(parts, span, slot_ref, *refs):
    tok_ref, gate_ref, shift_ref, scale_ref, mixed_ref, attended_ref = refs
    slot = slot_ref[span]
    attended = summed(parts)
    attended_ref[...] = attended
    normed, _ = normalize(tok_ref[...].astype(f32) + row_of(gate_ref, slot) * attended)
    mixed_ref[...] = (normed * (1.0 + row_of(scale_ref, slot)) + row_of(shift_ref, slot)).astype(half)


def back_b_kernel(parts, span, slot_ref, *refs):
    tok_ref, grad_ref, attended_ref, gate_ref, scale_ref, d_attn_ref, d_middle_ref, sums_ref = refs
    slot = slot_ref[span]
    gate = row_of(gate_ref, slot)
    attended = attended_ref[...]
    normed, recip = normalize(tok_ref[...].astype(f32) + gate * attended)
    d_mixed = summed(parts)
    back = norm_back(d_mixed * (1.0 + row_of(scale_ref, slot)), normed, recip)
    d_middle = grad_ref[...].astype(f32) + back
    d_middle_ref[...] = d_middle
    d_attn_ref[...] = (d_middle * gate).astype(half)
    sums_ref[0, 0:1, :] = total_of(d_middle * attended)
    sums_ref[0, 1:2, :] = total_of(d_mixed)
    sums_ref[0, 2:3, :] = total_of(d_mixed * normed)


def back_a_kernel(parts, span, slot_ref, *refs):
    tok_ref, d_middle_ref, scale_ref, out_ref, sums_ref = refs
    slot = slot_ref[span]
    normed, recip = normalize(tok_ref[...].astype(f32))
    d_mixed = summed(parts)
    back = norm_back(d_mixed * (1.0 + row_of(scale_ref, slot)), normed, recip)
    out_ref[...] = (d_middle_ref[...] + back).astype(half)
    sums_ref[0, 0:1, :] = total_of(d_mixed)
    sums_ref[0, 1:2, :] = total_of(d_mixed * normed)


def result_kernel(parts, span, slot_ref, *refs):
    tok_ref, grad_ref, attended_ref, gate_a_ref, gate_b_ref, out_ref, sums_ref = refs
    slot = slot_ref[span]
    middle = tok_ref[...].astype(f32) + row_of(gate_a_ref, slot) * attended_ref[...]
    mlp_out = summed(parts)
    out_ref[...] = (middle + row_of(gate_b_ref, slot) * mlp_out).astype(half)
    sums_ref[0, 0:1, :] = total_of(grad_ref[...].astype(f32) * mlp_out)


def on_own(kernel, name, me, slots, parts, whole, own, modes, columns, outs, terms):
    width = whole[0].shape[1]
    spans = slots.shape[0]
    rows = spans * SPAN
    parts = [part if isinstance(part, tuple) else (part,) for part in parts]
    arrays = [*flat(parts), *own]

    def call(me_ref, slot_ref, *refs):
        ins = refs[: len(arrays) + len(whole)]
        mode_refs = refs[len(ins) : len(ins) + len(columns)]
        out_refs = refs[len(ins) + len(columns) :]
        for span in range(spans):

            def view(ref, count=1):
                at = span % (spans // count) * SPAN
                return ref.at[at : at + SPAN, :]

            given, at = [], 0
            for part in parts:
                count = len(part)
                given.append(view(ins[at + span // (spans // count)], count))
                at += count
            own_refs = [view(ref) for ref in ins[at : at + len(own)]]
            whole_refs = [view(ref) for ref in ins[at + len(own) :]]
            targets = [view(ref) for ref in out_refs[: len(outs)]]
            sums = [ref.at[span : span + 1] for ref in out_refs[len(outs) :]]
            kernel(given, span, slot_ref, *whole_refs, *own_refs, *mode_refs, *targets, *sums)

    return pl.pallas_call(
        call,
        grid_spec=pltpu.PrefetchScalarGridSpec(
            num_scalar_prefetch=2,
            grid=(1,),
            in_specs=[held(array.shape) for array in arrays]
            + [spec((rows, width), lambda i, m, s: (m[0], 0))] * len(whole)
            + mode_specs(modes, columns),
            out_specs=[fixed((rows, width))] * len(outs) + ([fixed((spans, terms, width))] if terms else []),
        ),
        out_shape=[shaped((rows, width), kind) for kind in outs]
        + ([shaped((spans, terms, width), f32)] if terms else []),
        compiler_params=params(24),
        cost_estimate=cost(0 if name in ("result", "back_a") else 5),
        name=name,
    )(me[None], slots, *arrays, *[in_hbm(array) for array in whole], *([modes] * len(columns)))


def unpack_kernel(sum_ref, qkv_ref, out_ref):
    step = pl.program_id(0)

    @pl.when(step < 3)
    def _():
        qkv_ref[0] = sum_ref[...].astype(f32)

    @pl.when(step == 3)
    def _():
        out_ref[...] = sum_ref[...].astype(f32).T


def unpack_call(sums, local):
    rows = sums.shape[0]
    return pl.pallas_call(
        unpack_kernel,
        grid=(4,),
        in_specs=[spec((rows, local), lambda i: (0, i))],
        out_specs=[
            spec((1, rows, local), lambda i: (jnp.minimum(i, 2), 0, 0)),
            fixed((local, rows)),
        ],
        out_shape=[pltpu.HBM((3, rows, local), f32), pltpu.HBM((local, rows), f32)],
        compiler_params=params(16),
        cost_estimate=cost(2),
        name="unpack",
    )(in_hbm(sums))


def make_body(n_wide, n_narrow):
    def body(
        tokens,
        cotangent,
        noise_emb,
        offsets,
        lengths,
        group_ids,
        group_table,
        w_qkv,
        w_out,
        w_up,
        b_up,
        w_down,
        w_mod,
        b_mod,
    ):
        tok_dev, width = tokens.shape
        slots = offsets.shape[1]
        local = w_qkv.shape[2]
        groups = group_table.shape[0]
        rows = tok_dev // n_narrow
        spans = rows // SPAN
        last = n_narrow - 1
        me = lax.axis_index("narrow")
        place = lax.axis_index("wide")
        order = me ^ jnp.arange(n_narrow, dtype=jnp.int32)

        starts = (order[:, None] * spans + jnp.arange(spans, dtype=jnp.int32)[None, :]).reshape(-1, 1) * SPAN
        inside = (starts >= offsets) & (starts < offsets + lengths)
        slot_hot = inside.astype(f32)
        slot_of = jnp.sum(inside * jnp.arange(slots, dtype=jnp.int32)[None, :], axis=1).astype(jnp.int32)
        slot_own = slot_of[:spans]
        lanes = jnp.arange(HEAD_DIM, dtype=jnp.int32)
        same = jnp.repeat(slot_of, SPAN)[:, None] == lanes[None, :]
        kcode = same.astype(half)
        qcode = jnp.where(same, 0.0, MASKED).astype(half)

        group_hot = (group_ids[0][:, None] == jnp.arange(groups, dtype=jnp.int32)[None, :]).astype(f32)
        cond = noise_emb + jnp.dot(group_hot, group_table, precision=highest)
        silu_low = jax.nn.silu(cond).astype(half)
        w_mod_t = w_mod.transpose(1, 0, 2)

        silu_all = lax.all_gather(jnp.concatenate([silu_low, silu_low], axis=0), "wide", axis=0)

        own_a = modes_call(silu_low, w_mod_t, b_mod, 0, 2)
        got_a = exchange([own_a] * n_narrow, n_narrow)
        own_b = modes_call(after(silu_low, own_a), w_mod_t, b_mod, 2, 4)
        modes_a = in_order(got_a, me, 2)
        mixed_a = by_chunk(mix_kernel, "mix_a", after(order, own_b), slot_of, tokens, modes_a, (0, 1))
        qkv = project_call(mixed_a, w_qkv, HEAD_DIM ** (-0.5))

        far = attend_call(qkv, qcode, kcode, w_out, rows, last, 1)
        via = collect_far(far[2], n_narrow)
        got_b = exchange([after(own_b, far[1])] * n_narrow, n_narrow)
        near = far
        if last > 1:
            near = attend_call(qkv, after(qcode, far[1], silu_all), kcode, w_out, rows, 1, last - 1)
        own = attend_call(qkv, after(qcode, near[1]), kcode, w_out, rows, 0, 1)
        modes = jnp.concatenate([modes_a, in_order([after(got, near[1]) for got in got_b], me, 2)], axis=0)
        in_turn = [own, near, far] if last > 1 else [own, far]
        heads_out = jnp.concatenate([outs[0] for outs in in_turn], axis=0)
        lse = jnp.concatenate([outs[1] for outs in in_turn], axis=0)
        sent = [near[2][(d - 1) * rows : d * rows] for d in range(1, last)]
        mid = rows // 2
        if n_narrow == 4:
            via_two, via_one = [after(got, own[1]) for got in via]
            second = hop(sent[0][mid:], 1, n_narrow)
            first = hop(sent[1][:mid], 2, n_narrow)
            merged = [
                (half_chunk.astype(f32) + got.astype(f32)).astype(half)
                for half_chunk, got in ((sent[0][:mid], via_two), (sent[1][mid:], via_one))
            ]
            attended_parts = [
                own[2],
                (hop(merged[0], 1, n_narrow), second),
                (first, hop(merged[1], 2, n_narrow)),
            ]
        else:
            attended_parts = exchange([own[2]] + sent + [far[2]], n_narrow)

        calls = [[(d, 0), (d, 1)] for d in range(n_narrow)]
        if n_narrow == 4:
            calls[1:3] = [[(1, 0), (2, 0)], [(1, 1), (2, 1)]]
        halves = flat(calls)
        block = rows // 2
        order_mlp = jnp.stack([2 * (me ^ d) + h for d, h in halves])
        slot_mlp = slot_of.reshape(2 * n_narrow, -1)[jnp.array([2 * d + h for d, h in halves])].reshape(-1)
        d_mlp = by_chunk(gate_kernel, "d_mlp", after(order_mlp, own[1]), slot_mlp, cotangent, modes, (5,))
        d_hidden = product(d_mlp, w_down, ((1,), (1,)), "d_hidden")
        mixed_own, attended = on_own(
            middle_kernel, "middle", me, after(slot_own, d_hidden), attended_parts, [tokens], [],
            modes, (2, 3, 4), [half, f32], 0,
        )
        pieces = {(0, h): mixed_own[h * block : (h + 1) * block] for h in range(2)}

        def send(half):
            for d in range(1, n_narrow if n_narrow != 4 else 3):
                pieces[d, half] = hop(pieces[0, half], d, n_narrow)

        send(0)
        pair, d_mixed, b_sums, due = None, {}, [], []
        for k, call in enumerate(calls):
            given = [pieces[half_chunk] for half_chunk in call] if k else [mixed_own]
            if k == 3 and n_narrow == 4:
                given = [pieces[half_chunk] for half_chunk in call]
            outs = mlp_call(given, w_up, after(b_up, *due), d_hidden, k, pair)
            pair = list(outs[:2])
            for i, half_chunk in enumerate(call):
                d_mixed[half_chunk] = outs[2][i * block : (i + 1) * block] if call[0][0] != call[1][0] else outs[2]
            b_sums.append(outs[3])
            due = [outs[3]]
            if k == 1 and n_narrow == 4:
                pieces[3, 0] = hop(after(pieces[2, 0], outs[3]), 1, n_narrow)
                pieces[3, 1] = hop(after(pieces[1, 1], outs[3]), 2, n_narrow)
            if not k:
                pieces[0, 1] = after(pieces[0, 1], outs[3])
                send(1)
        hidden, d_pre = pair

        def of_distance(d):
            first, second = d_mixed[d, 0], d_mixed[d, 1]
            if first is second:
                return first
            return after(joined([first, second]), pieces[last, 0], pieces[last, 1])

        d_mixed_parts = exchange([of_distance(d) for d in range(n_narrow)], n_narrow)
        mixed_b = jnp.concatenate([mixed_own] + [pieces[half_chunk] for half_chunk in halves[2:]], axis=0)

        def mlp_chunks(array):
            at = {half_chunk: k * block for k, half_chunk in enumerate(halves)}
            return [
                joined([array[at[d, h] : at[d, h] + block] for h in range(2)]) for d in range(n_narrow)
            ]

        grad_b_up = after(sum(b_sums)[0], hidden)

        grad_w_up = product(mixed_b, d_pre, ((0,), (0,)), "grad_w_up", out=pltpu.HBM, micros=4)
        sum_w_up = lax.psum_scatter(grad_w_up, "wide", scatter_dimension=0, tiled=True)
        grad_w_down = product(
            d_mlp, hidden, ((0,), (0,)), "grad_w_down", out=pltpu.HBM, micros=4, gate=after(order, grad_w_up)
        )

        d_attn_own, d_middle, sums_b = on_own(
            back_b_kernel, "back_b", me, after(slot_own, grad_w_down), d_mixed_parts, [tokens, cotangent],
            [attended], modes, (2, 4), [half, f32], 3,
        )

        def to_modes(sums):
            sent = [lax.dynamic_slice_in_dim(sums, (me ^ d) * local, local, 2) for d in range(n_narrow)]
            got = exchange(sent, n_narrow)
            modes_back = jnp.einsum("bs,bgv->gsv", slot_hot, jnp.concatenate(got, axis=0), precision=highest)
            return sent, modes_back.astype(half)

        d_attn_near = spread_near(d_attn_own, n_narrow)

        mlp_sent = product(hidden, w_down, ((1,), (0,)), "mlp_out", micros=200, gate=after(order, sums_b))
        d_attn_pieces = spread(d_attn_near, n_narrow, mlp_sent)
        mlp_sent = after(mlp_sent, *d_attn_near[1:])
        mlp_parts = exchange(mlp_chunks(mlp_sent), n_narrow)
        back = attend_back_call(qkv, qcode, kcode, lse, w_out, d_attn_pieces[:last], 0, None)
        back_far = attend_back_call(
            qkv, after(qcode, back[0]), kcode, lse, w_out, d_attn_pieces[last:], last, back[1:]
        )
        d_key, d_value = back_far[1:]
        far_a = project_back_call(back_far[0], d_key, d_value, w_qkv, rows, last, 1, last)
        via_a = collect_far(far_a, n_narrow)
        near_a = project_back_call(back[0], after(d_key, far_a), d_value, w_qkv, rows, 0, last, 0)
        sent_a = [near_a[d * rows : (d + 1) * rows] for d in range(last)] + [far_a]
        near_sent = collect_near(sent_a, n_narrow, via_a)
        d_mixed_a_parts = exchange(sent_a[:1] + near_sent, n_narrow)
        sum_w_down = lax.psum_scatter(after(grad_w_down, *d_attn_near[1:]), "wide", scatter_dimension=0, tiled=True)

        d_query = jnp.concatenate([back[0], back_far[0]], axis=0)
        d_proj = jnp.concatenate([after(d_query, near_a), d_key, d_value], axis=1)
        wide_cols = d_proj.shape[1] + local
        grads = product(
            mixed_a, d_proj, ((0,), (0,)), "grad_w_qkv", block=local, out=pltpu.HBM, micros=0,
            columns=wide_cols, gate=after(order, *mlp_parts),
        )
        d_attn = jnp.concatenate([joined(pieces) for pieces in d_attn_pieces], axis=0)
        grads = product(
            d_attn, heads_out, ((0,), (0,)), "grad_w_out", block=local, out=pltpu.HBM, micros=0,
            columns=wide_cols, first=d_proj.shape[1], before=grads, gate=after(order, *via_a),
        )
        sum_rest = lax.psum_scatter(grads, "wide", scatter_dimension=0, tiled=True)
        result_own, sums_out = on_own(
            result_kernel, "result", me, after(slot_own, grads, *near_sent), mlp_parts, [tokens, cotangent],
            [attended], modes, (2, 5), [half], 1,
        )
        grad_tok_own, sums_a = on_own(
            back_a_kernel, "back_a", me, after(slot_own, result_own, sum_w_up), d_mixed_a_parts, [tokens],
            [d_middle], modes, (1,), [half], 2,
        )
        sums_sent, d_modes = to_modes(jnp.concatenate([sums_a, sums_b, sums_out], axis=1))
        d_silu_part = silu_back_call(after(d_modes, sum_w_down), w_mod_t).astype(half)
        d_silu = sum(part.astype(f32) for part in exchange([d_silu_part] * n_narrow, n_narrow))
        sigma = jax.nn.sigmoid(cond)
        grad_noise = d_silu * sigma * (1.0 + cond * (1.0 - sigma))
        table_part = jnp.dot(group_hot.T, grad_noise, precision=highest).astype(half)

        grad_tok_near = spread_near(after(grad_tok_own, d_silu_part), n_narrow)
        result_near = spread_near(after(result_own, d_silu_part), n_narrow)
        ff = w_up.shape[1]
        small = jnp.pad(grad_b_up.astype(half), (0, -ff % width)).reshape(-1, width)
        late = lax.all_gather(
            jnp.concatenate([d_modes.reshape(-1, width), small, table_part], axis=0), "wide", axis=0
        )
        result = settle(spread(result_near, n_narrow, late), after(order, sum_w_down))
        grad_tokens = settle(spread(grad_tok_near, n_narrow, late), after(order, result))

        col = width // n_wide
        ff_part = ff // n_wide
        part_b = local // n_wide
        silu_cols = lax.dynamic_slice_in_dim(silu_all[:, :slots], place * col, col, 2).reshape(-1, col)
        mode_rows = 6 * slots * local // width
        small_rows = mode_rows + small.shape[0]
        b_up_all = late[:, mode_rows:small_rows].reshape(n_wide, -1)[:, :ff]
        sum_b_up = jnp.sum(
            lax.dynamic_slice_in_dim(b_up_all, place * ff_part, ff_part, 1).astype(f32), axis=0
        )
        d_modes_all = late[:, :mode_rows].reshape(n_wide, 6, slots, local)
        d_modes_all = d_modes_all.transpose(1, 0, 2, 3).reshape(6, n_wide * slots, local)
        grad_w_mod = jnp.einsum("sd,gsv->gdv", silu_cols, d_modes_all, preferred_element_type=f32).transpose(1, 0, 2)
        sum_b_mod = jnp.sum(
            lax.dynamic_slice_in_dim(d_modes_all, place * part_b, part_b, 2).astype(f32), axis=1
        )
        sum_table = jnp.sum(
            lax.dynamic_slice_in_dim(late[:, small_rows:], place * col, col, 2).astype(f32), axis=0
        )

        out_qkv, out_w_out = unpack_call(after(sum_rest, result, grad_tokens), local)
        return (
            result,
            grad_tokens,
            grad_noise,
            sum_table,
            out_qkv,
            out_w_out,
            sum_w_up.astype(f32),
            sum_b_up,
            sum_w_down.astype(f32).T,
            grad_w_mod,
            sum_b_mod,
        )

    return body


def solution(mesh):
    in_specs = (
        P("wide", None),
        P("wide", None),
        P("wide", None),
        P("wide", None),
        P("wide", None),
        P("wide", None),
        P(),
        P(None, None, "narrow"),
        P("narrow", None),
        P(None, "narrow"),
        P("narrow"),
        P("narrow", None),
        P(None, None, "narrow"),
        P(None, "narrow"),
    )
    out_specs = (
        P("wide", None),
        P("wide", None),
        P("wide", None),
        P(None, "wide"),
        P(None, "wide", "narrow"),
        P("narrow", "wide"),
        P("wide", "narrow"),
        P(("narrow", "wide")),
        P("narrow", "wide"),
        P("wide", None, "narrow"),
        P(None, ("narrow", "wide")),
    )
    body = make_body(mesh.shape["wide"], mesh.shape["narrow"])
    return jax.shard_map(body, mesh=mesh, in_specs=in_specs, out_specs=out_specs, check_vma=False)
```
